32 devices in a mesh: section: 8 (over z, y), rep: 4 (over x, core).
Axes of the slice: x: 2, y: 2, z: 4, core: 2. Of those that a mesh axis runs over, the one named last changes fastest.
Arguments:
- document_token_embedding: bfloat16 [8, 128, 4096], P('rep'), may hold values from -6 to 6
- doc_lengths: int32 [8, 4], P('rep'), may hold values from 1 to 32, as said below
- docid_embed: bfloat16 [8, 32, 4096], P('rep'), may hold values from -6 to 6
- docid_targets: int32 [8, 32], P('rep'), may hold values from 0 to 16383
- enc_gain: float32 [5, 4096], replicated, may hold values from 0.1 to 1.9
- dec_gain: float32 [2, 4096], replicated, may hold values from 0.1 to 1.9
- w_enc_qkv: bfloat16 [3, 12288, 4096], P(None, 'section'), may hold values from -0.03125 to 0.03125
- w_enc_out: bfloat16 [12288, 4096], P('section'), may hold values from -0.75 to 0.75
- cross_query_key_value_weight: bfloat16 [3, 4096, 4096], P(None, 'section'), may hold values from -0.03125 to 0.03125
- w_cross_out: bfloat16 [4096, 4096], P('section'), may hold values from -0.75 to 0.75
- docid_head_weight: bfloat16 [4096, 16384], P(None, 'section'), may hold values from -0.25 to 0.25
Outputs:
- logits: bfloat16 [8, 32, 16384], P('rep', None, 'section')
- token_loss: float32 [8, 32], P('rep')
- mean_loss: float32 [], replicated
The draws below stay inside these ranges and needn't reach their ends.
Inputs may be any that keep to these rules, and one draw needn't show every extreme that they name: `doc_lengths`: in every draw some document has exactly 32 tokens.
All inputs are finite; a program needn't handle non-finite values.
Results may differ from the reference program's by a relative error of at most 0.019.
Values may be sent and summed in bfloat16 or wider, within the bound.
A program may use at most 128 MiB of HBM per device.

```python
import jax
import jax.numpy as jnp
from jax import lax

D = 4096
HD = 64
XHEADS = 64
HEADS = 48
VOCAB = 16384
GROUPS = 4
DOCS = 4
DLEN = 8
LMAX = 32
ROWS = 128
DROWS = 32
BATCH = 8


def draw_doc_lengths(key, part):
    key_left, key_right, key_pick = jax.random.split(jax.random.fold_in(key, 17), 3)
    left_draw = jax.random.randint(key_left, (BATCH, DOCS), 0, LMAX)
    right_draw = jax.random.randint(key_right, (BATCH, DOCS), 0, LMAX)
    lengths = 1 + left_draw * right_draw // LMAX
    chosen = jax.random.randint(key_pick, (), 0, BATCH * DOCS)
    flattened = jnp.where(jnp.arange(BATCH * DOCS) == chosen, LMAX, lengths.reshape(-1))
    return flattened.reshape(BATCH, DOCS).astype(jnp.int32)


def touch_ends(array, stream_key, low, top_value):
    extent = array.shape
    place = [jax.random.randint(jax.random.fold_in(stream_key, axis), (), 0, extent[axis]) for axis in range(len(extent))]
    array = array.at[tuple(place)].set(low)
    longest = extent.index(max(extent))
    place[longest] = (place[longest] + 1) % extent[longest]
    return array.at[tuple(place)].set(top_value)


def block_levels(rng, shape, shards, low, top_value):
    def one(dim, shards_of):
        steps = jax.random.uniform(jax.random.fold_in(jax.random.fold_in(rng, 6), dim), (shards_of,), jnp.float32, low / len(shards), top_value / len(shards))
        return jnp.repeat(jnp.exp(steps), shape[dim] // shards_of).reshape((-1,) + (1,) * (len(shape) - dim - 1))

    level = one(*shards[0])
    for cut in shards[1:]:
        level = level * one(*cut)
    return level


def noise(own_key, extent, spread, reach, pieces=(), dtype=jnp.bfloat16):
    array = jax.random.normal(own_key, extent, jnp.float32) * spread
    if len(pieces) > 0:
        array = block_levels(own_key, extent, pieces, -0.22, 0.18) * array
    return jnp.clip(array, min=-reach, max=reach).astype(dtype)


def setup_inputs(seed: int = 0) -> dict:
    seeds = jax.random.split(jax.random.key(seed), 12)
    document_token_embedding = noise(seeds[0], (BATCH, ROWS, D), 1.0, 6.0, ((0, 4),))
    doc_lengths = draw_doc_lengths(jax.random.fold_in(seeds[11], 71), 0)
    docid_embed = noise(seeds[2], (BATCH, DROWS, D), 1.0, 6.0, ((0, 4),))
    docid_targets = touch_ends(jax.random.randint(seeds[3], (BATCH, DROWS), 0, VOCAB), jax.random.fold_in(seeds[3], 1), 0, VOCAB - 1).astype(jnp.int32)
    enc_gain = jnp.clip(1.0 + 0.18 * jax.random.normal(seeds[4], (GROUPS + 1, D), jnp.float32), 0.1, 1.9)
    dec_gain = jnp.clip(1.0 + 0.18 * jax.random.normal(seeds[5], (2, D), jnp.float32), 0.1, 1.9)
    w_enc_qkv = noise(seeds[6], (3, GROUPS * HEADS * HD, D), (D * 8) ** -0.5, 0.03125, ((1, 8),))
    w_enc_out = noise(seeds[7], (GROUPS * HEADS * HD, D), HD ** -0.5, 0.75, ((0, 8),))
    cross_query_key_value_weight = noise(seeds[8], (3, XHEADS * HD, D), (D * 8) ** -0.5, 0.03125, ((1, 8),))
    w_cross_out = noise(seeds[9], (XHEADS * HD, D), HD ** -0.5, 0.75, ((0, 8),))
    docid_head_weight = noise(seeds[10], (D, VOCAB), (D // 9) ** -0.5, 0.25, ((1, 8),))
    return {"document_token_embedding": document_token_embedding, "doc_lengths": doc_lengths, "docid_embed": docid_embed, "docid_targets": docid_targets, "enc_gain": enc_gain, "dec_gain": dec_gain, "w_enc_qkv": w_enc_qkv, "w_enc_out": w_enc_out, "cross_query_key_value_weight": cross_query_key_value_weight, "w_cross_out": w_cross_out, "docid_head_weight": docid_head_weight}


def norm_rows(values, gain):
    values = values.astype(jnp.float32)
    scale = lax.rsqrt(lax.optimization_barrier(jnp.mean(values * values, axis=-1, keepdims=True)) + 1e-06)
    return values * scale * gain

def attend(queries, key_rows, values, allowed):
    scores = jnp.einsum('qhe,khe->hqk', queries.astype(jnp.float32), key_rows.astype(jnp.float32))
    attention_weight_rows = jnp.where(allowed[None], jnp.exp(scores), 0.0)
    probabilities = (attention_weight_rows / lax.optimization_barrier(jnp.sum(attention_weight_rows, axis=-1, keepdims=True))).astype(jnp.bfloat16)
    mixture = jnp.einsum('hqk,khe->qhe', probabilities.astype(jnp.float32), values.astype(jnp.float32))
    return mixture.astype(jnp.bfloat16)

def project(normed, weight):
    return jnp.dot(normed, weight.T, preferred_element_type=jnp.float32).astype(jnp.bfloat16)

def reference(document_token_embedding, doc_lengths, docid_embed, docid_targets, enc_gain, dec_gain, w_enc_qkv, w_enc_out, cross_query_key_value_weight, w_cross_out, docid_head_weight):
    width_heads = HEADS * HD
    positions = jnp.arange(DOCS * LMAX)
    key_doc = positions // LMAX
    key_place = positions % LMAX
    decoder_doc = jnp.arange(DOCS * DLEN) // DLEN

    def per_sample(sample):
        doc_rows, lengths, docid_rows, targets = sample
        live_keys = key_place < lengths[key_doc]
        allowed = (key_doc[:, None] == key_doc[None, :]) & live_keys[None, :]
        hidden = doc_rows
        for depth in range(GROUPS):
            normed = norm_rows(hidden, enc_gain[depth]).astype(jnp.bfloat16)
            lower = depth * width_heads
            upper = lower + width_heads
            projected = [project(normed, w_enc_qkv[member, lower:upper]).reshape(-1, HEADS, HD) for member in range(3)]
            mixture = attend(projected[0], projected[1], projected[2], allowed).reshape(-1, width_heads)
            update = jnp.dot(mixture, w_enc_out[lower:upper], preferred_element_type=jnp.float32)
            hidden = (hidden.astype(jnp.float32) + update).astype(jnp.bfloat16)
        encoder_memory = norm_rows(hidden, enc_gain[GROUPS]).astype(jnp.bfloat16)
        dec_normed = norm_rows(docid_rows, dec_gain[0]).astype(jnp.bfloat16)
        queries = project(dec_normed, cross_query_key_value_weight[0]).reshape(-1, XHEADS, HD)
        key_rows = project(encoder_memory, cross_query_key_value_weight[1]).reshape(-1, XHEADS, HD)
        values = project(encoder_memory, cross_query_key_value_weight[2]).reshape(-1, XHEADS, HD)
        cross_allowed = (decoder_doc[:, None] == key_doc[None, :]) & live_keys[None, :]
        mixture = attend(queries, key_rows, values, cross_allowed).reshape(-1, XHEADS * HD)
        update = jnp.dot(mixture, w_cross_out, preferred_element_type=jnp.float32)
        closing_rows = norm_rows(docid_rows.astype(jnp.float32) + update, dec_gain[1]).astype(jnp.bfloat16)
        scores_vocab = jnp.dot(closing_rows, docid_head_weight, preferred_element_type=jnp.float32)
        totals = jnp.log(lax.optimization_barrier(jnp.sum(jnp.exp(scores_vocab), axis=-1)))
        picked = jnp.take_along_axis(scores_vocab, targets[:, None].astype(jnp.int32), axis=-1)[:, 0]
        return (scores_vocab.astype(jnp.bfloat16), totals - picked)
    logits, token_loss = lax.map(per_sample, (document_token_embedding, doc_lengths, docid_embed, docid_targets))
    return (logits, token_loss, jnp.mean(token_loss))
```

```python
import functools

import jax
import jax.numpy as jnp
from jax import lax
from jax.experimental import pallas as pl
from jax.experimental.pallas import tpu as pltpu
from jax.sharding import PartitionSpec as P

HD = 64
GROUPS = 4
WTILE = 512
PARTS = 4
CHUNKS = 8
AHEAD = 2
MESH = pl.DeviceIdType.MESH


def from_partner(block, axis, distance):
    count = lax.axis_size(axis)
    route = []
    for low in range(count):
        high = low | 1 << distance
        if high != low and high < count:
            route += [(low, high), (high, low)]
    return lax.ppermute(block, axis, route)


def from_behind(block, axis, distance):
    devices = range(lax.axis_size(axis))
    route = [(i - distance, i) for i in devices if i - distance in devices]
    return lax.ppermute(block, axis, route)


def passed_along(shard, axis, by):
    size = lax.axis_size(axis)
    return lax.ppermute(shard, axis, [(i, (i + by) % size) for i in range(size)])


def norm_rows(values, gain):
    values = values.astype(jnp.float32)
    scale = lax.rsqrt(jnp.mean(values * values, axis=-1, keepdims=True) + 1e-06)
    return values * scale * gain


def attend(queries, key_rows, values, allowed):
    scores = jnp.einsum("qhe,khe->hqk", queries, key_rows, preferred_element_type=jnp.float32)
    attention_weight_rows = jnp.where(allowed[None], jnp.exp(scores), 0.0)
    probabilities = (
        attention_weight_rows / jnp.sum(attention_weight_rows, axis=-1, keepdims=True)
    ).astype(jnp.bfloat16)
    mixture = jnp.einsum("hqk,khe->qhe", probabilities, values, preferred_element_type=jnp.float32)
    return mixture.astype(jnp.bfloat16)


def live_keys(lengths, key_doc, key_place):
    owners = jnp.arange(lengths.shape[0])
    matches = (key_doc[:, None] == owners[None, :]) & (key_place[:, None] < lengths[None, :])
    return jnp.any(matches, axis=1)


def lane_gather(own_rows, lane_bits, lane_index, concat_dim):
    for bit_number in range(lane_bits):
        partner = from_partner(own_rows, "section", bit_number)
        lower_half = lane_index // (1 << bit_number) % 2 == 0
        own_rows = jnp.where(
            lower_half,
            jnp.concatenate([own_rows, partner], concat_dim),
            jnp.concatenate([partner, own_rows], concat_dim),
        )
    return own_rows


def lane_reduce(totals, lane_bits, lane_index):
    for bit_number in reversed(range(lane_bits)):
        half_rows = totals.shape[0] // 2
        lower_half = lane_index // (1 << bit_number) % 2 == 0
        kept_rows = jnp.where(lower_half, totals[:half_rows], totals[half_rows:])
        outgoing = jnp.where(lower_half, totals[half_rows:], totals[:half_rows])
        totals = kept_rows + from_partner(outgoing, "section", bit_number)
    return totals


def relay_memory(encoder_memory, group_index, lane_count):
    encoder_memory = jnp.where(group_index == 0, encoder_memory, jnp.zeros_like(encoder_memory))
    for stride in (1, 2):
        encoder_memory = encoder_memory + from_behind(
            encoder_memory, "section", stride * lane_count
        )
    return encoder_memory


def shards(
    document_token_embedding,
    doc_lengths,
    docid_embed,
    docid_targets,
    enc_gain,
    dec_gain,
    w_enc_qkv,
    w_enc_out,
    cross_query_key_value_weight,
    w_cross_out,
    docid_head_weight,
):
    lane_count = lax.axis_size("section") // GROUPS
    lane_bits = lane_count.bit_length() - 1
    section_index = lax.axis_index("section")
    group_index = section_index // lane_count
    lane_index = section_index % lane_count
    micro_count, row_count, model_width = document_token_embedding.shape
    doc_count = doc_lengths.shape[1]
    doc_span = row_count // doc_count
    block_rows = row_count // lane_count
    local_heads = w_enc_qkv.shape[1] // HD
    positions = jnp.arange(row_count)
    key_doc = positions // doc_span
    key_place = positions % doc_span
    same_doc = key_doc[:, None] == key_doc[None, :]

    def partial_update(normed, lengths):
        allowed = same_doc & live_keys(lengths, key_doc, key_place)[None, :]
        projected = jnp.einsum(
            "rd,mcd->mrc", normed, w_enc_qkv, preferred_element_type=jnp.float32
        ).astype(jnp.bfloat16)
        projected = projected.reshape(3, row_count, local_heads, HD)
        mixture = attend(projected[0], projected[1], projected[2], allowed).reshape(row_count, -1)
        return jnp.dot(mixture, w_enc_out, preferred_element_type=jnp.float32)

    def section_step(step_index, loop_state):
        handed, encoder_memory = loop_state
        micro_index = step_index - group_index
        slot_index = jnp.clip(micro_index, 0, micro_count - 1)
        lengths = lax.dynamic_index_in_dim(doc_lengths, slot_index, 0, keepdims=False)
        layer_gain = lax.dynamic_index_in_dim(enc_gain, group_index, 0, keepdims=False)
        incoming = lax.dynamic_index_in_dim(
            document_token_embedding, jnp.minimum(step_index, micro_count - 1), 0, keepdims=False
        )
        incoming = lax.dynamic_slice_in_dim(incoming, lane_index * block_rows, block_rows, 0)
        current = jnp.where(group_index == 0, incoming, handed)
        normed = lane_gather(
            norm_rows(current, layer_gain).astype(jnp.bfloat16), lane_bits, lane_index, 0
        )
        summed = lane_reduce(partial_update(normed, lengths), lane_bits, lane_index)
        result = (current.astype(jnp.float32) + summed).astype(jnp.bfloat16)
        handed = passed_along(result, "section", lane_count)
        finished_index = step_index - (GROUPS - 1)
        finished_slot = jnp.clip(finished_index, 0, micro_count - 1)
        keeping = (group_index == 0) & (finished_index >= 0) & (finished_index < micro_count)
        stored = lax.dynamic_update_index_in_dim(encoder_memory, handed, finished_slot, 0)
        encoder_memory = jnp.where(keeping, stored, encoder_memory)
        return (handed, encoder_memory)

    handed = jnp.zeros((block_rows, model_width), jnp.bfloat16)
    encoder_memory = jnp.zeros((micro_count, block_rows, model_width), jnp.bfloat16)
    handed, encoder_memory = lax.fori_loop(
        0, micro_count + GROUPS - 1, section_step, (handed, encoder_memory)
    )
    encoder_memory = norm_rows(encoder_memory, enc_gain[GROUPS]).astype(jnp.bfloat16)
    encoder_memory = relay_memory(encoder_memory, group_index, lane_count)
    encoder_memory = lane_gather(encoder_memory, lane_bits, lane_index, 1)
    decoder_rows = docid_embed.shape[1]
    docid_span = decoder_rows // doc_count
    decoder_doc = jnp.arange(decoder_rows) // docid_span
    cross_heads = cross_query_key_value_weight.shape[1] // HD
    dec_normed = norm_rows(docid_embed, dec_gain[0]).astype(jnp.bfloat16)
    queries = jnp.einsum(
        "brd,cd->brc",
        dec_normed,
        cross_query_key_value_weight[0],
        preferred_element_type=jnp.float32,
    ).astype(jnp.bfloat16)
    memory_heads = jnp.einsum(
        "pye,qve->qpyv",
        encoder_memory,
        cross_query_key_value_weight[1:],
        preferred_element_type=jnp.float32,
    ).astype(jnp.bfloat16)

    def cross_one(sample_queries, sample_keys, sample_values, lengths):
        allowed = (decoder_doc[:, None] == key_doc[None, :]) & live_keys(
            lengths, key_doc, key_place
        )[None, :]
        return attend(sample_queries, sample_keys, sample_values, allowed)

    mixture = jax.vmap(cross_one)(
        queries.reshape(micro_count, decoder_rows, cross_heads, HD),
        memory_heads[0].reshape(micro_count, row_count, cross_heads, HD),
        memory_heads[1].reshape(micro_count, row_count, cross_heads, HD),
        doc_lengths,
    )
    cross_terms = jnp.einsum(
        "brc,cd->brd",
        mixture.reshape(micro_count, decoder_rows, -1),
        w_cross_out,
        preferred_element_type=jnp.float32,
    )
    cross_sum = lax.psum(cross_terms, "section")
    closing_rows = norm_rows(docid_embed.astype(jnp.float32) + cross_sum, dec_gain[1]).astype(
        jnp.bfloat16
    )
    scores_vocab = jnp.einsum(
        "brd,dv->brv", closing_rows, docid_head_weight, preferred_element_type=jnp.float32
    )
    vocab_local = docid_head_weight.shape[1]
    vocab_start = section_index * vocab_local
    matches = docid_targets[..., None] == vocab_start + jnp.arange(vocab_local)
    exponent_total, picked = lax.psum(
        (
            jnp.sum(jnp.exp(scores_vocab), axis=-1),
            jnp.sum(jnp.where(matches, scores_vocab, 0.0), axis=-1),
        ),
        "section",
    )
    token_loss = jnp.log(exponent_total) - picked
    mean_loss = lax.psum(jnp.sum(token_loss), "rep") / (token_loss.size * lax.axis_size("rep"))
    return (scores_vocab.astype(jnp.bfloat16), token_loss, mean_loss)


def encoder_kernel(
    sent,
    x_ref,
    gain_ref,
    row_doc_ref,
    key_doc_ref,
    wqkv_ref,
    wout_ref,
    mem_ref,
    wqkv_v,
    wout_v,
    hid,
    work,
    part,
    qkv,
    mix,
    w_sem,
    o_sem,
    x_sem,
    gs,
    gr,
    rs,
    rr,
    zs,
    zr,
    bs,
    br,
    ms,
    mr,
):
    rows, width = hid.shape
    half = sent // 2
    columns = width // PARTS
    tiles = wqkv_v.shape[0]
    per = tiles // 3
    section = lax.axis_index("section")
    count = lax.axis_size("section")
    group = section // 2
    lane = section % 2
    partner = section + 1 - 2 * lane
    ahead = lax.rem(section + 2, count)
    behind = lax.rem(section + count - 2, count)
    own = pl.ds(pl.multiple_of(lane * half, 16), half)
    other = pl.ds(pl.multiple_of((1 - lane) * half, 16), half)

    def cols(c):
        return pl.ds(pl.multiple_of(c * columns, columns), columns)

    def weight_copy(j):
        return pltpu.make_async_copy(
            wqkv_ref.at[j // per, pl.ds((j % per) * WTILE, WTILE)], wqkv_v.at[j], w_sem.at[j]
        )

    def out_copy(c):
        return pltpu.make_async_copy(wout_ref.at[:, cols(c)], wout_v.at[c], o_sem.at[c])

    def remote(src, dst, send, recv, device):
        return pltpu.make_async_remote_copy(
            src_ref=src,
            dst_ref=dst,
            send_sem=send,
            recv_sem=recv,
            device_id={"section": device},
            device_id_type=MESH,
        )

    def gather(c, block):
        return remote(hid.at[block, cols(c)], hid.at[block, cols(c)], gs.at[c], gr.at[c], partner)

    def reduce(c):
        return remote(work.at[other, cols(c)], part.at[:, cols(c)], rs.at[c], rr.at[c], partner)

    def hand(c):
        return remote(hid.at[own, cols(c)], hid.at[own, cols(c)], zs.at[c], zr.at[c], ahead)

    def back(c):
        return remote(mem_ref.at[own, cols(c)], mem_ref.at[own, cols(c)], bs.at[c], br.at[c], behind)

    def spread(c, block):
        return remote(
            mem_ref.at[block, cols(c)], mem_ref.at[block, cols(c)], ms.at[c], mr.at[c], partner
        )

    def each(size, body):
        def step(i, carry):
            body(i)
            return carry

        lax.fori_loop(0, size, step, 0)

    entry = pltpu.make_async_copy(x_ref.at[pl.ds(0, sent)], hid.at[pl.ds(0, sent)], x_sem)

    @pl.when(group == 0)
    def _():
        entry.start()

    for j in range(tiles):
        weight_copy(j).start()
    for c in range(PARTS):
        out_copy(c).start()

    barrier = pltpu.get_barrier_semaphore()
    for device in (partner, ahead, behind):
        pl.semaphore_signal(barrier, inc=1, device_id={"section": device}, device_id_type=MESH)
    pl.semaphore_wait(barrier, 3)

    if sent < rows:
        hid[sent:, :] = jnp.zeros((rows - sent, width), hid.dtype)
    if sent < mem_ref.shape[0]:
        mem_ref[sent:, :] = jnp.zeros((mem_ref.shape[0] - sent, width), mem_ref.dtype)

    @pl.when(group == 0)
    def _():
        entry.wait()

    @pl.when(group > 0)
    def _():
        def arrive(c):
            hand(c).wait_recv()
            gather(c, own).start()

        each(PARTS, arrive)

        def complete(c):
            gather(c, other).wait_recv()
            gather(c, own).wait_send()

        each(PARTS, complete)

    def norm(r):
        block = pl.ds(pl.multiple_of(r * 16, 16), 16)
        values = hid[block, :].astype(jnp.float32)
        scale = lax.rsqrt(jnp.mean(values * values, axis=-1, keepdims=True) + 1e-06)
        work[block, :] = (values * scale * gain_ref[...]).astype(work.dtype)

    each(rows // 16, norm)

    def project(j):
        pltpu.make_async_copy(
            wqkv_ref.at[0, pl.ds(0, WTILE)], wqkv_v.at[j], w_sem.at[j]
        ).wait()
        qkv[j] = lax.dot_general(
            work[...], wqkv_v[j], (((1,), (1,)), ((), ())), preferred_element_type=jnp.float32
        ).astype(qkv.dtype)

    each(tiles, project)
    pairs = WTILE // (2 * HD)

    def attend_pair(p):
        tile = p // pairs
        span = pl.ds(pl.multiple_of((p % pairs) * 2 * HD, 2 * HD), 2 * HD)
        queries = qkv[tile, :, span]
        keys = qkv[per + tile, :, span]
        values = qkv[2 * per + tile, :, span]
        allowed = row_doc_ref[...] == key_doc_ref[...]
        first = lax.broadcasted_iota(jnp.int32, (rows, 2 * HD), 1) < HD
        mixed = []
        for side in range(2):
            keep = first if side == 0 else jnp.logical_not(first)
            chosen = jnp.where(keep, queries.astype(jnp.float32), 0.0).astype(jnp.bfloat16)
            scores = lax.dot_general(
                chosen, keys, (((1,), (1,)), ((), ())), preferred_element_type=jnp.float32
            )
            weights = jnp.where(allowed, jnp.exp(scores), 0.0)
            shares = (weights / jnp.sum(weights, axis=-1, keepdims=True)).astype(jnp.bfloat16)
            mixed.append(jnp.dot(shares, values, preferred_element_type=jnp.float32))
        mix[:, pl.ds(pl.multiple_of(p * 2 * HD, 2 * HD), 2 * HD)] = jnp.where(
            first, mixed[0], mixed[1]
        ).astype(mix.dtype)

    each(per * pairs, attend_pair)

    def output(c):
        out_copy(c).wait()
        work[:, cols(c)] = jnp.dot(
            mix[...], wout_v[c], preferred_element_type=jnp.float32
        ).astype(work.dtype)
        reduce(c).start()

    each(PARTS, output)

    def total(c):
        reduce(c).wait_recv()
        return (
            hid[own, cols(c)].astype(jnp.float32)
            + work[own, cols(c)].astype(jnp.float32)
            + part[:, cols(c)].astype(jnp.float32)
        ).astype(hid.dtype)

    @pl.when(group < GROUPS - 1)
    def _():
        def finish(c):
            hid[own, cols(c)] = total(c)
            hand(c).start()

        each(PARTS, finish)

        def relay(c):
            back(c).wait_recv()

            @pl.when(group > 0)
            def _():
                back(c).start()

            spread(c, own).start()

        each(PARTS, relay)

    @pl.when(group == GROUPS - 1)
    def _():
        def finish(c):
            mem_ref[own, cols(c)] = total(c)
            back(c).start()
            spread(c, own).start()

        each(PARTS, finish)

    def drain(c):
        spread(c, other).wait_recv()
        spread(c, own).wait_send()
        reduce(c).wait_send()

        @pl.when(group < GROUPS - 1)
        def _():
            hand(c).wait_send()

        @pl.when(group > 0)
        def _():
            back(c).wait_send()

    each(PARTS, drain)


def encode(rows, sent, number, x, gain, row_doc, key_doc, wqkv, wout):
    total_rows, width = x.shape
    inner = wout.shape[0]
    tiles = 3 * (inner // WTILE)
    dma = pltpu.SemaphoreType.DMA
    vmem = pl.BlockSpec(memory_space=pltpu.VMEM)
    anywhere = pl.BlockSpec(memory_space=pl.ANY)
    return pl.pallas_call(
        functools.partial(encoder_kernel, sent),
        out_shape=jax.ShapeDtypeStruct((total_rows, width), jnp.bfloat16),
        in_specs=[anywhere, vmem, vmem, vmem, anywhere, anywhere],
        out_specs=vmem,
        scratch_shapes=[
            pltpu.VMEM((tiles, WTILE, width), jnp.bfloat16),
            pltpu.VMEM((PARTS, inner, width // PARTS), jnp.bfloat16),
            pltpu.VMEM((rows, width), jnp.bfloat16),
            pltpu.VMEM((rows, width), jnp.bfloat16),
            pltpu.VMEM((sent // 2, width), jnp.bfloat16),
            pltpu.VMEM((tiles, rows, WTILE), jnp.bfloat16),
            pltpu.VMEM((rows, inner), jnp.bfloat16),
            dma((tiles,)),
            dma((PARTS,)),
            dma,
        ]
        + [dma((PARTS,))] * 10,
        compiler_params=pltpu.CompilerParams(
            collective_id=number, has_side_effects=True, vmem_limit_bytes=67043328
        ),
        name=f"encoder_{sent}",
    )(x, gain, row_doc[:rows, None], key_doc[None, :rows], wqkv, wout)


def stream_kernel(
    sent,
    x_ref,
    gain_ref,
    row_doc_ref,
    key_doc_ref,
    wqkv_ref,
    wout_ref,
    mem_ref,
    wqkv_v,
    wout_v,
    hid,
    work,
    part,
    acc,
    squares,
    mix,
    w_sem,
    o_sem,
    x_sem,
    gs,
    gr,
    rs,
    rr,
    zs,
    zr,
    bs,
    br,
    ms,
    mr,
):
    rows, width = hid.shape
    half = sent // 2
    chunks, tiles, tile_columns, columns = wqkv_v.shape
    per = tiles // 3
    section = lax.axis_index("section")
    count = lax.axis_size("section")
    group = section // 2
    lane = section % 2
    partner = section + 1 - 2 * lane
    ahead = lax.rem(section + 2, count)
    behind = lax.rem(section + count - 2, count)
    own = pl.ds(pl.multiple_of(lane * half, 16), half)
    other = pl.ds(pl.multiple_of((1 - lane) * half, 16), half)

    def cols(c):
        return pl.ds(pl.multiple_of(c * columns, columns), columns)

    def weight_copy(c):
        return pltpu.make_async_copy(wqkv_ref.at[:, :, cols(c)], wqkv_v.at[c], w_sem.at[c])

    def out_copy(c):
        return pltpu.make_async_copy(wout_ref.at[:, cols(c)], wout_v.at[c], o_sem.at[c])

    def remote(src, dst, send, recv, device):
        return pltpu.make_async_remote_copy(
            src_ref=src,
            dst_ref=dst,
            send_sem=send,
            recv_sem=recv,
            device_id={"section": device},
            device_id_type=MESH,
        )

    def gather(c, block):
        return remote(hid.at[block, cols(c)], hid.at[block, cols(c)], gs.at[c], gr.at[c], partner)

    def reduce(c):
        return remote(work.at[other, cols(c)], part.at[:, cols(c)], rs.at[c], rr.at[c], partner)

    def hand(c):
        return remote(hid.at[own, cols(c)], hid.at[own, cols(c)], zs.at[c], zr.at[c], ahead)

    def back(c):
        return remote(mem_ref.at[own, cols(c)], mem_ref.at[own, cols(c)], bs.at[c], br.at[c], behind)

    def spread(c, block):
        return remote(
            mem_ref.at[block, cols(c)], mem_ref.at[block, cols(c)], ms.at[c], mr.at[c], partner
        )

    def each(size, body):
        def step(i, carry):
            body(i)
            return carry

        lax.fori_loop(0, size, step, 0)

    entry = pltpu.make_async_copy(x_ref.at[pl.ds(0, sent)], hid.at[pl.ds(0, sent)], x_sem)

    @pl.when(group == 0)
    def _():
        entry.start()

    for c in range(chunks):
        weight_copy(c).start()
    for c in range(chunks):
        out_copy(c).start()

    barrier = pltpu.get_barrier_semaphore()
    for device in (partner, ahead, behind):
        pl.semaphore_signal(barrier, inc=1, device_id={"section": device}, device_id_type=MESH)
    pl.semaphore_wait(barrier, 3)

    if sent < rows:
        hid[sent:, :] = jnp.zeros((rows - sent, width), hid.dtype)
    if sent < mem_ref.shape[0]:
        mem_ref[sent:, :] = jnp.zeros((mem_ref.shape[0] - sent, width), mem_ref.dtype)
    acc[...] = jnp.zeros_like(acc)
    squares[...] = jnp.zeros_like(squares)

    def project(c, weight_dim):
        values = hid[:, cols(c)].astype(jnp.float32)
        squares[...] += jnp.sum(values * values, axis=-1, keepdims=True)
        scaled = (values * gain_ref[:, cols(c)]).astype(jnp.bfloat16)

        def some(t):
            for u in range(per):
                j = t * per + u
                acc[j] += lax.dot_general(
                    scaled,
                    wqkv_v[c, j],
                    (((1,), (weight_dim,)), ((), ())),
                    preferred_element_type=jnp.float32,
                )

        each(3, some)

    @pl.when(group == 0)
    def _():
        entry.wait()

        def first(c):
            weight_copy(c).wait()
            project(c, 1)

        each(chunks, first)

    @pl.when(group > 0)
    def _():
        side = tile_columns // 2

        def turn(c):
            weight_copy(c).wait()

            def block(j):
                whole = wqkv_v[c, j]
                for a in range(2):
                    for b in range(2):
                        piece = whole[a * side : (a + 1) * side, b * side : (b + 1) * side]
                        wqkv_v[c, j, b * side : (b + 1) * side, a * side : (a + 1) * side] = piece.T

            each(tiles, block)

        each(chunks, turn)

        def step(i):
            @pl.when(i < chunks)
            def _():
                hand(i).wait_recv()
                gather(i, own).start()

            @pl.when(i >= AHEAD)
            def _():
                gather(i - AHEAD, other).wait_recv()
                project(i - AHEAD, 0)

        each(chunks + AHEAD, step)

        def complete(c):
            gather(c, own).wait_send()

        each(chunks, complete)

    scale = lax.rsqrt(squares[...] * (1.0 / width) + 1e-06)
    pairs = tile_columns // (2 * HD)
    allowed = row_doc_ref[...] == key_doc_ref[...]
    allowed = jnp.concatenate([allowed, allowed], 0)
    first = lax.broadcasted_iota(jnp.int32, (rows, 2 * HD), 1) < HD

    def attend_tile(tile):
        for p in range(pairs):
            span = slice(p * 2 * HD, (p + 1) * 2 * HD)
            queries = acc[tile, :, span] * scale
            keys = (acc[per + tile, :, span] * scale).astype(jnp.bfloat16)
            values = (acc[2 * per + tile, :, span] * scale).astype(jnp.bfloat16)
            both = jnp.concatenate(
                [jnp.where(first, queries, 0.0), jnp.where(first, 0.0, queries)], 0
            ).astype(jnp.bfloat16)
            scores = lax.dot_general(
                both, keys, (((1,), (1,)), ((), ())), preferred_element_type=jnp.float32
            )
            weights = jnp.where(allowed, jnp.exp(scores), 0.0)
            shares = weights * (1.0 / jnp.sum(weights, axis=-1, keepdims=True))
            mixed = jnp.dot(shares.astype(jnp.bfloat16), values, preferred_element_type=jnp.float32)
            place = pl.multiple_of(tile * tile_columns + p * 2 * HD, 2 * HD)
            mix[:, pl.ds(place, 2 * HD)] = jnp.where(first, mixed[:rows], mixed[rows:]).astype(
                mix.dtype
            )

    each(per, attend_tile)

    def output(c):
        out_copy(c).wait()
        work[:, cols(c)] = jnp.dot(
            mix[...], wout_v[c], preferred_element_type=jnp.float32
        ).astype(work.dtype)
        reduce(c).start()

    each(chunks, output)

    def total(c):
        reduce(c).wait_recv()
        return (
            hid[own, cols(c)].astype(jnp.float32)
            + work[own, cols(c)].astype(jnp.float32)
            + part[:, cols(c)].astype(jnp.float32)
        ).astype(hid.dtype)

    @pl.when(group < GROUPS - 1)
    def _():
        def finish(c):
            hid[own, cols(c)] = total(c)
            hand(c).start()

        each(chunks, finish)

        def relay(c):
            back(c).wait_recv()

            @pl.when(group > 0)
            def _():
                back(c).start()

            spread(c, own).start()

        each(chunks, relay)

    @pl.when(group == GROUPS - 1)
    def _():
        def finish(c):
            mem_ref[own, cols(c)] = total(c)
            back(c).start()
            spread(c, own).start()

        each(chunks, finish)

    def drain(c):
        spread(c, other).wait_recv()
        spread(c, own).wait_send()
        reduce(c).wait_send()

        @pl.when(group < GROUPS - 1)
        def _():
            hand(c).wait_send()

        @pl.when(group > 0)
        def _():
            back(c).wait_send()

    each(chunks, drain)


def stream(rows, sent, number, x, gain, row_doc, key_doc, wqkv, wout):
    total_rows, width = x.shape
    inner = wout.shape[0]
    tiles = 3 * (inner // WTILE)
    dma = pltpu.SemaphoreType.DMA
    vmem = pl.BlockSpec(memory_space=pltpu.VMEM)
    anywhere = pl.BlockSpec(memory_space=pl.ANY)
    return pl.pallas_call(
        functools.partial(stream_kernel, sent),
        out_shape=jax.ShapeDtypeStruct((total_rows, width), jnp.bfloat16),
        in_specs=[anywhere, vmem, vmem, vmem, anywhere, anywhere],
        out_specs=vmem,
        scratch_shapes=[
            pltpu.VMEM((CHUNKS, tiles, WTILE, width // CHUNKS), jnp.bfloat16),
            pltpu.VMEM((CHUNKS, inner, width // CHUNKS), jnp.bfloat16),
            pltpu.VMEM((rows, width), jnp.bfloat16),
            pltpu.VMEM((rows, width), jnp.bfloat16),
            pltpu.VMEM((sent // 2, width), jnp.bfloat16),
            pltpu.VMEM((tiles, rows, WTILE), jnp.float32),
            pltpu.VMEM((rows, 1), jnp.float32),
            pltpu.VMEM((rows, inner), jnp.bfloat16),
            dma((CHUNKS,)),
            dma((CHUNKS,)),
            dma,
        ]
        + [dma((CHUNKS,))] * 10,
        compiler_params=pltpu.CompilerParams(
            collective_id=number, has_side_effects=True, vmem_limit_bytes=67043328
        ),
        name=f"stream_{sent}",
    )(x, gain, row_doc[:rows, None], key_doc[None, :rows], wqkv.reshape(tiles, WTILE, width), wout)


def butterfly(value, axis, combine):
    for bit in range(lax.axis_size(axis).bit_length() - 1):
        value = combine(value, from_partner(value, axis, bit))
    return value


def greet(me, count):
    barrier = pltpu.get_barrier_semaphore()
    for k in range(1, count):
        pl.semaphore_signal(
            barrier, inc=1, device_id={"section": lax.rem(me + k, count)}, device_id_type=MESH
        )
    pl.semaphore_wait(barrier, count - 1)


def to_peer(src, dst, send, recv, peer):
    return pltpu.make_async_remote_copy(
        src_ref=src,
        dst_ref=dst,
        send_sem=send,
        recv_sem=recv,
        device_id={"section": peer},
        device_id_type=MESH,
    )


def closing_kernel(terms, residual, gain, out, landed, s1, r1, s2, r2):
    count = terms.shape[0]
    me = lax.axis_index("section")
    greet(me, count)

    def scatter(k, slot):
        peer = lax.rem(me + k, count)
        return to_peer(terms.at[peer], landed.at[slot], s1.at[k], r1.at[k], peer)

    def gather(k, slot):
        return to_peer(out.at[slot], out.at[slot], s2.at[k], r2.at[k], lax.rem(me + k, count))

    for k in range(1, count):
        scatter(k, me).start()
    total = residual[...] + terms[me].astype(jnp.float32)
    for k in range(1, count):
        slot = lax.rem(me + count - k, count)
        scatter(k, slot).wait_recv()
        total = total + landed[slot].astype(jnp.float32)
    scale = lax.rsqrt(jnp.mean(total * total, axis=-1, keepdims=True) + 1e-06)
    out[me] = (total * scale * gain[...]).astype(out.dtype)
    for k in range(1, count):
        gather(k, me).start()
    for k in range(1, count):
        gather(k, lax.rem(me + count - k, count)).wait_recv()
    for k in range(1, count):
        scatter(k, me).wait_send()
        gather(k, me).wait_send()


def closing_rows_of(terms, residual, gain):
    count = terms.shape[0]
    dma = pltpu.SemaphoreType.DMA
    vmem = pl.BlockSpec(memory_space=pltpu.VMEM)
    return pl.pallas_call(
        closing_kernel,
        out_shape=jax.ShapeDtypeStruct(terms.shape, jnp.bfloat16),
        in_specs=[vmem] * 3,
        out_specs=vmem,
        scratch_shapes=[pltpu.VMEM(terms.shape, jnp.bfloat16)] + [dma((count,))] * 4,
        compiler_params=pltpu.CompilerParams(collective_id=8, has_side_effects=True),
        name="closing",
    )(terms, residual, gain)


def sums_kernel(value, out, landed, send, recv):
    count = landed.shape[0]
    me = lax.axis_index("section")
    greet(me, count)

    def share(k, slot):
        return to_peer(value, landed.at[slot], send.at[k], recv.at[k], lax.rem(me + k, count))

    for k in range(1, count):
        share(k, me).start()
    landed[me] = value[...]
    for k in range(1, count):
        share(k, lax.rem(me + count - k, count)).wait_recv()
    total = landed[0]
    for k in range(1, count):
        total = total + landed[k]
    out[...] = total
    for k in range(1, count):
        share(k, me).wait_send()


def section_sum(value, count):
    dma = pltpu.SemaphoreType.DMA
    vmem = pl.BlockSpec(memory_space=pltpu.VMEM)
    return pl.pallas_call(
        sums_kernel,
        out_shape=jax.ShapeDtypeStruct(value.shape, value.dtype),
        in_specs=[vmem],
        out_specs=vmem,
        scratch_shapes=[pltpu.VMEM((count,) + value.shape, value.dtype)] + [dma((count,))] * 2,
        compiler_params=pltpu.CompilerParams(collective_id=9, has_side_effects=True),
        name="section_sum",
    )(value)


def fast_shards(
    document_token_embedding,
    doc_lengths,
    docid_embed,
    docid_targets,
    enc_gain,
    dec_gain,
    w_enc_qkv,
    w_enc_out,
    cross_query_key_value_weight,
    w_cross_out,
    docid_head_weight,
):
    section_index = lax.axis_index("section")
    group_index = section_index // 2
    micro_count, row_count, width = document_token_embedding.shape
    doc_count = doc_lengths.shape[1]
    doc_span = row_count // doc_count
    all_rows = micro_count * row_count
    positions = jnp.arange(all_rows)
    lengths = doc_lengths.reshape(-1)
    live = (jnp.arange(doc_span)[None, :] < lengths[:, None]).reshape(-1)
    ends = jnp.cumsum(lengths)
    live_count = ends[-1]
    starts = jnp.concatenate([jnp.zeros((1,), ends.dtype), ends[:-1]])
    inside = (positions[:, None] >= starts[None, :]) & (positions[:, None] < ends[None, :])
    docs = jnp.arange(lengths.shape[0])
    row_doc = jnp.sum(jnp.where(inside, docs[None, :], 0), axis=1).astype(jnp.int32)
    key_doc = jnp.where(positions < live_count, row_doc, -1).astype(jnp.int32)
    source = jnp.sum(
        jnp.where(inside, docs[None, :] * doc_span + positions[:, None] - starts[None, :], 0), axis=1
    )
    source = jnp.where(positions < live_count, source, -1)
    pick = (source[:, None] == positions[None, :]).astype(jnp.bfloat16)
    packed = jnp.dot(
        pick,
        document_token_embedding.reshape(all_rows, width),
        preferred_element_type=jnp.float32,
    ).astype(jnp.bfloat16)
    largest = butterfly(live_count.astype(jnp.float32)[None], "rep", jnp.maximum)[0]
    gain = lax.dynamic_slice_in_dim(enc_gain, group_index, 1, 0)
    unit = all_rows // 2
    sizes = [(unit, unit * 3 // 4), (unit, unit), (all_rows, all_rows)]
    choice = jnp.sum(jnp.stack([(largest > sent).astype(jnp.int32) for _, sent in sizes[:-1]]))
    branches = [
        functools.partial(encode if rows > unit else stream, rows, sent, number)
        for number, (rows, sent) in enumerate(sizes)
    ]
    hidden = lax.switch(
        choice, branches, packed, gain, row_doc, key_doc, w_enc_qkv, w_enc_out
    )
    memory = norm_rows(hidden, enc_gain[GROUPS]).astype(jnp.bfloat16)

    decoder_rows = docid_embed.shape[1]
    every = micro_count * decoder_rows
    docid_span = decoder_rows // doc_count
    decoder_doc = jnp.arange(every) // docid_span
    cross_heads = cross_query_key_value_weight.shape[1] // HD
    flat_docid = docid_embed.reshape(every, width)
    dec_normed = norm_rows(flat_docid, dec_gain[0]).astype(jnp.bfloat16)

    def project(values, weight):
        return (
            jnp.einsum("rd,cd->rc", values, weight, preferred_element_type=jnp.float32)
            .astype(jnp.bfloat16)
            .reshape(-1, cross_heads, HD)
        )

    queries = project(dec_normed, cross_query_key_value_weight[0])
    keys = project(memory, cross_query_key_value_weight[1])
    values = project(memory, cross_query_key_value_weight[2])
    allowed = decoder_doc[:, None] == key_doc[None, :]
    mixture = attend(queries, keys, values, allowed).reshape(every, -1)
    cross_terms = jnp.dot(mixture, w_cross_out, preferred_element_type=jnp.float32)
    section_count = lax.axis_size("section")
    share = every // section_count
    residual = lax.dynamic_slice_in_dim(flat_docid, section_index * share, share, 0)
    closing = closing_rows_of(
        cross_terms.astype(jnp.bfloat16).reshape(section_count, share, width),
        residual.astype(jnp.float32),
        dec_gain[1:2],
    ).reshape(every, width)
    scores_vocab = jnp.dot(closing, docid_head_weight, preferred_element_type=jnp.float32)
    vocab_local = docid_head_weight.shape[1]
    targets = docid_targets.reshape(-1)
    matches = targets[:, None] == section_index * vocab_local + jnp.arange(vocab_local)
    sums = jnp.stack(
        [
            jnp.sum(jnp.exp(scores_vocab), axis=-1),
            jnp.sum(jnp.where(matches, scores_vocab, 0.0), axis=-1),
        ]
    )
    padding = ((0, -sums.shape[0] % 8), (0, -sums.shape[1] % 128))
    sums = section_sum(jnp.pad(sums, padding), section_count)[:2, :every]
    token_loss = jnp.log(sums[0]) - sums[1]
    loss_sum = butterfly(jnp.sum(token_loss)[None], "rep", jnp.add)[0]
    mean_loss = loss_sum / (token_loss.size * lax.axis_size("rep"))
    logits = scores_vocab.astype(jnp.bfloat16).reshape(micro_count, decoder_rows, vocab_local)
    return (logits, token_loss.reshape(docid_targets.shape), mean_loss)


def solution(mesh):
    in_specs = (
        P("rep", None, None),
        P("rep", None),
        P("rep", None, None),
        P("rep", None),
        P(),
        P(),
        P(None, "section", None),
        P("section", None),
        P(None, "section", None),
        P("section", None),
        P(None, "section"),
    )
    out_specs = (P("rep", None, "section"), P("rep", None), P())
    local = shards if mesh.shape["section"] != 2 * GROUPS else fast_shards
    return jax.shard_map(local, mesh=mesh, in_specs=in_specs, out_specs=out_specs, check_vma=False)
```

```python
import functools

import jax
import jax.numpy as jnp
from jax import lax
from jax.experimental import pallas as pl
from jax.experimental.pallas import tpu as pltpu
from jax.sharding import PartitionSpec as P

HD = 64
GROUPS = 4
WTILE = 512
PARTS = 4
CHUNKS = 8
AHEAD = 2
MESH = pl.DeviceIdType.MESH


def from_partner(block, axis, distance):
    count = lax.axis_size(axis)
    route = []
    for low in range(count):
        high = low | 1 << distance
        if high != low and high < count:
            route += [(low, high), (high, low)]
    return lax.ppermute(block, axis, route)


def from_behind(block, axis, distance):
    devices = range(lax.axis_size(axis))
    route = [(i - distance, i) for i in devices if i - distance in devices]
    return lax.ppermute(block, axis, route)


def passed_along(shard, axis, by):
    size = lax.axis_size(axis)
    return lax.ppermute(shard, axis, [(i, (i + by) % size) for i in range(size)])


def norm_rows(values, gain):
    values = values.astype(jnp.float32)
    scale = lax.rsqrt(jnp.mean(values * values, axis=-1, keepdims=True) + 1e-06)
    return values * scale * gain


def attend(queries, key_rows, values, allowed):
    scores = jnp.einsum("qhe,khe->hqk", queries, key_rows, preferred_element_type=jnp.float32)
    attention_weight_rows = jnp.where(allowed[None], jnp.exp(scores), 0.0)
    probabilities = (
        attention_weight_rows / jnp.sum(attention_weight_rows, axis=-1, keepdims=True)
    ).astype(jnp.bfloat16)
    mixture = jnp.einsum("hqk,khe->qhe", probabilities, values, preferred_element_type=jnp.float32)
    return mixture.astype(jnp.bfloat16)


def live_keys(lengths, key_doc, key_place):
    owners = jnp.arange(lengths.shape[0])
    matches = (key_doc[:, None] == owners[None, :]) & (key_place[:, None] < lengths[None, :])
    return jnp.any(matches, axis=1)


def lane_gather(own_rows, lane_bits, lane_index, concat_dim):
    for bit_number in range(lane_bits):
        partner = from_partner(own_rows, "section", bit_number)
        lower_half = lane_index // (1 << bit_number) % 2 == 0
        own_rows = jnp.where(
            lower_half,
            jnp.concatenate([own_rows, partner], concat_dim),
            jnp.concatenate([partner, own_rows], concat_dim),
        )
    return own_rows


def lane_reduce(totals, lane_bits, lane_index):
    for bit_number in reversed(range(lane_bits)):
        half_rows = totals.shape[0] // 2
        lower_half = lane_index // (1 << bit_number) % 2 == 0
        kept_rows = jnp.where(lower_half, totals[:half_rows], totals[half_rows:])
        outgoing = jnp.where(lower_half, totals[half_rows:], totals[:half_rows])
        totals = kept_rows + from_partner(outgoing, "section", bit_number)
    return totals


def relay_memory(encoder_memory, group_index, lane_count):
    encoder_memory = jnp.where(group_index == 0, encoder_memory, jnp.zeros_like(encoder_memory))
    for stride in (1, 2):
        encoder_memory = encoder_memory + from_behind(
            encoder_memory, "section", stride * lane_count
        )
    return encoder_memory


def shards(
    document_token_embedding,
    doc_lengths,
    docid_embed,
    docid_targets,
    enc_gain,
    dec_gain,
    w_enc_qkv,
    w_enc_out,
    cross_query_key_value_weight,
    w_cross_out,
    docid_head_weight,
):
    lane_count = lax.axis_size("section") // GROUPS
    lane_bits = lane_count.bit_length() - 1
    section_index = lax.axis_index("section")
    group_index = section_index // lane_count
    lane_index = section_index % lane_count
    micro_count, row_count, model_width = document_token_embedding.shape
    doc_count = doc_lengths.shape[1]
    doc_span = row_count // doc_count
    block_rows = row_count // lane_count
    local_heads = w_enc_qkv.shape[1] // HD
    positions = jnp.arange(row_count)
    key_doc = positions // doc_span
    key_place = positions % doc_span
    same_doc = key_doc[:, None] == key_doc[None, :]

    def partial_update(normed, lengths):
        allowed = same_doc & live_keys(lengths, key_doc, key_place)[None, :]
        projected = jnp.einsum(
            "rd,mcd->mrc", normed, w_enc_qkv, preferred_element_type=jnp.float32
        ).astype(jnp.bfloat16)
        projected = projected.reshape(3, row_count, local_heads, HD)
        mixture = attend(projected[0], projected[1], projected[2], allowed).reshape(row_count, -1)
        return jnp.dot(mixture, w_enc_out, preferred_element_type=jnp.float32)

    def section_step(step_index, loop_state):
        handed, encoder_memory = loop_state
        micro_index = step_index - group_index
        slot_index = jnp.clip(micro_index, 0, micro_count - 1)
        lengths = lax.dynamic_index_in_dim(doc_lengths, slot_index, 0, keepdims=False)
        layer_gain = lax.dynamic_index_in_dim(enc_gain, group_index, 0, keepdims=False)
        incoming = lax.dynamic_index_in_dim(
            document_token_embedding, jnp.minimum(step_index, micro_count - 1), 0, keepdims=False
        )
        incoming = lax.dynamic_slice_in_dim(incoming, lane_index * block_rows, block_rows, 0)
        current = jnp.where(group_index == 0, incoming, handed)
        normed = lane_gather(
            norm_rows(current, layer_gain).astype(jnp.bfloat16), lane_bits, lane_index, 0
        )
        summed = lane_reduce(partial_update(normed, lengths), lane_bits, lane_index)
        result = (current.astype(jnp.float32) + summed).astype(jnp.bfloat16)
        handed = passed_along(result, "section", lane_count)
        finished_index = step_index - (GROUPS - 1)
        finished_slot = jnp.clip(finished_index, 0, micro_count - 1)
        keeping = (group_index == 0) & (finished_index >= 0) & (finished_index < micro_count)
        stored = lax.dynamic_update_index_in_dim(encoder_memory, handed, finished_slot, 0)
        encoder_memory = jnp.where(keeping, stored, encoder_memory)
        return (handed, encoder_memory)

    handed = jnp.zeros((block_rows, model_width), jnp.bfloat16)
    encoder_memory = jnp.zeros((micro_count, block_rows, model_width), jnp.bfloat16)
    handed, encoder_memory = lax.fori_loop(
        0, micro_count + GROUPS - 1, section_step, (handed, encoder_memory)
    )
    encoder_memory = norm_rows(encoder_memory, enc_gain[GROUPS]).astype(jnp.bfloat16)
    encoder_memory = relay_memory(encoder_memory, group_index, lane_count)
    encoder_memory = lane_gather(encoder_memory, lane_bits, lane_index, 1)
    decoder_rows = docid_embed.shape[1]
    docid_span = decoder_rows // doc_count
    decoder_doc = jnp.arange(decoder_rows) // docid_span
    cross_heads = cross_query_key_value_weight.shape[1] // HD
    dec_normed = norm_rows(docid_embed, dec_gain[0]).astype(jnp.bfloat16)
    queries = jnp.einsum(
        "brd,cd->brc",
        dec_normed,
        cross_query_key_value_weight[0],
        preferred_element_type=jnp.float32,
    ).astype(jnp.bfloat16)
    memory_heads = jnp.einsum(
        "pye,qve->qpyv",
        encoder_memory,
        cross_query_key_value_weight[1:],
        preferred_element_type=jnp.float32,
    ).astype(jnp.bfloat16)

    def cross_one(sample_queries, sample_keys, sample_values, lengths):
        allowed = (decoder_doc[:, None] == key_doc[None, :]) & live_keys(
            lengths, key_doc, key_place
        )[None, :]
        return attend(sample_queries, sample_keys, sample_values, allowed)

    mixture = jax.vmap(cross_one)(
        queries.reshape(micro_count, decoder_rows, cross_heads, HD),
        memory_heads[0].reshape(micro_count, row_count, cross_heads, HD),
        memory_heads[1].reshape(micro_count, row_count, cross_heads, HD),
        doc_lengths,
    )
    cross_terms = jnp.einsum(
        "brc,cd->brd",
        mixture.reshape(micro_count, decoder_rows, -1),
        w_cross_out,
        preferred_element_type=jnp.float32,
    )
    cross_sum = lax.psum(cross_terms, "section")
    closing_rows = norm_rows(docid_embed.astype(jnp.float32) + cross_sum, dec_gain[1]).astype(
        jnp.bfloat16
    )
    scores_vocab = jnp.einsum(
        "brd,dv->brv", closing_rows, docid_head_weight, preferred_element_type=jnp.float32
    )
    vocab_local = docid_head_weight.shape[1]
    vocab_start = section_index * vocab_local
    matches = docid_targets[..., None] == vocab_start + jnp.arange(vocab_local)
    exponent_total, picked = lax.psum(
        (
            jnp.sum(jnp.exp(scores_vocab), axis=-1),
            jnp.sum(jnp.where(matches, scores_vocab, 0.0), axis=-1),
        ),
        "section",
    )
    token_loss = jnp.log(exponent_total) - picked
    mean_loss = lax.psum(jnp.sum(token_loss), "rep") / (token_loss.size * lax.axis_size("rep"))
    return (scores_vocab.astype(jnp.bfloat16), token_loss, mean_loss)


def encoder_kernel(
    sent,
    x_ref,
    gain_ref,
    row_doc_ref,
    key_doc_ref,
    wqkv_ref,
    wout_ref,
    mem_ref,
    wqkv_v,
    wout_v,
    hid,
    work,
    part,
    qkv,
    mix,
    w_sem,
    o_sem,
    x_sem,
    gs,
    gr,
    rs,
    rr,
    zs,
    zr,
    bs,
    br,
    ms,
    mr,
):
    rows, width = hid.shape
    half = sent // 2
    columns = width // PARTS
    tiles = wqkv_v.shape[0]
    per = tiles // 3
    section = lax.axis_index("section")
    count = lax.axis_size("section")
    group = section // 2
    lane = section % 2
    partner = section + 1 - 2 * lane
    ahead = lax.rem(section + 2, count)
    behind = lax.rem(section + count - 2, count)
    own = pl.ds(pl.multiple_of(lane * half, 16), half)
    other = pl.ds(pl.multiple_of((1 - lane) * half, 16), half)

    def cols(c):
        return pl.ds(pl.multiple_of(c * columns, columns), columns)

    def weight_copy(j):
        return pltpu.make_async_copy(
            wqkv_ref.at[j // per, pl.ds((j % per) * WTILE, WTILE)], wqkv_v.at[j], w_sem.at[j]
        )

    def out_copy(c):
        return pltpu.make_async_copy(wout_ref.at[:, cols(c)], wout_v.at[c], o_sem.at[c])

    def remote(src, dst, send, recv, device):
        return pltpu.make_async_remote_copy(
            src_ref=src,
            dst_ref=dst,
            send_sem=send,
            recv_sem=recv,
            device_id={"section": device},
            device_id_type=MESH,
        )

    def gather(c, block):
        return remote(hid.at[block, cols(c)], hid.at[block, cols(c)], gs.at[c], gr.at[c], partner)

    def reduce(c):
        return remote(work.at[other, cols(c)], part.at[:, cols(c)], rs.at[c], rr.at[c], partner)

    def hand(c):
        return remote(hid.at[own, cols(c)], hid.at[own, cols(c)], zs.at[c], zr.at[c], ahead)

    def back(c):
        return remote(mem_ref.at[own, cols(c)], mem_ref.at[own, cols(c)], bs.at[c], br.at[c], behind)

    def spread(c, block):
        return remote(
            mem_ref.at[block, cols(c)], mem_ref.at[block, cols(c)], ms.at[c], mr.at[c], partner
        )

    def each(size, body):
        def step(i, carry):
            body(i)
            return carry

        lax.fori_loop(0, size, step, 0)

    entry = pltpu.make_async_copy(x_ref.at[pl.ds(0, sent)], hid.at[pl.ds(0, sent)], x_sem)

    @pl.when(group == 0)
    def _():
        entry.start()

    for j in range(tiles):
        weight_copy(j).start()
    for c in range(PARTS):
        out_copy(c).start()

    barrier = pltpu.get_barrier_semaphore()
    for device in (partner, ahead, behind):
        pl.semaphore_signal(barrier, inc=1, device_id={"section": device}, device_id_type=MESH)
    pl.semaphore_wait(barrier, 3)

    if sent < rows:
        hid[sent:, :] = jnp.zeros((rows - sent, width), hid.dtype)
    if sent < mem_ref.shape[0]:
        mem_ref[sent:, :] = jnp.zeros((mem_ref.shape[0] - sent, width), mem_ref.dtype)

    @pl.when(group == 0)
    def _():
        entry.wait()

    @pl.when(group > 0)
    def _():
        def arrive(c):
            hand(c).wait_recv()
            gather(c, own).start()

        each(PARTS, arrive)

        def complete(c):
            gather(c, other).wait_recv()
            gather(c, own).wait_send()

        each(PARTS, complete)

    def norm(r):
        block = pl.ds(pl.multiple_of(r * 16, 16), 16)
        values = hid[block, :].astype(jnp.float32)
        scale = lax.rsqrt(jnp.mean(values * values, axis=-1, keepdims=True) + 1e-06)
        work[block, :] = (values * scale * gain_ref[...]).astype(work.dtype)

    each(rows // 16, norm)

    def project(j):
        pltpu.make_async_copy(
            wqkv_ref.at[0, pl.ds(0, WTILE)], wqkv_v.at[j], w_sem.at[j]
        ).wait()
        qkv[j] = lax.dot_general(
            work[...], wqkv_v[j], (((1,), (1,)), ((), ())), preferred_element_type=jnp.float32
        ).astype(qkv.dtype)

    each(tiles, project)
    pairs = WTILE // (2 * HD)

    def attend_pair(p):
        tile = p // pairs
        span = pl.ds(pl.multiple_of((p % pairs) * 2 * HD, 2 * HD), 2 * HD)
        queries = qkv[tile, :, span]
        keys = qkv[per + tile, :, span]
        values = qkv[2 * per + tile, :, span]
        allowed = row_doc_ref[...] == key_doc_ref[...]
        first = lax.broadcasted_iota(jnp.int32, (rows, 2 * HD), 1) < HD
        mixed = []
        for side in range(2):
            keep = first if side == 0 else jnp.logical_not(first)
            chosen = jnp.where(keep, queries.astype(jnp.float32), 0.0).astype(jnp.bfloat16)
            scores = lax.dot_general(
                chosen, keys, (((1,), (1,)), ((), ())), preferred_element_type=jnp.float32
            )
            weights = jnp.where(allowed, jnp.exp(scores), 0.0)
            shares = (weights / jnp.sum(weights, axis=-1, keepdims=True)).astype(jnp.bfloat16)
            mixed.append(jnp.dot(shares, values, preferred_element_type=jnp.float32))
        mix[:, pl.ds(pl.multiple_of(p * 2 * HD, 2 * HD), 2 * HD)] = jnp.where(
            first, mixed[0], mixed[1]
        ).astype(mix.dtype)

    each(per * pairs, attend_pair)

    def output(c):
        out_copy(c).wait()
        work[:, cols(c)] = jnp.dot(
            mix[...], wout_v[c], preferred_element_type=jnp.float32
        ).astype(work.dtype)
        reduce(c).start()

    each(PARTS, output)

    def total(c):
        reduce(c).wait_recv()
        return (
            hid[own, cols(c)].astype(jnp.float32)
            + work[own, cols(c)].astype(jnp.float32)
            + part[:, cols(c)].astype(jnp.float32)
        ).astype(hid.dtype)

    @pl.when(group < GROUPS - 1)
    def _():
        def finish(c):
            hid[own, cols(c)] = total(c)
            hand(c).start()

        each(PARTS, finish)

        def relay(c):
            back(c).wait_recv()

            @pl.when(group > 0)
            def _():
                back(c).start()

            spread(c, own).start()

        each(PARTS, relay)

    @pl.when(group == GROUPS - 1)
    def _():
        def finish(c):
            mem_ref[own, cols(c)] = total(c)
            back(c).start()
            spread(c, own).start()

        each(PARTS, finish)

    def drain(c):
        spread(c, other).wait_recv()
        spread(c, own).wait_send()
        reduce(c).wait_send()

        @pl.when(group < GROUPS - 1)
        def _():
            hand(c).wait_send()

        @pl.when(group > 0)
        def _():
            back(c).wait_send()

    each(PARTS, drain)


def encode(rows, sent, number, x, gain, row_doc, key_doc, wqkv, wout):
    total_rows, width = x.shape
    inner = wout.shape[0]
    tiles = 3 * (inner // WTILE)
    dma = pltpu.SemaphoreType.DMA
    vmem = pl.BlockSpec(memory_space=pltpu.VMEM)
    anywhere = pl.BlockSpec(memory_space=pl.ANY)
    return pl.pallas_call(
        functools.partial(encoder_kernel, sent),
        out_shape=jax.ShapeDtypeStruct((total_rows, width), jnp.bfloat16),
        in_specs=[anywhere, vmem, vmem, vmem, anywhere, anywhere],
        out_specs=vmem,
        scratch_shapes=[
            pltpu.VMEM((tiles, WTILE, width), jnp.bfloat16),
            pltpu.VMEM((PARTS, inner, width // PARTS), jnp.bfloat16),
            pltpu.VMEM((rows, width), jnp.bfloat16),
            pltpu.VMEM((rows, width), jnp.bfloat16),
            pltpu.VMEM((sent // 2, width), jnp.bfloat16),
            pltpu.VMEM((tiles, rows, WTILE), jnp.bfloat16),
            pltpu.VMEM((rows, inner), jnp.bfloat16),
            dma((tiles,)),
            dma((PARTS,)),
            dma,
        ]
        + [dma((PARTS,))] * 10,
        compiler_params=pltpu.CompilerParams(
            collective_id=number, has_side_effects=True, vmem_limit_bytes=67043328
        ),
        name=f"encoder_{sent}",
    )(x, gain, row_doc[:rows, None], key_doc[None, :rows], wqkv, wout)


def stream_kernel(
    sent,
    lengths_ref,
    x_ref,
    enc_gain_ref,
    dec_gain_ref,
    docid_ref,
    target_ref,
    wqkv_ref,
    wout_ref,
    wcross_ref,
    wclose_ref,
    whead_ref,
    logits_ref,
    loss_ref,
    mean_ref,
    wqkv_v,
    wout_v,
    entered,
    hid,
    work,
    part,
    acc,
    squares,
    mix,
    memory,
    cross_acc,
    query_acc,
    terms,
    landed,
    closing,
    scores,
    stats,
    stats_landed,
    loss_landed,
    w_sem,
    o_sem,
    x_sem,
    gs,
    gr,
    rs,
    rr,
    zs,
    zr,
    bs,
    br,
    ms,
    mr,
    k_sem,
    q_sem,
    c_sem,
    h_sem,
    ts,
    tr,
    fs,
    fr,
    ss,
    sr,
    ls,
    lr,
):
    rows, width = hid.shape
    half = sent // 2
    chunks, tiles, tile_columns, columns = wqkv_v.shape
    per = tiles // 3
    doc_total = lengths_ref.shape[0]
    doc_span = x_ref.shape[0] // doc_total
    share_count, share, _ = docid_ref.shape
    every = share_count * share
    blocks = whead_ref.shape[1] // tile_columns
    section = lax.axis_index("section")
    count = lax.axis_size("section")
    rep = lax.axis_index("rep")
    rep_count = lax.axis_size("rep")
    group = section // 2
    lane = section % 2
    partner = section + 1 - 2 * lane
    ahead = lax.rem(section + 2, count)
    behind = lax.rem(section + count - 2, count)
    own = pl.ds(pl.multiple_of(lane * half, 16), half)
    other = pl.ds(pl.multiple_of((1 - lane) * half, 16), half)

    def cols(c):
        return pl.ds(pl.multiple_of(c * columns, columns), columns)

    def weight_copy(c):
        return pltpu.make_async_copy(wqkv_ref.at[:, :, cols(c)], wqkv_v.at[c], w_sem.at[c])

    def out_copy(c):
        return pltpu.make_async_copy(wout_ref.at[:, cols(c)], wout_v.at[c], o_sem.at[c])

    def entry_copy(c):
        return pltpu.make_async_copy(x_ref.at[:, cols(c)], entered.at[:, cols(c)], x_sem.at[c])

    def key_copy(c):
        return pltpu.make_async_copy(
            wcross_ref.at[pl.ds(1, 2), :, cols(c)], wqkv_v.at[c, pl.ds(0, 2)], k_sem.at[c]
        )

    def query_copy(c):
        return pltpu.make_async_copy(wcross_ref.at[0, :, cols(c)], wqkv_v.at[c, 2], q_sem.at[c])

    def close_copy(c):
        return pltpu.make_async_copy(wclose_ref.at[:, cols(c)], wqkv_v.at[c, 3], c_sem.at[c])

    def head_copy(i):
        c = i // blocks
        b = i % blocks
        return pltpu.make_async_copy(
            whead_ref.at[cols(c), pl.ds(pl.multiple_of(b * tile_columns, 128), tile_columns)],
            wqkv_v.at[c, 4 + b],
            h_sem.at[i],
        )

    def remote(src, dst, send, recv, device):
        return pltpu.make_async_remote_copy(
            src_ref=src,
            dst_ref=dst,
            send_sem=send,
            recv_sem=recv,
            device_id={"section": device},
            device_id_type=MESH,
        )

    def gather(c, block):
        return remote(hid.at[block, cols(c)], hid.at[block, cols(c)], gs.at[c], gr.at[c], partner)

    def reduce(c):
        return remote(work.at[other, cols(c)], part.at[:, cols(c)], rs.at[c], rr.at[c], partner)

    def hand(c):
        return remote(hid.at[own, cols(c)], hid.at[own, cols(c)], zs.at[c], zr.at[c], ahead)

    def back(c):
        return remote(memory.at[own, cols(c)], memory.at[own, cols(c)], bs.at[c], br.at[c], behind)

    def spread(c, block):
        return remote(
            memory.at[block, cols(c)], memory.at[block, cols(c)], ms.at[c], mr.at[c], partner
        )

    def peer(k):
        return lax.rem(section + k, count)

    def source_of(k):
        return lax.rem(section + count - k, count)

    def scatter(k, slot):
        return remote(terms.at[peer(k)], landed.at[slot], ts.at[k], tr.at[k], peer(k))

    def collect(k, slot):
        return remote(closing.at[slot], closing.at[slot], fs.at[k], fr.at[k], peer(k))

    def share_stats(k, slot):
        return remote(stats, stats_landed.at[slot], ss.at[k], sr.at[k], peer(k))

    def share_loss(k, slot):
        return pltpu.make_async_remote_copy(
            src_ref=loss_ref,
            dst_ref=loss_landed.at[slot],
            send_sem=ls.at[k],
            recv_sem=lr.at[k],
            device_id={"rep": lax.rem(rep + k, rep_count)},
            device_id_type=MESH,
        )

    def each(size, body):
        def step(i, carry):
            body(i)
            return carry

        lax.fori_loop(0, size, step, 0)

    @pl.when(group == 0)
    def _():
        for c in range(chunks):
            entry_copy(c).start()

    for c in range(chunks):
        weight_copy(c).start()
    for c in range(chunks):
        out_copy(c).start()

    barrier = pltpu.get_barrier_semaphore()
    for k in range(1, count):
        pl.semaphore_signal(barrier, inc=1, device_id={"section": peer(k)}, device_id_type=MESH)
    for k in range(1, rep_count):
        pl.semaphore_signal(
            barrier, inc=1, device_id={"rep": lax.rem(rep + k, rep_count)}, device_id_type=MESH
        )
    pl.semaphore_wait(barrier, count + rep_count - 2)

    if sent < rows:
        hid[sent:, :] = jnp.zeros((rows - sent, width), hid.dtype)
        memory[sent:, :] = jnp.zeros((rows - sent, width), memory.dtype)
    acc[...] = jnp.zeros_like(acc)
    cross_acc[...] = jnp.zeros_like(cross_acc)
    query_acc[...] = jnp.zeros_like(query_acc)
    scores[...] = jnp.zeros_like(scores)
    squares[...] = jnp.zeros_like(squares)

    def placed(shape, dim):
        position = lax.broadcasted_iota(jnp.int32, shape, dim)
        owner = jnp.full(shape, -1, jnp.int32)
        source = jnp.full(shape, -1, jnp.int32)
        start = 0
        for d in range(doc_total):
            end = start + lengths_ref[d]
            inside = (position >= start) & (position < end)
            owner = jnp.where(inside, d, owner)
            source = jnp.where(inside, d * doc_span + position - start, source)
            start = end
        return owner, source

    row_doc, row_source = placed((rows, 1), 0)
    row_doc = jnp.maximum(row_doc, 0)
    key_doc, _ = placed((1, rows), 1)

    def project(c, weight_dim):
        values = hid[:, cols(c)].astype(jnp.float32)
        squares[...] += jnp.sum(values * values, axis=-1, keepdims=True)
        scaled = (values * enc_gain_ref[pl.ds(group, 1), cols(c)]).astype(jnp.bfloat16)

        def some(t):
            for u in range(per):
                j = t * per + u
                acc[j] += lax.dot_general(
                    scaled,
                    wqkv_v[c, j],
                    (((1,), (weight_dim,)), ((), ())),
                    preferred_element_type=jnp.float32,
                )

        each(3, some)

    @pl.when(group == 0)
    def _():
        origin = lax.broadcasted_iota(jnp.int32, (rows, x_ref.shape[0]), 1)
        pick = (row_source == origin).astype(jnp.float32).astype(jnp.bfloat16)

        def first(c):
            entry_copy(c).wait()
            hid[:, cols(c)] = jnp.dot(
                pick, entered[:, cols(c)], preferred_element_type=jnp.float32
            ).astype(hid.dtype)
            weight_copy(c).wait()
            project(c, 1)

        each(chunks, first)

    @pl.when(group > 0)
    def _():
        side = tile_columns // 2

        def turn(c):
            weight_copy(c).wait()

            def block(j):
                whole = wqkv_v[c, j]
                for a in range(2):
                    for b in range(2):
                        piece = whole[a * side : (a + 1) * side, b * side : (b + 1) * side]
                        wqkv_v[c, j, b * side : (b + 1) * side, a * side : (a + 1) * side] = piece.T

            each(tiles, block)

        each(chunks, turn)

        def step(i):
            @pl.when(i < chunks)
            def _():
                hand(i).wait_recv()
                gather(i, own).start()

            @pl.when(i >= AHEAD)
            def _():
                gather(i - AHEAD, other).wait_recv()
                project(i - AHEAD, 0)

        each(chunks + AHEAD, step)

        def complete(c):
            gather(c, own).wait_send()

        each(chunks, complete)

    def fetch(c):
        query_copy(c).start()
        key_copy(c).start()
        close_copy(c).start()

    each(chunks, fetch)

    def fetch_head(i):
        head_copy(i).start()

    each(chunks * blocks, fetch_head)

    def mixed_pair(queries, keys, values, allowed):
        size = queries.shape[0]
        first = lax.broadcasted_iota(jnp.int32, (size, 2 * HD), 1) < HD
        both = jnp.concatenate(
            [jnp.where(first, queries, 0.0), jnp.where(first, 0.0, queries)], 0
        ).astype(jnp.bfloat16)
        raw = lax.dot_general(
            both, keys, (((1,), (1,)), ((), ())), preferred_element_type=jnp.float32
        )
        weights = jnp.where(allowed, jnp.exp(raw), 0.0)
        shares = weights * (1.0 / jnp.sum(weights, axis=-1, keepdims=True))
        mixed = jnp.dot(shares.astype(jnp.bfloat16), values, preferred_element_type=jnp.float32)
        return jnp.where(first, mixed[:size], mixed[size:])

    pairs = tile_columns // (2 * HD)
    scale = lax.rsqrt(squares[...] * (1.0 / width) + 1e-06)
    allowed = row_doc == key_doc
    allowed = jnp.concatenate([allowed, allowed], 0)

    def attend_tile(tile):
        for p in range(pairs):
            span = slice(p * 2 * HD, (p + 1) * 2 * HD)
            mixed = mixed_pair(
                acc[tile, :, span] * scale,
                (acc[per + tile, :, span] * scale).astype(jnp.bfloat16),
                (acc[2 * per + tile, :, span] * scale).astype(jnp.bfloat16),
                allowed,
            )
            place = pl.multiple_of(tile * tile_columns + p * 2 * HD, 2 * HD)
            mix[:, pl.ds(place, 2 * HD)] = mixed.astype(mix.dtype)

    each(per, attend_tile)

    def output(c):
        out_copy(c).wait()
        work[:, cols(c)] = jnp.dot(
            mix[...], wout_v[c], preferred_element_type=jnp.float32
        ).astype(work.dtype)
        reduce(c).start()

    each(chunks, output)

    def total(c):
        reduce(c).wait_recv()
        return (
            hid[own, cols(c)].astype(jnp.float32)
            + work[own, cols(c)].astype(jnp.float32)
            + part[:, cols(c)].astype(jnp.float32)
        ).astype(hid.dtype)

    @pl.when(group < GROUPS - 1)
    def _():
        def finish(c):
            hid[own, cols(c)] = total(c)
            hand(c).start()

        each(chunks, finish)

    @pl.when(group == GROUPS - 1)
    def _():
        def finish(c):
            memory[own, cols(c)] = total(c)
            back(c).start()
            spread(c, own).start()

        each(chunks, finish)

    def docid_rows(c):
        return docid_ref[:, :, cols(c)].astype(jnp.float32).reshape(every, columns)

    def ask(c, sums):
        values = docid_rows(c)
        scaled = (values * dec_gain_ref[0:1, cols(c)]).astype(jnp.bfloat16)
        query_copy(c).wait()
        query_acc[...] += lax.dot_general(
            scaled, wqkv_v[c, 2], (((1,), (1,)), ((), ())), preferred_element_type=jnp.float32
        )
        return sums + jnp.sum(values * values, axis=-1, keepdims=True)

    query_squares = lax.fori_loop(0, chunks, ask, jnp.zeros((every, 1), jnp.float32))
    query_scale = lax.rsqrt(query_squares * (1.0 / width) + 1e-06)
    squares[...] = jnp.zeros_like(squares)

    def recall(c):
        spread(c, other).wait_recv()
        key_copy(c).wait()
        values = memory[:, cols(c)].astype(jnp.float32)
        squares[...] += jnp.sum(values * values, axis=-1, keepdims=True)
        scaled = (values * enc_gain_ref[GROUPS : GROUPS + 1, cols(c)]).astype(jnp.bfloat16)
        for j in range(2):
            cross_acc[j] += lax.dot_general(
                scaled, wqkv_v[c, j], (((1,), (1,)), ((), ())), preferred_element_type=jnp.float32
            )

    def relay(i):
        @pl.when((i < chunks) & (group < GROUPS - 1))
        def _():
            back(i).wait_recv()

            @pl.when(group > 0)
            def _():
                back(i).start()

            spread(i, own).start()

        @pl.when(i >= AHEAD)
        def _():
            recall(i - AHEAD)

    each(chunks + AHEAD, relay)

    memory_scale = lax.rsqrt(squares[...] * (1.0 / width) + 1e-06)
    asking = lax.broadcasted_iota(jnp.int32, (every, 1), 0) // (every // doc_total)
    visible = asking == key_doc
    visible = jnp.concatenate([visible, visible], 0)
    crossed = []
    for p in range(pairs):
        span = slice(p * 2 * HD, (p + 1) * 2 * HD)
        crossed.append(
            mixed_pair(
                query_acc[:, span] * query_scale,
                (cross_acc[0, :, span] * memory_scale).astype(jnp.bfloat16),
                (cross_acc[1, :, span] * memory_scale).astype(jnp.bfloat16),
                visible,
            ).astype(jnp.bfloat16)
        )
    crossed = jnp.concatenate(crossed, 1)

    def close(c):
        close_copy(c).wait()
        product = jnp.dot(crossed, wqkv_v[c, 3], preferred_element_type=jnp.float32)
        terms[:, :, cols(c)] = product.reshape(share_count, share, columns).astype(terms.dtype)

    each(chunks, close)
    for k in range(1, count):
        scatter(k, section).start()
    summed = docid_ref[section].astype(jnp.float32) + terms[section].astype(jnp.float32)
    for k in range(1, count):
        scatter(k, source_of(k)).wait_recv()
        summed = summed + landed[source_of(k)].astype(jnp.float32)
    close_scale = lax.rsqrt(jnp.mean(summed * summed, axis=-1, keepdims=True) + 1e-06)
    closing[section] = (summed * close_scale * dec_gain_ref[1:2, :]).astype(closing.dtype)
    for k in range(1, count):
        collect(k, section).start()

    def arrive_head(i):
        head_copy(i).wait()

    each(chunks * blocks, arrive_head)
    for k in range(1, count):
        collect(k, source_of(k)).wait_recv()

    def head(c):
        final = closing[:, :, cols(c)].astype(jnp.float32).reshape(every, columns)
        final = final.astype(jnp.bfloat16)
        for b in range(blocks):
            scores[b] += jnp.dot(final, wqkv_v[c, 4 + b], preferred_element_type=jnp.float32)

    each(chunks, head)
    summed_exp = jnp.zeros((every, 1), jnp.float32)
    picked = jnp.zeros((every, 1), jnp.float32)
    for b in range(blocks):
        values = scores[b]
        logits_ref[:, b * tile_columns : (b + 1) * tile_columns] = values.astype(logits_ref.dtype)
        entry = lax.broadcasted_iota(jnp.int32, (every, tile_columns), 1)
        entry = entry + (section * blocks + b) * tile_columns
        summed_exp = summed_exp + jnp.sum(jnp.exp(values), axis=-1, keepdims=True)
        picked = picked + jnp.sum(
            jnp.where(entry == target_ref[...], values, 0.0), axis=-1, keepdims=True
        )
    place = lax.broadcasted_iota(jnp.int32, (every, 128), 1)
    packed = jnp.where(place == 0, summed_exp, jnp.where(place == 1, picked, 0.0))
    packed = jnp.concatenate([packed, jnp.zeros((128 - every, 128), jnp.float32)], 0)
    stats[...] = packed.T[:8]
    for k in range(1, count):
        share_stats(k, section).start()
    stats_landed[section] = stats[...]
    for k in range(1, count):
        share_stats(k, source_of(k)).wait_recv()
    gathered = stats_landed[0]
    for k in range(1, count):
        gathered = gathered + stats_landed[k]
    here = lax.broadcasted_iota(jnp.int32, (1, 128), 1) < every
    token = jnp.log(jnp.where(here, gathered[0:1], 1.0)) - jnp.where(here, gathered[1:2], 0.0)
    loss_ref[...] = jnp.broadcast_to(token, loss_ref.shape)
    for k in range(1, rep_count):
        share_loss(k, rep).start()
    loss_landed[rep] = loss_ref[...]
    for k in range(1, rep_count):
        share_loss(k, lax.rem(rep + rep_count - k, rep_count)).wait_recv()
    losses = loss_landed[0]
    for k in range(1, rep_count):
        losses = losses + loss_landed[k]
    mean = jnp.sum(losses[0:1], axis=-1, keepdims=True) / (every * rep_count)
    mean_ref[...] = jnp.broadcast_to(mean, mean_ref.shape)

    def drain(c):
        spread(c, own).wait_send()
        reduce(c).wait_send()

        @pl.when(group < GROUPS - 1)
        def _():
            hand(c).wait_send()

        @pl.when(group > 0)
        def _():
            back(c).wait_send()

    each(chunks, drain)
    for k in range(1, count):
        scatter(k, section).wait_send()
        collect(k, section).wait_send()
        share_stats(k, section).wait_send()
    for k in range(1, rep_count):
        share_loss(k, rep).wait_send()


def stream(sent, number, lengths, x, enc_gain, dec_gain, docid, targets, *weights):
    total_rows, width = x.shape
    wqkv, wout, wcross, wclose, whead = weights
    rows = total_rows // 2
    inner = wout.shape[0]
    tiles = 3 * (inner // WTILE)
    columns = width // CHUNKS
    share_count, share, _ = docid.shape
    every = share_count * share
    vocab = whead.shape[1]
    dma = pltpu.SemaphoreType.DMA
    vmem = pl.BlockSpec(memory_space=pltpu.VMEM)
    smem = pl.BlockSpec(memory_space=pltpu.SMEM)
    anywhere = pl.BlockSpec(memory_space=pl.ANY)
    small = (8, 128)
    bf16 = jnp.bfloat16
    f32 = jnp.float32
    reps = lax.axis_size("rep")
    logits, loss, mean = pl.pallas_call(
        functools.partial(stream_kernel, sent),
        out_shape=(
            jax.ShapeDtypeStruct((every, vocab), bf16),
            jax.ShapeDtypeStruct(small, f32),
            jax.ShapeDtypeStruct(small, f32),
        ),
        in_specs=[smem, anywhere, vmem, vmem, vmem, vmem] + [anywhere] * 5,
        out_specs=(vmem, vmem, vmem),
        scratch_shapes=[
            pltpu.VMEM((CHUNKS, tiles, WTILE, columns), bf16),
            pltpu.VMEM((CHUNKS, inner, columns), bf16),
            pltpu.VMEM((total_rows, width), bf16),
            pltpu.VMEM((rows, width), bf16),
            pltpu.VMEM((rows, width), bf16),
            pltpu.VMEM((sent // 2, width), bf16),
            pltpu.VMEM((tiles, rows, WTILE), f32),
            pltpu.VMEM((rows, 1), f32),
            pltpu.VMEM((rows, inner), bf16),
            pltpu.VMEM((rows, width), bf16),
            pltpu.VMEM((2, rows, WTILE), f32),
            pltpu.VMEM((every, WTILE), f32),
            pltpu.VMEM(docid.shape, bf16),
            pltpu.VMEM(docid.shape, bf16),
            pltpu.VMEM(docid.shape, bf16),
            pltpu.VMEM((vocab // WTILE, every, WTILE), f32),
            pltpu.VMEM(small, f32),
            pltpu.VMEM((share_count,) + small, f32),
            pltpu.VMEM((reps,) + small, f32),
        ]
        + [dma((CHUNKS,))] * 16
        + [dma((CHUNKS * (vocab // WTILE),))]
        + [dma((share_count,))] * 6
        + [dma((reps,))] * 2,
        compiler_params=pltpu.CompilerParams(
            collective_id=number, has_side_effects=True, vmem_limit_bytes=67043328
        ),
        name=f"stream_{sent}",
    )(
        lengths,
        x,
        enc_gain,
        dec_gain,
        docid,
        targets,
        wqkv.reshape(tiles, WTILE, width),
        wout,
        wcross,
        wclose,
        whead,
    )
    return logits, loss[0, :every], mean[0, 0]


def largest_kernel(limits, lengths_ref, out_ref, mine, landed, send, recv):
    me = lax.axis_index("rep")
    count = lax.axis_size("rep")
    barrier = pltpu.get_barrier_semaphore()
    for k in range(1, count):
        pl.semaphore_signal(
            barrier, inc=1, device_id={"rep": lax.rem(me + k, count)}, device_id_type=MESH
        )
    live = lengths_ref[0]
    for d in range(1, lengths_ref.shape[0]):
        live = live + lengths_ref[d]
    mine[...] = jnp.full(mine.shape, live, jnp.int32).astype(jnp.float32)
    pl.semaphore_wait(barrier, count - 1)

    def share(k, slot):
        return pltpu.make_async_remote_copy(
            src_ref=mine,
            dst_ref=landed.at[slot],
            send_sem=send.at[k],
            recv_sem=recv.at[k],
            device_id={"rep": lax.rem(me + k, count)},
            device_id_type=MESH,
        )

    for k in range(1, count):
        share(k, me).start()
    most = mine[...]
    for k in range(1, count):
        slot = lax.rem(me + count - k, count)
        share(k, slot).wait_recv()
        most = jnp.maximum(most, landed[slot])
    choice = jnp.zeros(most.shape, jnp.float32)
    for limit in limits:
        choice = choice + jnp.where(most > limit, 1.0, 0.0)
    out_ref[...] = choice.astype(jnp.int32)
    for k in range(1, count):
        share(k, me).wait_send()


def branch_choice(limits, lengths):
    count = lax.axis_size("rep")
    dma = pltpu.SemaphoreType.DMA
    small = (8, 128)
    return pl.pallas_call(
        functools.partial(largest_kernel, limits),
        out_shape=jax.ShapeDtypeStruct(small, jnp.int32),
        in_specs=[pl.BlockSpec(memory_space=pltpu.SMEM)],
        out_specs=pl.BlockSpec(memory_space=pltpu.VMEM),
        scratch_shapes=[pltpu.VMEM(small, jnp.float32), pltpu.VMEM((count,) + small, jnp.float32)]
        + [dma((count,))] * 2,
        compiler_params=pltpu.CompilerParams(collective_id=10, has_side_effects=True),
        name="largest",
    )(lengths)[0, 0]


def butterfly(value, axis, combine):
    for bit in range(lax.axis_size(axis).bit_length() - 1):
        value = combine(value, from_partner(value, axis, bit))
    return value


def greet(me, count):
    barrier = pltpu.get_barrier_semaphore()
    for k in range(1, count):
        pl.semaphore_signal(
            barrier, inc=1, device_id={"section": lax.rem(me + k, count)}, device_id_type=MESH
        )
    pl.semaphore_wait(barrier, count - 1)


def to_peer(src, dst, send, recv, peer):
    return pltpu.make_async_remote_copy(
        src_ref=src,
        dst_ref=dst,
        send_sem=send,
        recv_sem=recv,
        device_id={"section": peer},
        device_id_type=MESH,
    )


def closing_kernel(terms, residual, gain, out, landed, s1, r1, s2, r2):
    count = terms.shape[0]
    me = lax.axis_index("section")
    greet(me, count)

    def scatter(k, slot):
        peer = lax.rem(me + k, count)
        return to_peer(terms.at[peer], landed.at[slot], s1.at[k], r1.at[k], peer)

    def gather(k, slot):
        return to_peer(out.at[slot], out.at[slot], s2.at[k], r2.at[k], lax.rem(me + k, count))

    for k in range(1, count):
        scatter(k, me).start()
    total = residual[...] + terms[me].astype(jnp.float32)
    for k in range(1, count):
        slot = lax.rem(me + count - k, count)
        scatter(k, slot).wait_recv()
        total = total + landed[slot].astype(jnp.float32)
    scale = lax.rsqrt(jnp.mean(total * total, axis=-1, keepdims=True) + 1e-06)
    out[me] = (total * scale * gain[...]).astype(out.dtype)
    for k in range(1, count):
        gather(k, me).start()
    for k in range(1, count):
        gather(k, lax.rem(me + count - k, count)).wait_recv()
    for k in range(1, count):
        scatter(k, me).wait_send()
        gather(k, me).wait_send()


def closing_rows_of(terms, residual, gain):
    count = terms.shape[0]
    dma = pltpu.SemaphoreType.DMA
    vmem = pl.BlockSpec(memory_space=pltpu.VMEM)
    return pl.pallas_call(
        closing_kernel,
        out_shape=jax.ShapeDtypeStruct(terms.shape, jnp.bfloat16),
        in_specs=[vmem] * 3,
        out_specs=vmem,
        scratch_shapes=[pltpu.VMEM(terms.shape, jnp.bfloat16)] + [dma((count,))] * 4,
        compiler_params=pltpu.CompilerParams(collective_id=8, has_side_effects=True),
        name="closing",
    )(terms, residual, gain)


def sums_kernel(value, out, landed, send, recv):
    count = landed.shape[0]
    me = lax.axis_index("section")
    greet(me, count)

    def share(k, slot):
        return to_peer(value, landed.at[slot], send.at[k], recv.at[k], lax.rem(me + k, count))

    for k in range(1, count):
        share(k, me).start()
    landed[me] = value[...]
    for k in range(1, count):
        share(k, lax.rem(me + count - k, count)).wait_recv()
    total = landed[0]
    for k in range(1, count):
        total = total + landed[k]
    out[...] = total
    for k in range(1, count):
        share(k, me).wait_send()


def section_sum(value, count):
    dma = pltpu.SemaphoreType.DMA
    vmem = pl.BlockSpec(memory_space=pltpu.VMEM)
    return pl.pallas_call(
        sums_kernel,
        out_shape=jax.ShapeDtypeStruct(value.shape, value.dtype),
        in_specs=[vmem],
        out_specs=vmem,
        scratch_shapes=[pltpu.VMEM((count,) + value.shape, value.dtype)] + [dma((count,))] * 2,
        compiler_params=pltpu.CompilerParams(collective_id=9, has_side_effects=True),
        name="section_sum",
    )(value)


def large_shards(
    document_token_embedding,
    doc_lengths,
    docid_embed,
    docid_targets,
    enc_gain,
    dec_gain,
    w_enc_qkv,
    w_enc_out,
    cross_query_key_value_weight,
    w_cross_out,
    docid_head_weight,
):
    section_index = lax.axis_index("section")
    group_index = section_index // 2
    micro_count, row_count, width = document_token_embedding.shape
    doc_count = doc_lengths.shape[1]
    doc_span = row_count // doc_count
    all_rows = micro_count * row_count
    positions = jnp.arange(all_rows)
    row_doc = (positions // doc_span).astype(jnp.int32)
    live = (jnp.arange(doc_span)[None, :] < doc_lengths.reshape(-1)[:, None]).reshape(-1)
    key_doc = jnp.where(live, row_doc, -1).astype(jnp.int32)
    gain = lax.dynamic_slice_in_dim(enc_gain, group_index, 1, 0)
    hidden = encode(
        all_rows,
        all_rows,
        2,
        document_token_embedding.reshape(all_rows, width),
        gain,
        row_doc,
        key_doc,
        w_enc_qkv,
        w_enc_out,
    )
    memory = norm_rows(hidden, enc_gain[GROUPS]).astype(jnp.bfloat16)

    decoder_rows = docid_embed.shape[1]
    every = micro_count * decoder_rows
    docid_span = decoder_rows // doc_count
    decoder_doc = jnp.arange(every) // docid_span
    cross_heads = cross_query_key_value_weight.shape[1] // HD
    flat_docid = docid_embed.reshape(every, width)
    dec_normed = norm_rows(flat_docid, dec_gain[0]).astype(jnp.bfloat16)

    def project(values, weight):
        return (
            jnp.einsum("rd,cd->rc", values, weight, preferred_element_type=jnp.float32)
            .astype(jnp.bfloat16)
            .reshape(-1, cross_heads, HD)
        )

    queries = project(dec_normed, cross_query_key_value_weight[0])
    keys = project(memory, cross_query_key_value_weight[1])
    values = project(memory, cross_query_key_value_weight[2])
    allowed = decoder_doc[:, None] == key_doc[None, :]
    mixture = attend(queries, keys, values, allowed).reshape(every, -1)
    cross_terms = jnp.dot(mixture, w_cross_out, preferred_element_type=jnp.float32)
    section_count = lax.axis_size("section")
    share = every // section_count
    residual = lax.dynamic_slice_in_dim(flat_docid, section_index * share, share, 0)
    closing = closing_rows_of(
        cross_terms.astype(jnp.bfloat16).reshape(section_count, share, width),
        residual.astype(jnp.float32),
        dec_gain[1:2],
    ).reshape(every, width)
    scores_vocab = jnp.dot(closing, docid_head_weight, preferred_element_type=jnp.float32)
    vocab_local = docid_head_weight.shape[1]
    targets = docid_targets.reshape(-1)
    matches = targets[:, None] == section_index * vocab_local + jnp.arange(vocab_local)
    sums = jnp.stack(
        [
            jnp.sum(jnp.exp(scores_vocab), axis=-1),
            jnp.sum(jnp.where(matches, scores_vocab, 0.0), axis=-1),
        ]
    )
    padding = ((0, -sums.shape[0] % 8), (0, -sums.shape[1] % 128))
    sums = section_sum(jnp.pad(sums, padding), section_count)[:2, :every]
    token_loss = jnp.log(sums[0]) - sums[1]
    loss_sum = butterfly(jnp.sum(token_loss)[None], "rep", jnp.add)[0]
    mean_loss = loss_sum / (token_loss.size * lax.axis_size("rep"))
    logits = scores_vocab.astype(jnp.bfloat16).reshape(micro_count, decoder_rows, vocab_local)
    return (logits, token_loss.reshape(docid_targets.shape), mean_loss)


def fast_shards(
    document_token_embedding,
    doc_lengths,
    docid_embed,
    docid_targets,
    enc_gain,
    dec_gain,
    *weights,
):
    micro_count, row_count, width = document_token_embedding.shape
    decoder_rows = docid_embed.shape[1]
    sizes = (row_count * 3 // 4, row_count)
    section_count = lax.axis_size("section")
    lengths = doc_lengths.reshape(-1)
    choice = branch_choice(sizes, lengths)

    def streamed(sent, number):
        def run():
            logits, token_loss, mean_loss = stream(
                sent,
                number,
                lengths,
                document_token_embedding.reshape(micro_count * row_count, width),
                enc_gain,
                dec_gain,
                docid_embed.reshape(section_count, -1, width),
                docid_targets.reshape(-1, 1),
                *weights,
            )
            return (
                logits.reshape(micro_count, decoder_rows, -1),
                token_loss.reshape(docid_targets.shape),
                mean_loss,
            )

        return run

    def large():
        return large_shards(
            document_token_embedding,
            doc_lengths,
            docid_embed,
            docid_targets,
            enc_gain,
            dec_gain,
            *weights,
        )

    branches = [streamed(sent, number) for number, sent in enumerate(sizes)] + [large]
    return lax.switch(choice, branches)


def solution(mesh):
    in_specs = (
        P("rep", None, None),
        P("rep", None),
        P("rep", None, None),
        P("rep", None),
        P(),
        P(),
        P(None, "section", None),
        P("section", None),
        P(None, "section", None),
        P("section", None),
        P(None, "section"),
    )
    out_specs = (P("rep", None, "section"), P("rep", None), P())
    local = shards if mesh.shape["section"] != 2 * GROUPS else fast_shards
    return jax.shard_map(local, mesh=mesh, in_specs=in_specs, out_specs=out_specs, check_vma=False)
```

```python
import functools

import jax
import jax.numpy as jnp
from jax import lax
from jax.experimental import pallas as pl
from jax.experimental.pallas import tpu as pltpu
from jax.sharding import PartitionSpec as P

HD = 64
GROUPS = 4
WTILE = 512
PARTS = 4
CHUNKS = 8
AHEAD = 3
HALVES = 2
TAIL = 4
MESH = pl.DeviceIdType.MESH


def from_partner(block, axis, distance):
    count = lax.axis_size(axis)
    route = []
    for low in range(count):
        high = low | 1 << distance
        if high != low and high < count:
            route += [(low, high), (high, low)]
    return lax.ppermute(block, axis, route)


def from_behind(block, axis, distance):
    devices = range(lax.axis_size(axis))
    route = [(i - distance, i) for i in devices if i - distance in devices]
    return lax.ppermute(block, axis, route)


def passed_along(shard, axis, by):
    size = lax.axis_size(axis)
    return lax.ppermute(shard, axis, [(i, (i + by) % size) for i in range(size)])


def norm_rows(values, gain):
    values = values.astype(jnp.float32)
    scale = lax.rsqrt(jnp.mean(values * values, axis=-1, keepdims=True) + 1e-06)
    return values * scale * gain


def attend(queries, key_rows, values, allowed):
    scores = jnp.einsum("qhe,khe->hqk", queries, key_rows, preferred_element_type=jnp.float32)
    attention_weight_rows = jnp.where(allowed[None], jnp.exp(scores), 0.0)
    probabilities = (
        attention_weight_rows / jnp.sum(attention_weight_rows, axis=-1, keepdims=True)
    ).astype(jnp.bfloat16)
    mixture = jnp.einsum("hqk,khe->qhe", probabilities, values, preferred_element_type=jnp.float32)
    return mixture.astype(jnp.bfloat16)


def live_keys(lengths, key_doc, key_place):
    owners = jnp.arange(lengths.shape[0])
    matches = (key_doc[:, None] == owners[None, :]) & (key_place[:, None] < lengths[None, :])
    return jnp.any(matches, axis=1)


def lane_gather(own_rows, lane_bits, lane_index, concat_dim):
    for bit_number in range(lane_bits):
        partner = from_partner(own_rows, "section", bit_number)
        lower_half = lane_index // (1 << bit_number) % 2 == 0
        own_rows = jnp.where(
            lower_half,
            jnp.concatenate([own_rows, partner], concat_dim),
            jnp.concatenate([partner, own_rows], concat_dim),
        )
    return own_rows


def lane_reduce(totals, lane_bits, lane_index):
    for bit_number in reversed(range(lane_bits)):
        half_rows = totals.shape[0] // 2
        lower_half = lane_index // (1 << bit_number) % 2 == 0
        kept_rows = jnp.where(lower_half, totals[:half_rows], totals[half_rows:])
        outgoing = jnp.where(lower_half, totals[half_rows:], totals[:half_rows])
        totals = kept_rows + from_partner(outgoing, "section", bit_number)
    return totals


def relay_memory(encoder_memory, group_index, lane_count):
    encoder_memory = jnp.where(group_index == 0, encoder_memory, jnp.zeros_like(encoder_memory))
    for stride in (1, 2):
        encoder_memory = encoder_memory + from_behind(
            encoder_memory, "section", stride * lane_count
        )
    return encoder_memory


def shards(
    document_token_embedding,
    doc_lengths,
    docid_embed,
    docid_targets,
    enc_gain,
    dec_gain,
    w_enc_qkv,
    w_enc_out,
    cross_query_key_value_weight,
    w_cross_out,
    docid_head_weight,
):
    lane_count = lax.axis_size("section") // GROUPS
    lane_bits = lane_count.bit_length() - 1
    section_index = lax.axis_index("section")
    group_index = section_index // lane_count
    lane_index = section_index % lane_count
    micro_count, row_count, model_width = document_token_embedding.shape
    doc_count = doc_lengths.shape[1]
    doc_span = row_count // doc_count
    block_rows = row_count // lane_count
    local_heads = w_enc_qkv.shape[1] // HD
    positions = jnp.arange(row_count)
    key_doc = positions // doc_span
    key_place = positions % doc_span
    same_doc = key_doc[:, None] == key_doc[None, :]

    def partial_update(normed, lengths):
        allowed = same_doc & live_keys(lengths, key_doc, key_place)[None, :]
        projected = jnp.einsum(
            "rd,mcd->mrc", normed, w_enc_qkv, preferred_element_type=jnp.float32
        ).astype(jnp.bfloat16)
        projected = projected.reshape(3, row_count, local_heads, HD)
        mixture = attend(projected[0], projected[1], projected[2], allowed).reshape(row_count, -1)
        return jnp.dot(mixture, w_enc_out, preferred_element_type=jnp.float32)

    def section_step(step_index, loop_state):
        handed, encoder_memory = loop_state
        micro_index = step_index - group_index
        slot_index = jnp.clip(micro_index, 0, micro_count - 1)
        lengths = lax.dynamic_index_in_dim(doc_lengths, slot_index, 0, keepdims=False)
        layer_gain = lax.dynamic_index_in_dim(enc_gain, group_index, 0, keepdims=False)
        incoming = lax.dynamic_index_in_dim(
            document_token_embedding, jnp.minimum(step_index, micro_count - 1), 0, keepdims=False
        )
        incoming = lax.dynamic_slice_in_dim(incoming, lane_index * block_rows, block_rows, 0)
        current = jnp.where(group_index == 0, incoming, handed)
        normed = lane_gather(
            norm_rows(current, layer_gain).astype(jnp.bfloat16), lane_bits, lane_index, 0
        )
        summed = lane_reduce(partial_update(normed, lengths), lane_bits, lane_index)
        result = (current.astype(jnp.float32) + summed).astype(jnp.bfloat16)
        handed = passed_along(result, "section", lane_count)
        finished_index = step_index - (GROUPS - 1)
        finished_slot = jnp.clip(finished_index, 0, micro_count - 1)
        keeping = (group_index == 0) & (finished_index >= 0) & (finished_index < micro_count)
        stored = lax.dynamic_update_index_in_dim(encoder_memory, handed, finished_slot, 0)
        encoder_memory = jnp.where(keeping, stored, encoder_memory)
        return (handed, encoder_memory)

    handed = jnp.zeros((block_rows, model_width), jnp.bfloat16)
    encoder_memory = jnp.zeros((micro_count, block_rows, model_width), jnp.bfloat16)
    handed, encoder_memory = lax.fori_loop(
        0, micro_count + GROUPS - 1, section_step, (handed, encoder_memory)
    )
    encoder_memory = norm_rows(encoder_memory, enc_gain[GROUPS]).astype(jnp.bfloat16)
    encoder_memory = relay_memory(encoder_memory, group_index, lane_count)
    encoder_memory = lane_gather(encoder_memory, lane_bits, lane_index, 1)
    decoder_rows = docid_embed.shape[1]
    docid_span = decoder_rows // doc_count
    decoder_doc = jnp.arange(decoder_rows) // docid_span
    cross_heads = cross_query_key_value_weight.shape[1] // HD
    dec_normed = norm_rows(docid_embed, dec_gain[0]).astype(jnp.bfloat16)
    queries = jnp.einsum(
        "brd,cd->brc",
        dec_normed,
        cross_query_key_value_weight[0],
        preferred_element_type=jnp.float32,
    ).astype(jnp.bfloat16)
    memory_heads = jnp.einsum(
        "pye,qve->qpyv",
        encoder_memory,
        cross_query_key_value_weight[1:],
        preferred_element_type=jnp.float32,
    ).astype(jnp.bfloat16)

    def cross_one(sample_queries, sample_keys, sample_values, lengths):
        allowed = (decoder_doc[:, None] == key_doc[None, :]) & live_keys(
            lengths, key_doc, key_place
        )[None, :]
        return attend(sample_queries, sample_keys, sample_values, allowed)

    mixture = jax.vmap(cross_one)(
        queries.reshape(micro_count, decoder_rows, cross_heads, HD),
        memory_heads[0].reshape(micro_count, row_count, cross_heads, HD),
        memory_heads[1].reshape(micro_count, row_count, cross_heads, HD),
        doc_lengths,
    )
    cross_terms = jnp.einsum(
        "brc,cd->brd",
        mixture.reshape(micro_count, decoder_rows, -1),
        w_cross_out,
        preferred_element_type=jnp.float32,
    )
    cross_sum = lax.psum(cross_terms, "section")
    closing_rows = norm_rows(docid_embed.astype(jnp.float32) + cross_sum, dec_gain[1]).astype(
        jnp.bfloat16
    )
    scores_vocab = jnp.einsum(
        "brd,dv->brv", closing_rows, docid_head_weight, preferred_element_type=jnp.float32
    )
    vocab_local = docid_head_weight.shape[1]
    vocab_start = section_index * vocab_local
    matches = docid_targets[..., None] == vocab_start + jnp.arange(vocab_local)
    exponent_total, picked = lax.psum(
        (
            jnp.sum(jnp.exp(scores_vocab), axis=-1),
            jnp.sum(jnp.where(matches, scores_vocab, 0.0), axis=-1),
        ),
        "section",
    )
    token_loss = jnp.log(exponent_total) - picked
    mean_loss = lax.psum(jnp.sum(token_loss), "rep") / (token_loss.size * lax.axis_size("rep"))
    return (scores_vocab.astype(jnp.bfloat16), token_loss, mean_loss)


def encoder_kernel(
    sent,
    x_ref,
    gain_ref,
    row_doc_ref,
    key_doc_ref,
    wqkv_ref,
    wout_ref,
    mem_ref,
    wqkv_v,
    wout_v,
    hid,
    work,
    part,
    qkv,
    mix,
    w_sem,
    o_sem,
    x_sem,
    gs,
    gr,
    rs,
    rr,
    zs,
    zr,
    bs,
    br,
    ms,
    mr,
):
    rows, width = hid.shape
    half = sent // 2
    columns = width // PARTS
    tiles = wqkv_v.shape[0]
    per = tiles // 3
    section = lax.axis_index("section")
    count = lax.axis_size("section")
    group = section // 2
    lane = section % 2
    partner = section + 1 - 2 * lane
    ahead = lax.rem(section + 2, count)
    behind = lax.rem(section + count - 2, count)
    own = pl.ds(pl.multiple_of(lane * half, 16), half)
    other = pl.ds(pl.multiple_of((1 - lane) * half, 16), half)

    def cols(c):
        return pl.ds(pl.multiple_of(c * columns, columns), columns)

    def weight_copy(j):
        return pltpu.make_async_copy(
            wqkv_ref.at[j // per, pl.ds((j % per) * WTILE, WTILE)], wqkv_v.at[j], w_sem.at[j]
        )

    def out_copy(c):
        return pltpu.make_async_copy(wout_ref.at[:, cols(c)], wout_v.at[c], o_sem.at[c])

    def remote(src, dst, send, recv, device):
        return pltpu.make_async_remote_copy(
            src_ref=src,
            dst_ref=dst,
            send_sem=send,
            recv_sem=recv,
            device_id={"section": device},
            device_id_type=MESH,
        )

    def gather(c, block):
        return remote(hid.at[block, cols(c)], hid.at[block, cols(c)], gs.at[c], gr.at[c], partner)

    def reduce(c):
        return remote(work.at[other, cols(c)], part.at[:, cols(c)], rs.at[c], rr.at[c], partner)

    def hand(c):
        return remote(hid.at[own, cols(c)], hid.at[own, cols(c)], zs.at[c], zr.at[c], ahead)

    def back(c):
        return remote(mem_ref.at[own, cols(c)], mem_ref.at[own, cols(c)], bs.at[c], br.at[c], behind)

    def spread(c, block):
        return remote(
            mem_ref.at[block, cols(c)], mem_ref.at[block, cols(c)], ms.at[c], mr.at[c], partner
        )

    def each(size, body):
        def step(i, carry):
            body(i)
            return carry

        lax.fori_loop(0, size, step, 0)

    entry = pltpu.make_async_copy(x_ref.at[pl.ds(0, sent)], hid.at[pl.ds(0, sent)], x_sem)

    @pl.when(group == 0)
    def _():
        entry.start()

    for j in range(tiles):
        weight_copy(j).start()
    for c in range(PARTS):
        out_copy(c).start()

    barrier = pltpu.get_barrier_semaphore()
    for device in (partner, ahead, behind):
        pl.semaphore_signal(barrier, inc=1, device_id={"section": device}, device_id_type=MESH)
    pl.semaphore_wait(barrier, 3)

    if sent < rows:
        hid[sent:, :] = jnp.zeros((rows - sent, width), hid.dtype)
    if sent < mem_ref.shape[0]:
        mem_ref[sent:, :] = jnp.zeros((mem_ref.shape[0] - sent, width), mem_ref.dtype)

    @pl.when(group == 0)
    def _():
        entry.wait()

    @pl.when(group > 0)
    def _():
        def arrive(c):
            hand(c).wait_recv()
            gather(c, own).start()

        each(PARTS, arrive)

        def complete(c):
            gather(c, other).wait_recv()
            gather(c, own).wait_send()

        each(PARTS, complete)

    def norm(r):
        block = pl.ds(pl.multiple_of(r * 16, 16), 16)
        values = hid[block, :].astype(jnp.float32)
        scale = lax.rsqrt(jnp.mean(values * values, axis=-1, keepdims=True) + 1e-06)
        work[block, :] = (values * scale * gain_ref[...]).astype(work.dtype)

    each(rows // 16, norm)

    def project(j):
        pltpu.make_async_copy(
            wqkv_ref.at[0, pl.ds(0, WTILE)], wqkv_v.at[j], w_sem.at[j]
        ).wait()
        qkv[j] = lax.dot_general(
            work[...], wqkv_v[j], (((1,), (1,)), ((), ())), preferred_element_type=jnp.float32
        ).astype(qkv.dtype)

    each(tiles, project)
    pairs = WTILE // (2 * HD)

    def attend_pair(p):
        tile = p // pairs
        span = pl.ds(pl.multiple_of((p % pairs) * 2 * HD, 2 * HD), 2 * HD)
        queries = qkv[tile, :, span]
        keys = qkv[per + tile, :, span]
        values = qkv[2 * per + tile, :, span]
        allowed = row_doc_ref[...] == key_doc_ref[...]
        first = lax.broadcasted_iota(jnp.int32, (rows, 2 * HD), 1) < HD
        mixed = []
        for side in range(2):
            keep = first if side == 0 else jnp.logical_not(first)
            chosen = jnp.where(keep, queries.astype(jnp.float32), 0.0).astype(jnp.bfloat16)
            scores = lax.dot_general(
                chosen, keys, (((1,), (1,)), ((), ())), preferred_element_type=jnp.float32
            )
            weights = jnp.where(allowed, jnp.exp(scores), 0.0)
            shares = (weights / jnp.sum(weights, axis=-1, keepdims=True)).astype(jnp.bfloat16)
            mixed.append(jnp.dot(shares, values, preferred_element_type=jnp.float32))
        mix[:, pl.ds(pl.multiple_of(p * 2 * HD, 2 * HD), 2 * HD)] = jnp.where(
            first, mixed[0], mixed[1]
        ).astype(mix.dtype)

    each(per * pairs, attend_pair)

    def output(c):
        out_copy(c).wait()
        work[:, cols(c)] = jnp.dot(
            mix[...], wout_v[c], preferred_element_type=jnp.float32
        ).astype(work.dtype)
        reduce(c).start()

    each(PARTS, output)

    def total(c):
        reduce(c).wait_recv()
        return (
            hid[own, cols(c)].astype(jnp.float32)
            + work[own, cols(c)].astype(jnp.float32)
            + part[:, cols(c)].astype(jnp.float32)
        ).astype(hid.dtype)

    @pl.when(group < GROUPS - 1)
    def _():
        def finish(c):
            hid[own, cols(c)] = total(c)
            hand(c).start()

        each(PARTS, finish)

        def relay(c):
            back(c).wait_recv()

            @pl.when(group > 0)
            def _():
                back(c).start()

            spread(c, own).start()

        each(PARTS, relay)

    @pl.when(group == GROUPS - 1)
    def _():
        def finish(c):
            mem_ref[own, cols(c)] = total(c)
            back(c).start()
            spread(c, own).start()

        each(PARTS, finish)

    def drain(c):
        spread(c, other).wait_recv()
        spread(c, own).wait_send()
        reduce(c).wait_send()

        @pl.when(group < GROUPS - 1)
        def _():
            hand(c).wait_send()

        @pl.when(group > 0)
        def _():
            back(c).wait_send()

    each(PARTS, drain)


def encode(rows, sent, number, x, gain, row_doc, key_doc, wqkv, wout):
    total_rows, width = x.shape
    inner = wout.shape[0]
    tiles = 3 * (inner // WTILE)
    dma = pltpu.SemaphoreType.DMA
    vmem = pl.BlockSpec(memory_space=pltpu.VMEM)
    anywhere = pl.BlockSpec(memory_space=pl.ANY)
    return pl.pallas_call(
        functools.partial(encoder_kernel, sent),
        out_shape=jax.ShapeDtypeStruct((total_rows, width), jnp.bfloat16),
        in_specs=[anywhere, vmem, vmem, vmem, anywhere, anywhere],
        out_specs=vmem,
        scratch_shapes=[
            pltpu.VMEM((tiles, WTILE, width), jnp.bfloat16),
            pltpu.VMEM((PARTS, inner, width // PARTS), jnp.bfloat16),
            pltpu.VMEM((rows, width), jnp.bfloat16),
            pltpu.VMEM((rows, width), jnp.bfloat16),
            pltpu.VMEM((sent // 2, width), jnp.bfloat16),
            pltpu.VMEM((tiles, rows, WTILE), jnp.bfloat16),
            pltpu.VMEM((rows, inner), jnp.bfloat16),
            dma((tiles,)),
            dma((PARTS,)),
            dma,
        ]
        + [dma((PARTS,))] * 10,
        compiler_params=pltpu.CompilerParams(
            collective_id=number, has_side_effects=True, vmem_limit_bytes=67043328
        ),
        name=f"encoder_{sent}",
    )(x, gain, row_doc[:rows, None], key_doc[None, :rows], wqkv, wout)


def stream_kernel(
    sent,
    lengths_ref,
    x_ref,
    enc_gain_ref,
    dec_gain_ref,
    docid_ref,
    target_ref,
    wqkv_ref,
    wout_ref,
    wcross_ref,
    wclose_ref,
    whead_ref,
    logits_ref,
    loss_ref,
    mean_ref,
    wqkv_v,
    wout_v,
    entered,
    hid,
    work,
    part,
    acc,
    squares,
    mix,
    memory,
    cross_acc,
    query_acc,
    terms,
    landed,
    partial,
    crossed_over,
    summed,
    closing,
    scores,
    stats,
    stats_landed,
    loss_landed,
    w_sem,
    o_sem,
    x_sem,
    gs,
    gr,
    rs,
    rr,
    zs,
    zr,
    bs,
    br,
    ms,
    mr,
    k_sem,
    q_sem,
    c_sem,
    h_sem,
    ys,
    yr,
    ts,
    tr,
    us,
    ur,
    fs,
    fr,
    ss,
    sr,
    ls,
    lr,
):
    rows, width = hid.shape
    half = sent // 2
    chunks, tiles, tile_columns, columns = wqkv_v.shape
    per = tiles // 3
    micro_count, doc_count = lengths_ref.shape
    doc_total = micro_count * doc_count
    doc_span = x_ref.shape[0] // doc_total
    share_count, share, _ = docid_ref.shape
    every = share_count * share
    blocks = whead_ref.shape[1] // tile_columns
    section = lax.axis_index("section")
    count = lax.axis_size("section")
    rep = lax.axis_index("rep")
    rep_count = lax.axis_size("rep")
    group = section // 2
    lane = section % 2
    partner = section + 1 - 2 * lane
    ahead = lax.rem(section + 2, count)
    behind = lax.rem(section + count - 2, count)
    own = pl.ds(pl.multiple_of(lane * half, 16), half)
    other = pl.ds(pl.multiple_of((1 - lane) * half, 16), half)

    def cols(c):
        return pl.ds(pl.multiple_of(c * columns, columns), columns)

    def weight_copy(c):
        return pltpu.make_async_copy(wqkv_ref.at[:, :, cols(c)], wqkv_v.at[c], w_sem.at[c])

    def out_copy(c):
        return pltpu.make_async_copy(wout_ref.at[:, cols(c)], wout_v.at[c], o_sem.at[c])

    def entry_copy(c):
        return pltpu.make_async_copy(x_ref.at[:, cols(c)], entered.at[:, cols(c)], x_sem.at[c])

    def key_copy(c):
        return pltpu.make_async_copy(
            wcross_ref.at[pl.ds(1, 2), :, cols(c)], wqkv_v.at[c, pl.ds(0, 2)], k_sem.at[c]
        )

    def query_copy(c):
        return pltpu.make_async_copy(wcross_ref.at[0, :, cols(c)], wqkv_v.at[c, 2], q_sem.at[c])

    def close_copy(c):
        return pltpu.make_async_copy(wclose_ref.at[:, cols(c)], wqkv_v.at[c, 3], c_sem.at[c])

    def head_copy(i):
        c = i // blocks
        b = i % blocks
        return pltpu.make_async_copy(
            whead_ref.at[cols(c), pl.ds(pl.multiple_of(b * tile_columns, 128), tile_columns)],
            wqkv_v.at[c, 4 + b],
            h_sem.at[i],
        )

    def remote(src, dst, send, recv, device):
        return pltpu.make_async_remote_copy(
            src_ref=src,
            dst_ref=dst,
            send_sem=send,
            recv_sem=recv,
            device_id={"section": device},
            device_id_type=MESH,
        )

    pieces = chunks * HALVES
    piece = columns // HALVES

    def span_of(i):
        return pl.ds(pl.multiple_of(i * piece, piece), piece)

    def gather(i, block):
        place = hid.at[block, span_of(i)]
        return remote(place, place, gs.at[i], gr.at[i], partner)

    def reduce(i):
        place = span_of(i)
        return remote(work.at[other, place], part.at[:, place], rs.at[i], rr.at[i], partner)

    def hand(i):
        place = hid.at[own, span_of(i)]
        return remote(place, place, zs.at[i], zr.at[i], ahead)

    def back(i):
        place = memory.at[own, span_of(i)]
        return remote(place, place, bs.at[i], br.at[i], behind)

    def spread(i, block):
        place = memory.at[block, span_of(i)]
        return remote(place, place, ms.at[i], mr.at[i], partner)

    def peer(k):
        return lax.rem(section + k, count)

    def source_of(k):
        return lax.rem(section + count - k, count)

    stretch = width // TAIL
    lanes = count // GROUPS
    own_slot = lane * GROUPS + group

    def tail_cols(t):
        return pl.ds(pl.multiple_of(t * stretch, stretch), stretch)

    def group_after(k):
        return lax.rem(group + k, GROUPS)

    def group_before(k):
        return lax.rem(group + GROUPS - k, GROUPS)

    def swap(t):
        theirs = pl.ds((1 - lane) * GROUPS, GROUPS)
        place = tail_cols(t)
        return remote(
            terms.at[theirs, :, place], landed.at[:, :, place], ys.at[t], yr.at[t], partner
        )

    def scatter(t, k):
        place = tail_cols(t)
        i = k * TAIL + t
        return remote(
            partial.at[group_after(k), :, place],
            crossed_over.at[group, :, place],
            ts.at[i],
            tr.at[i],
            group_after(k) * lanes + lane,
        )

    def scattered(t, k):
        place = tail_cols(t)
        i = k * TAIL + t
        return remote(
            partial.at[group, :, place],
            crossed_over.at[group_before(k), :, place],
            ts.at[i],
            tr.at[i],
            group_after(k) * lanes + lane,
        )

    def collect(t, k, slot):
        place = closing.at[slot, :, tail_cols(t)]
        i = k * TAIL + t
        return remote(place, place, us.at[i], ur.at[i], group_after(k) * lanes + lane)

    def across(t, member, side):
        place = closing.at[side * GROUPS + member, :, tail_cols(t)]
        i = member * TAIL + t
        return remote(place, place, fs.at[i], fr.at[i], partner)

    def share_stats(k, slot):
        return remote(stats, stats_landed.at[slot], ss.at[k], sr.at[k], peer(k))

    def share_loss(k, slot):
        return pltpu.make_async_remote_copy(
            src_ref=loss_ref,
            dst_ref=loss_landed.at[slot],
            send_sem=ls.at[k],
            recv_sem=lr.at[k],
            device_id={"rep": lax.rem(rep + k, rep_count)},
            device_id_type=MESH,
        )

    def each(size, body):
        def step(i, carry):
            body(i)
            return carry

        lax.fori_loop(0, size, step, 0)

    @pl.when(group == 0)
    def _():
        for c in range(chunks):
            entry_copy(c).start()

    for c in range(chunks):
        weight_copy(c).start()
    for c in range(chunks):
        out_copy(c).start()

    barrier = pltpu.get_barrier_semaphore()
    for k in range(1, count):
        pl.semaphore_signal(barrier, inc=1, device_id={"section": peer(k)}, device_id_type=MESH)
    for k in range(1, rep_count):
        pl.semaphore_signal(
            barrier, inc=1, device_id={"rep": lax.rem(rep + k, rep_count)}, device_id_type=MESH
        )
    pl.semaphore_wait(barrier, count + rep_count - 2)

    if sent < rows:
        hid[sent:, :] = jnp.zeros((rows - sent, width), hid.dtype)
        memory[sent:, :] = jnp.zeros((rows - sent, width), memory.dtype)
    acc[...] = jnp.zeros_like(acc)
    cross_acc[...] = jnp.zeros_like(cross_acc)
    query_acc[...] = jnp.zeros_like(query_acc)
    scores[...] = jnp.zeros_like(scores)
    squares[...] = jnp.zeros_like(squares)

    def placed(shape, dim):
        position = lax.broadcasted_iota(jnp.int32, shape, dim)
        owner = jnp.full(shape, -1, jnp.int32)
        source = jnp.full(shape, -1, jnp.int32)
        start = 0
        for d in range(doc_total):
            end = start + lengths_ref[d // doc_count, d % doc_count]
            inside = (position >= start) & (position < end)
            owner = jnp.where(inside, d, owner)
            source = jnp.where(inside, d * doc_span + position - start, source)
            start = end
        return owner, source

    row_doc, row_source = placed((rows, 1), 0)
    row_doc = jnp.maximum(row_doc, 0)
    key_doc, _ = placed((1, rows), 1)

    asked = target_ref.shape[1]
    wanted = jnp.concatenate(
        [jnp.broadcast_to(target_ref[m : m + 1, :], (asked, asked)) for m in range(micro_count)], 0
    )
    diagonal = lax.broadcasted_iota(jnp.int32, (every, asked), 0) % asked
    diagonal = diagonal == lax.broadcasted_iota(jnp.int32, (every, asked), 1)
    wanted = jnp.sum(
        jnp.where(diagonal, wanted.astype(jnp.float32), 0.0), axis=-1, keepdims=True
    )

    def project(c, weight_dim):
        values = hid[:, cols(c)].astype(jnp.float32)
        squares[...] += jnp.sum(values * values, axis=-1, keepdims=True)
        scaled = (values * enc_gain_ref[pl.ds(group, 1), cols(c)]).astype(jnp.bfloat16)

        def some(t):
            for u in range(per):
                j = t * per + u
                acc[j] += lax.dot_general(
                    scaled,
                    wqkv_v[c, j],
                    (((1,), (weight_dim,)), ((), ())),
                    preferred_element_type=jnp.float32,
                )

        each(3, some)

    @pl.when(group == 0)
    def _():
        origin = lax.broadcasted_iota(jnp.int32, (rows, x_ref.shape[0]), 1)
        pick = (row_source == origin).astype(jnp.float32).astype(jnp.bfloat16)

        def first(c):
            entry_copy(c).wait()
            hid[:, cols(c)] = jnp.dot(
                pick, entered[:, cols(c)], preferred_element_type=jnp.float32
            ).astype(hid.dtype)
            weight_copy(c).wait()
            project(c, 1)

        each(chunks, first)

    @pl.when(group > 0)
    def _():
        side = tile_columns // 2

        def turn(c):
            weight_copy(c).wait()

            def block(j):
                whole = wqkv_v[c, j]
                for a in range(2):
                    for b in range(2):
                        quarter = whole[a * side : (a + 1) * side, b * side : (b + 1) * side]
                        wqkv_v[c, j, b * side : (b + 1) * side, a * side : (a + 1) * side] = (
                            quarter.T
                        )

            each(tiles, block)

        each(chunks, turn)

        def step(i):
            @pl.when(i < chunks)
            def _():
                for u in range(HALVES):
                    hand(i * HALVES + u).wait_recv()
                    gather(i * HALVES + u, own).start()

            @pl.when(i >= AHEAD)
            def _():
                for u in range(HALVES):
                    gather((i - AHEAD) * HALVES + u, other).wait_recv()
                project(i - AHEAD, 0)

        each(chunks + AHEAD, step)

        def complete(i):
            gather(i, own).wait_send()

        each(pieces, complete)

    def fetch(c):
        query_copy(c).start()
        key_copy(c).start()
        close_copy(c).start()

    each(chunks, fetch)

    def fetch_head(i):
        head_copy(i).start()

    each(chunks * blocks, fetch_head)

    def mixed_pair(queries, keys, values, allowed):
        size = queries.shape[0]
        first = lax.broadcasted_iota(jnp.int32, (size, 2 * HD), 1) < HD
        both = jnp.concatenate(
            [jnp.where(first, queries, 0.0), jnp.where(first, 0.0, queries)], 0
        ).astype(jnp.bfloat16)
        raw = lax.dot_general(
            both, keys, (((1,), (1,)), ((), ())), preferred_element_type=jnp.float32
        )
        weights = jnp.where(allowed, jnp.exp(raw), 0.0)
        shares = weights * (1.0 / jnp.sum(weights, axis=-1, keepdims=True))
        mixed = jnp.dot(shares.astype(jnp.bfloat16), values, preferred_element_type=jnp.float32)
        return jnp.where(first, mixed[:size], mixed[size:])

    pairs = tile_columns // (2 * HD)
    scale = lax.rsqrt(squares[...] * (1.0 / width) + 1e-06)
    allowed = row_doc == key_doc
    allowed = jnp.concatenate([allowed, allowed], 0)

    def attend_tile(tile):
        for p in range(pairs):
            span = slice(p * 2 * HD, (p + 1) * 2 * HD)
            mixed = mixed_pair(
                acc[tile, :, span] * scale,
                (acc[per + tile, :, span] * scale).astype(jnp.bfloat16),
                (acc[2 * per + tile, :, span] * scale).astype(jnp.bfloat16),
                allowed,
            )
            place = pl.multiple_of(tile * tile_columns + p * 2 * HD, 2 * HD)
            mix[:, pl.ds(place, 2 * HD)] = mixed.astype(mix.dtype)

    each(per, attend_tile)

    def output(c):
        out_copy(c).wait()
        work[:, cols(c)] = jnp.dot(
            mix[...], wout_v[c], preferred_element_type=jnp.float32
        ).astype(work.dtype)
        for u in range(HALVES):
            reduce(c * HALVES + u).start()

    each(chunks, output)

    def total(i):
        reduce(i).wait_recv()
        return (
            hid[own, span_of(i)].astype(jnp.float32)
            + work[own, span_of(i)].astype(jnp.float32)
            + part[:, span_of(i)].astype(jnp.float32)
        ).astype(hid.dtype)

    @pl.when(group < GROUPS - 1)
    def _():
        def finish(i):
            hid[own, span_of(i)] = total(i)
            hand(i).start()

        each(pieces, finish)

    @pl.when(group == GROUPS - 1)
    def _():
        def finish(i):
            memory[own, span_of(i)] = total(i)
            back(i).start()
            spread(i, own).start()

        each(pieces, finish)

    def docid_rows(c):
        return docid_ref[:, :, cols(c)].astype(jnp.float32).reshape(every, columns)

    def ask(c, sums):
        values = docid_rows(c)
        scaled = (values * dec_gain_ref[0:1, cols(c)]).astype(jnp.bfloat16)
        query_copy(c).wait()
        query_acc[...] += lax.dot_general(
            scaled, wqkv_v[c, 2], (((1,), (1,)), ((), ())), preferred_element_type=jnp.float32
        )
        return sums + jnp.sum(values * values, axis=-1, keepdims=True)

    query_squares = lax.fori_loop(0, chunks, ask, jnp.zeros((every, 1), jnp.float32))
    query_scale = lax.rsqrt(query_squares * (1.0 / width) + 1e-06)
    squares[...] = jnp.zeros_like(squares)

    def recall(c):
        for u in range(HALVES):
            spread(c * HALVES + u, other).wait_recv()
        key_copy(c).wait()
        values = memory[:, cols(c)].astype(jnp.float32)
        squares[...] += jnp.sum(values * values, axis=-1, keepdims=True)
        scaled = (values * enc_gain_ref[GROUPS : GROUPS + 1, cols(c)]).astype(jnp.bfloat16)
        for j in range(2):
            cross_acc[j] += lax.dot_general(
                scaled, wqkv_v[c, j], (((1,), (1,)), ((), ())), preferred_element_type=jnp.float32
            )

    def relay(i):
        @pl.when((i < chunks) & (group < GROUPS - 1))
        def _():
            for u in range(HALVES):
                back(i * HALVES + u).wait_recv()

                @pl.when(group > 0)
                def _():
                    back(i * HALVES + u).start()

                spread(i * HALVES + u, own).start()

        @pl.when(i >= AHEAD)
        def _():
            recall(i - AHEAD)

    each(chunks + AHEAD, relay)

    memory_scale = lax.rsqrt(squares[...] * (1.0 / width) + 1e-06)
    asking = lax.broadcasted_iota(jnp.int32, (every, 1), 0) // (every // doc_total)
    visible = asking == key_doc
    visible = jnp.concatenate([visible, visible], 0)
    crossed = []
    for p in range(pairs):
        span = slice(p * 2 * HD, (p + 1) * 2 * HD)
        crossed.append(
            mixed_pair(
                query_acc[:, span] * query_scale,
                (cross_acc[0, :, span] * memory_scale).astype(jnp.bfloat16),
                (cross_acc[1, :, span] * memory_scale).astype(jnp.bfloat16),
                visible,
            ).astype(jnp.bfloat16)
        )
    crossed = jnp.concatenate(crossed, 1)

    ratio = chunks // TAIL

    def close(t):
        for u in range(ratio):
            c = t * ratio + u
            close_copy(c).wait()
            product = jnp.dot(crossed, wqkv_v[c, 3], preferred_element_type=jnp.float32)
            terms[:, :, cols(c)] = product.reshape(share_count, share, columns).astype(terms.dtype)
        swap(t).start()

    each(TAIL, close)
    mine = pl.ds(lane * GROUPS, GROUPS)

    def halfway(t):
        swap(t).wait_recv()
        both = terms[mine, :, tail_cols(t)].astype(jnp.float32)
        both = both + landed[:, :, tail_cols(t)].astype(jnp.float32)
        partial[:, :, tail_cols(t)] = both.astype(partial.dtype)
        for m in range(1, GROUPS):
            scatter(t, m).start()

    each(TAIL, halfway)

    def finished(t, squares_so_far):
        place = tail_cols(t)
        value = docid_ref[own_slot, :, place].astype(jnp.float32)
        value = value + partial[group, :, place].astype(jnp.float32)
        for m in range(1, GROUPS):
            scattered(t, m).wait_recv()
            value = value + crossed_over[group_before(m), :, place].astype(jnp.float32)
        summed[:, place] = value
        return squares_so_far + jnp.sum(value * value, axis=-1, keepdims=True)

    close_squares = lax.fori_loop(0, TAIL, finished, jnp.zeros((share, 1), jnp.float32))
    close_scale = lax.rsqrt(close_squares * (1.0 / width) + 1e-06)

    def publish(t):
        place = tail_cols(t)
        value = summed[:, place] * close_scale * dec_gain_ref[1:2, place]
        closing[own_slot, :, place] = value.astype(closing.dtype)
        for m in range(1, GROUPS):
            collect(t, m, own_slot).start()
        across(t, group, lane).start()

    each(TAIL, publish)

    def arrive_head(i):
        head_copy(i).wait()

    each(chunks * blocks, arrive_head)

    def forward(t):
        for m in range(1, GROUPS):
            member = group_before(m)
            collect(t, m, lane * GROUPS + member).wait_recv()
            across(t, member, lane).start()

    def head(t):
        for m in range(GROUPS):
            across(t, m, 1 - lane).wait_recv()
        for u in range(ratio):
            c = t * ratio + u
            final = closing[:, :, cols(c)].astype(jnp.float32).reshape(every, columns)
            final = final.astype(jnp.bfloat16)
            for b in range(blocks):
                scores[b] += jnp.dot(final, wqkv_v[c, 4 + b], preferred_element_type=jnp.float32)

    def spread_rows(t):
        @pl.when(t < TAIL)
        def _():
            forward(t)

        @pl.when(t >= 1)
        def _():
            head(t - 1)

    each(TAIL + 1, spread_rows)
    summed_exp = jnp.zeros((every, 1), jnp.float32)
    picked = jnp.zeros((every, 1), jnp.float32)
    for b in range(blocks):
        values = scores[b]
        entry = lax.broadcasted_iota(jnp.int32, (every, tile_columns), 1)
        entry = (entry + (section * blocks + b) * tile_columns).astype(jnp.float32)
        summed_exp = summed_exp + jnp.sum(jnp.exp(values), axis=-1, keepdims=True)
        picked = picked + jnp.sum(
            jnp.where(entry == wanted, values, 0.0), axis=-1, keepdims=True
        )
    place = lax.broadcasted_iota(jnp.int32, (every, 128), 1)
    packed = jnp.where(place == 0, summed_exp, jnp.where(place == 1, picked, 0.0))
    packed = jnp.concatenate([packed, jnp.zeros((128 - every, 128), jnp.float32)], 0)
    stats[...] = packed.T[:8]
    for k in range(1, count):
        share_stats(k, section).start()
    stats_landed[section] = stats[...]
    for b in range(blocks):
        logits_ref[:, b * tile_columns : (b + 1) * tile_columns] = scores[b].astype(
            logits_ref.dtype
        )
    for k in range(1, count):
        share_stats(k, source_of(k)).wait_recv()
    gathered = stats_landed[0]
    for k in range(1, count):
        gathered = gathered + stats_landed[k]
    here = lax.broadcasted_iota(jnp.int32, (1, 128), 1) < every
    token = jnp.log(jnp.where(here, gathered[0:1], 1.0)) - jnp.where(here, gathered[1:2], 0.0)
    loss_ref[...] = jnp.broadcast_to(token, loss_ref.shape)
    for k in range(1, rep_count):
        share_loss(k, rep).start()
    loss_landed[rep] = loss_ref[...]
    for k in range(1, rep_count):
        share_loss(k, lax.rem(rep + rep_count - k, rep_count)).wait_recv()
    losses = loss_landed[0]
    for k in range(1, rep_count):
        losses = losses + loss_landed[k]
    mean = jnp.sum(losses[0:1], axis=-1, keepdims=True) / (every * rep_count)
    mean_ref[...] = jnp.broadcast_to(mean, mean_ref.shape)

    def drain(i):
        spread(i, own).wait_send()
        reduce(i).wait_send()

        @pl.when(group < GROUPS - 1)
        def _():
            hand(i).wait_send()

        @pl.when(group > 0)
        def _():
            back(i).wait_send()

    each(pieces, drain)

    def drain_tail(t):
        swap(t).wait_send()
        for m in range(1, GROUPS):
            scatter(t, m).wait_send()
            collect(t, m, own_slot).wait_send()
        for m in range(GROUPS):
            across(t, m, lane).wait_send()

    each(TAIL, drain_tail)
    for k in range(1, count):
        share_stats(k, section).wait_send()
    for k in range(1, rep_count):
        share_loss(k, rep).wait_send()


def stream(sent, number, lengths, x, enc_gain, dec_gain, docid, targets, *weights):
    total_rows, width = x.shape
    wqkv, wout, wcross, wclose, whead = weights
    rows = total_rows // 2
    inner = wout.shape[0]
    tiles = 3 * (inner // WTILE)
    columns = width // CHUNKS
    share_count, share, _ = docid.shape
    every = share_count * share
    vocab = whead.shape[1]
    dma = pltpu.SemaphoreType.DMA
    vmem = pl.BlockSpec(memory_space=pltpu.VMEM)
    smem = pl.BlockSpec(memory_space=pltpu.SMEM)
    anywhere = pl.BlockSpec(memory_space=pl.ANY)
    small = (8, 128)
    bf16 = jnp.bfloat16
    f32 = jnp.float32
    reps = lax.axis_size("rep")
    logits, loss, mean = pl.pallas_call(
        functools.partial(stream_kernel, sent),
        out_shape=(
            jax.ShapeDtypeStruct((every, vocab), bf16),
            jax.ShapeDtypeStruct(small, f32),
            jax.ShapeDtypeStruct(small, f32),
        ),
        in_specs=[smem, anywhere, vmem, vmem, vmem, vmem] + [anywhere] * 5,
        out_specs=(vmem, vmem, vmem),
        scratch_shapes=[
            pltpu.VMEM((CHUNKS, tiles, WTILE, columns), bf16),
            pltpu.VMEM((CHUNKS, inner, columns), bf16),
            pltpu.VMEM((total_rows, width), bf16),
            pltpu.VMEM((rows, width), bf16),
            pltpu.VMEM((rows, width), bf16),
            pltpu.VMEM((sent // 2, width), bf16),
            pltpu.VMEM((tiles, rows, WTILE), f32),
            pltpu.VMEM((rows, 1), f32),
            pltpu.VMEM((rows, inner), bf16),
            pltpu.VMEM((rows, width), bf16),
            pltpu.VMEM((2, rows, WTILE), f32),
            pltpu.VMEM((every, WTILE), f32),
            pltpu.VMEM(docid.shape, bf16),
            pltpu.VMEM((GROUPS,) + docid.shape[1:], bf16),
            pltpu.VMEM((GROUPS,) + docid.shape[1:], bf16),
            pltpu.VMEM((GROUPS,) + docid.shape[1:], bf16),
            pltpu.VMEM(docid.shape[1:], f32),
            pltpu.VMEM(docid.shape, bf16),
            pltpu.VMEM((vocab // WTILE, every, WTILE), f32),
            pltpu.VMEM(small, f32),
            pltpu.VMEM((share_count,) + small, f32),
            pltpu.VMEM((reps,) + small, f32),
        ]
        + [dma((CHUNKS,))] * 3
        + [dma((CHUNKS * HALVES,))] * 10
        + [dma((CHUNKS,))] * 3
        + [dma((CHUNKS * (vocab // WTILE),))]
        + [dma((TAIL,))] * 2
        + [dma((GROUPS * TAIL,))] * 6
        + [dma((share_count,))] * 2
        + [dma((reps,))] * 2,
        compiler_params=pltpu.CompilerParams(
            collective_id=number, has_side_effects=True, vmem_limit_bytes=67043328
        ),
        name=f"stream_{sent}",
    )(
        lengths,
        x,
        enc_gain,
        dec_gain,
        docid,
        targets,
        wqkv.reshape(tiles, WTILE, width),
        wout,
        wcross,
        wclose,
        whead,
    )
    return logits, loss[0, :every], mean[0, 0]


def largest_kernel(limits, lengths_ref, out_ref, mine, landed, send, recv):
    me = lax.axis_index("rep")
    count = lax.axis_size("rep")
    barrier = pltpu.get_barrier_semaphore()
    for k in range(1, count):
        pl.semaphore_signal(
            barrier, inc=1, device_id={"rep": lax.rem(me + k, count)}, device_id_type=MESH
        )
    live = 0
    for m in range(lengths_ref.shape[0]):
        for d in range(lengths_ref.shape[1]):
            live = live + lengths_ref[m, d]
    mine[...] = jnp.full(mine.shape, live, jnp.int32).astype(jnp.float32)
    pl.semaphore_wait(barrier, count - 1)

    def share(k, slot):
        return pltpu.make_async_remote_copy(
            src_ref=mine,
            dst_ref=landed.at[slot],
            send_sem=send.at[k],
            recv_sem=recv.at[k],
            device_id={"rep": lax.rem(me + k, count)},
            device_id_type=MESH,
        )

    for k in range(1, count):
        share(k, me).start()
    most = mine[...]
    for k in range(1, count):
        slot = lax.rem(me + count - k, count)
        share(k, slot).wait_recv()
        most = jnp.maximum(most, landed[slot])
    choice = jnp.zeros(most.shape, jnp.float32)
    for limit in limits:
        choice = choice + jnp.where(most > limit, 1.0, 0.0)
    out_ref[0, 0] = jnp.max(choice).astype(jnp.int32)
    for k in range(1, count):
        share(k, me).wait_send()


def branch_choice(limits, lengths):
    count = lax.axis_size("rep")
    dma = pltpu.SemaphoreType.DMA
    small = (8, 128)
    return pl.pallas_call(
        functools.partial(largest_kernel, limits),
        out_shape=jax.ShapeDtypeStruct((1, 1), jnp.int32),
        in_specs=[pl.BlockSpec(memory_space=pltpu.SMEM)],
        out_specs=pl.BlockSpec(memory_space=pltpu.SMEM),
        scratch_shapes=[pltpu.VMEM(small, jnp.float32), pltpu.VMEM((count,) + small, jnp.float32)]
        + [dma((count,))] * 2,
        compiler_params=pltpu.CompilerParams(collective_id=10, has_side_effects=True),
        name="largest",
    )(lengths)[0, 0]


def butterfly(value, axis, combine):
    for bit in range(lax.axis_size(axis).bit_length() - 1):
        value = combine(value, from_partner(value, axis, bit))
    return value


def greet(me, count):
    barrier = pltpu.get_barrier_semaphore()
    for k in range(1, count):
        pl.semaphore_signal(
            barrier, inc=1, device_id={"section": lax.rem(me + k, count)}, device_id_type=MESH
        )
    pl.semaphore_wait(barrier, count - 1)


def to_peer(src, dst, send, recv, peer):
    return pltpu.make_async_remote_copy(
        src_ref=src,
        dst_ref=dst,
        send_sem=send,
        recv_sem=recv,
        device_id={"section": peer},
        device_id_type=MESH,
    )


def closing_kernel(terms, residual, gain, out, landed, s1, r1, s2, r2):
    count = terms.shape[0]
    me = lax.axis_index("section")
    greet(me, count)

    def scatter(k, slot):
        peer = lax.rem(me + k, count)
        return to_peer(terms.at[peer], landed.at[slot], s1.at[k], r1.at[k], peer)

    def gather(k, slot):
        return to_peer(out.at[slot], out.at[slot], s2.at[k], r2.at[k], lax.rem(me + k, count))

    for k in range(1, count):
        scatter(k, me).start()
    total = residual[...] + terms[me].astype(jnp.float32)
    for k in range(1, count):
        slot = lax.rem(me + count - k, count)
        scatter(k, slot).wait_recv()
        total = total + landed[slot].astype(jnp.float32)
    scale = lax.rsqrt(jnp.mean(total * total, axis=-1, keepdims=True) + 1e-06)
    out[me] = (total * scale * gain[...]).astype(out.dtype)
    for k in range(1, count):
        gather(k, me).start()
    for k in range(1, count):
        gather(k, lax.rem(me + count - k, count)).wait_recv()
    for k in range(1, count):
        scatter(k, me).wait_send()
        gather(k, me).wait_send()


def closing_rows_of(terms, residual, gain):
    count = terms.shape[0]
    dma = pltpu.SemaphoreType.DMA
    vmem = pl.BlockSpec(memory_space=pltpu.VMEM)
    return pl.pallas_call(
        closing_kernel,
        out_shape=jax.ShapeDtypeStruct(terms.shape, jnp.bfloat16),
        in_specs=[vmem] * 3,
        out_specs=vmem,
        scratch_shapes=[pltpu.VMEM(terms.shape, jnp.bfloat16)] + [dma((count,))] * 4,
        compiler_params=pltpu.CompilerParams(collective_id=8, has_side_effects=True),
        name="closing",
    )(terms, residual, gain)


def sums_kernel(value, out, landed, send, recv):
    count = landed.shape[0]
    me = lax.axis_index("section")
    greet(me, count)

    def share(k, slot):
        return to_peer(value, landed.at[slot], send.at[k], recv.at[k], lax.rem(me + k, count))

    for k in range(1, count):
        share(k, me).start()
    landed[me] = value[...]
    for k in range(1, count):
        share(k, lax.rem(me + count - k, count)).wait_recv()
    total = landed[0]
    for k in range(1, count):
        total = total + landed[k]
    out[...] = total
    for k in range(1, count):
        share(k, me).wait_send()


def section_sum(value, count):
    dma = pltpu.SemaphoreType.DMA
    vmem = pl.BlockSpec(memory_space=pltpu.VMEM)
    return pl.pallas_call(
        sums_kernel,
        out_shape=jax.ShapeDtypeStruct(value.shape, value.dtype),
        in_specs=[vmem],
        out_specs=vmem,
        scratch_shapes=[pltpu.VMEM((count,) + value.shape, value.dtype)] + [dma((count,))] * 2,
        compiler_params=pltpu.CompilerParams(collective_id=9, has_side_effects=True),
        name="section_sum",
    )(value)


def large_shards(
    document_token_embedding,
    doc_lengths,
    docid_embed,
    docid_targets,
    enc_gain,
    dec_gain,
    w_enc_qkv,
    w_enc_out,
    cross_query_key_value_weight,
    w_cross_out,
    docid_head_weight,
):
    section_index = lax.axis_index("section")
    group_index = section_index // 2
    micro_count, row_count, width = document_token_embedding.shape
    doc_count = doc_lengths.shape[1]
    doc_span = row_count // doc_count
    all_rows = micro_count * row_count
    positions = jnp.arange(all_rows)
    row_doc = (positions // doc_span).astype(jnp.int32)
    live = (jnp.arange(doc_span)[None, :] < doc_lengths.reshape(-1)[:, None]).reshape(-1)
    key_doc = jnp.where(live, row_doc, -1).astype(jnp.int32)
    gain = lax.dynamic_slice_in_dim(enc_gain, group_index, 1, 0)
    hidden = encode(
        all_rows,
        all_rows,
        2,
        document_token_embedding.reshape(all_rows, width),
        gain,
        row_doc,
        key_doc,
        w_enc_qkv,
        w_enc_out,
    )
    memory = norm_rows(hidden, enc_gain[GROUPS]).astype(jnp.bfloat16)

    decoder_rows = docid_embed.shape[1]
    every = micro_count * decoder_rows
    docid_span = decoder_rows // doc_count
    decoder_doc = jnp.arange(every) // docid_span
    cross_heads = cross_query_key_value_weight.shape[1] // HD
    flat_docid = docid_embed.reshape(every, width)
    dec_normed = norm_rows(flat_docid, dec_gain[0]).astype(jnp.bfloat16)

    def project(values, weight):
        return (
            jnp.einsum("rd,cd->rc", values, weight, preferred_element_type=jnp.float32)
            .astype(jnp.bfloat16)
            .reshape(-1, cross_heads, HD)
        )

    queries = project(dec_normed, cross_query_key_value_weight[0])
    keys = project(memory, cross_query_key_value_weight[1])
    values = project(memory, cross_query_key_value_weight[2])
    allowed = decoder_doc[:, None] == key_doc[None, :]
    mixture = attend(queries, keys, values, allowed).reshape(every, -1)
    cross_terms = jnp.dot(mixture, w_cross_out, preferred_element_type=jnp.float32)
    section_count = lax.axis_size("section")
    share = every // section_count
    residual = lax.dynamic_slice_in_dim(flat_docid, section_index * share, share, 0)
    closing = closing_rows_of(
        cross_terms.astype(jnp.bfloat16).reshape(section_count, share, width),
        residual.astype(jnp.float32),
        dec_gain[1:2],
    ).reshape(every, width)
    scores_vocab = jnp.dot(closing, docid_head_weight, preferred_element_type=jnp.float32)
    vocab_local = docid_head_weight.shape[1]
    targets = docid_targets.reshape(-1)
    matches = targets[:, None] == section_index * vocab_local + jnp.arange(vocab_local)
    sums = jnp.stack(
        [
            jnp.sum(jnp.exp(scores_vocab), axis=-1),
            jnp.sum(jnp.where(matches, scores_vocab, 0.0), axis=-1),
        ]
    )
    padding = ((0, -sums.shape[0] % 8), (0, -sums.shape[1] % 128))
    sums = section_sum(jnp.pad(sums, padding), section_count)[:2, :every]
    token_loss = jnp.log(sums[0]) - sums[1]
    loss_sum = butterfly(jnp.sum(token_loss)[None], "rep", jnp.add)[0]
    mean_loss = loss_sum / (token_loss.size * lax.axis_size("rep"))
    logits = scores_vocab.astype(jnp.bfloat16).reshape(micro_count, decoder_rows, vocab_local)
    return (logits, token_loss.reshape(docid_targets.shape), mean_loss)


def fast_shards(
    document_token_embedding,
    doc_lengths,
    docid_embed,
    docid_targets,
    enc_gain,
    dec_gain,
    *weights,
):
    micro_count, row_count, width = document_token_embedding.shape
    decoder_rows = docid_embed.shape[1]
    sizes = (row_count * 3 // 4, row_count)
    section_count = lax.axis_size("section")
    choice = branch_choice(sizes, doc_lengths)

    def streamed(sent, number):
        def run():
            logits, token_loss, mean_loss = stream(
                sent,
                number,
                doc_lengths,
                document_token_embedding.reshape(micro_count * row_count, width),
                enc_gain,
                dec_gain,
                docid_embed.reshape(section_count, -1, width),
                docid_targets,
                *weights,
            )
            return (
                logits.reshape(micro_count, decoder_rows, -1),
                token_loss.reshape(docid_targets.shape),
                mean_loss,
            )

        return run

    def large():
        return large_shards(
            document_token_embedding,
            doc_lengths,
            docid_embed,
            docid_targets,
            enc_gain,
            dec_gain,
            *weights,
        )

    branches = [streamed(sent, number) for number, sent in enumerate(sizes)] + [large]
    return lax.switch(choice, branches)


def solution(mesh):
    in_specs = (
        P("rep", None, None),
        P("rep", None),
        P("rep", None, None),
        P("rep", None),
        P(),
        P(),
        P(None, "section", None),
        P("section", None),
        P(None, "section", None),
        P("section", None),
        P(None, "section"),
    )
    out_specs = (P("rep", None, "section"), P("rep", None), P())
    local = shards if mesh.shape["section"] != 2 * GROUPS else fast_shards
    return jax.shard_map(local, mesh=mesh, in_specs=in_specs, out_specs=out_specs, check_vma=False)
```

```python
import functools

import jax
import jax.numpy as jnp
from jax import lax
from jax.experimental import pallas as pl
from jax.experimental.pallas import tpu as pltpu
from jax.sharding import PartitionSpec as P

HD = 64
GROUPS = 4
WTILE = 512
PARTS = 4
CHUNKS = 8
AHEAD = 3
HALVES = 2
TAIL = 4
MESH = pl.DeviceIdType.MESH


def from_partner(block, axis, distance):
    count = lax.axis_size(axis)
    route = []
    for low in range(count):
        high = low | 1 << distance
        if high != low and high < count:
            route += [(low, high), (high, low)]
    return lax.ppermute(block, axis, route)


def from_behind(block, axis, distance):
    devices = range(lax.axis_size(axis))
    route = [(i - distance, i) for i in devices if i - distance in devices]
    return lax.ppermute(block, axis, route)


def passed_along(shard, axis, by):
    size = lax.axis_size(axis)
    return lax.ppermute(shard, axis, [(i, (i + by) % size) for i in range(size)])


def norm_rows(values, gain):
    values = values.astype(jnp.float32)
    scale = lax.rsqrt(jnp.mean(values * values, axis=-1, keepdims=True) + 1e-06)
    return values * scale * gain


def attend(queries, key_rows, values, allowed):
    scores = jnp.einsum("qhe,khe->hqk", queries, key_rows, preferred_element_type=jnp.float32)
    attention_weight_rows = jnp.where(allowed[None], jnp.exp(scores), 0.0)
    probabilities = (
        attention_weight_rows / jnp.sum(attention_weight_rows, axis=-1, keepdims=True)
    ).astype(jnp.bfloat16)
    mixture = jnp.einsum("hqk,khe->qhe", probabilities, values, preferred_element_type=jnp.float32)
    return mixture.astype(jnp.bfloat16)


def live_keys(lengths, key_doc, key_place):
    owners = jnp.arange(lengths.shape[0])
    matches = (key_doc[:, None] == owners[None, :]) & (key_place[:, None] < lengths[None, :])
    return jnp.any(matches, axis=1)


def lane_gather(own_rows, lane_bits, lane_index, concat_dim):
    for bit_number in range(lane_bits):
        partner = from_partner(own_rows, "section", bit_number)
        lower_half = lane_index // (1 << bit_number) % 2 == 0
        own_rows = jnp.where(
            lower_half,
            jnp.concatenate([own_rows, partner], concat_dim),
            jnp.concatenate([partner, own_rows], concat_dim),
        )
    return own_rows


def lane_reduce(totals, lane_bits, lane_index):
    for bit_number in reversed(range(lane_bits)):
        half_rows = totals.shape[0] // 2
        lower_half = lane_index // (1 << bit_number) % 2 == 0
        kept_rows = jnp.where(lower_half, totals[:half_rows], totals[half_rows:])
        outgoing = jnp.where(lower_half, totals[half_rows:], totals[:half_rows])
        totals = kept_rows + from_partner(outgoing, "section", bit_number)
    return totals


def relay_memory(encoder_memory, group_index, lane_count):
    encoder_memory = jnp.where(group_index == 0, encoder_memory, jnp.zeros_like(encoder_memory))
    for stride in (1, 2):
        encoder_memory = encoder_memory + from_behind(
            encoder_memory, "section", stride * lane_count
        )
    return encoder_memory


def shards(
    document_token_embedding,
    doc_lengths,
    docid_embed,
    docid_targets,
    enc_gain,
    dec_gain,
    w_enc_qkv,
    w_enc_out,
    cross_query_key_value_weight,
    w_cross_out,
    docid_head_weight,
):
    lane_count = lax.axis_size("section") // GROUPS
    lane_bits = lane_count.bit_length() - 1
    section_index = lax.axis_index("section")
    group_index = section_index // lane_count
    lane_index = section_index % lane_count
    micro_count, row_count, model_width = document_token_embedding.shape
    doc_count = doc_lengths.shape[1]
    doc_span = row_count // doc_count
    block_rows = row_count // lane_count
    local_heads = w_enc_qkv.shape[1] // HD
    positions = jnp.arange(row_count)
    key_doc = positions // doc_span
    key_place = positions % doc_span
    same_doc = key_doc[:, None] == key_doc[None, :]

    def partial_update(normed, lengths):
        allowed = same_doc & live_keys(lengths, key_doc, key_place)[None, :]
        projected = jnp.einsum(
            "rd,mcd->mrc", normed, w_enc_qkv, preferred_element_type=jnp.float32
        ).astype(jnp.bfloat16)
        projected = projected.reshape(3, row_count, local_heads, HD)
        mixture = attend(projected[0], projected[1], projected[2], allowed).reshape(row_count, -1)
        return jnp.dot(mixture, w_enc_out, preferred_element_type=jnp.float32)

    def section_step(step_index, loop_state):
        handed, encoder_memory = loop_state
        micro_index = step_index - group_index
        slot_index = jnp.clip(micro_index, 0, micro_count - 1)
        lengths = lax.dynamic_index_in_dim(doc_lengths, slot_index, 0, keepdims=False)
        layer_gain = lax.dynamic_index_in_dim(enc_gain, group_index, 0, keepdims=False)
        incoming = lax.dynamic_index_in_dim(
            document_token_embedding, jnp.minimum(step_index, micro_count - 1), 0, keepdims=False
        )
        incoming = lax.dynamic_slice_in_dim(incoming, lane_index * block_rows, block_rows, 0)
        current = jnp.where(group_index == 0, incoming, handed)
        normed = lane_gather(
            norm_rows(current, layer_gain).astype(jnp.bfloat16), lane_bits, lane_index, 0
        )
        summed = lane_reduce(partial_update(normed, lengths), lane_bits, lane_index)
        result = (current.astype(jnp.float32) + summed).astype(jnp.bfloat16)
        handed = passed_along(result, "section", lane_count)
        finished_index = step_index - (GROUPS - 1)
        finished_slot = jnp.clip(finished_index, 0, micro_count - 1)
        keeping = (group_index == 0) & (finished_index >= 0) & (finished_index < micro_count)
        stored = lax.dynamic_update_index_in_dim(encoder_memory, handed, finished_slot, 0)
        encoder_memory = jnp.where(keeping, stored, encoder_memory)
        return (handed, encoder_memory)

    handed = jnp.zeros((block_rows, model_width), jnp.bfloat16)
    encoder_memory = jnp.zeros((micro_count, block_rows, model_width), jnp.bfloat16)
    handed, encoder_memory = lax.fori_loop(
        0, micro_count + GROUPS - 1, section_step, (handed, encoder_memory)
    )
    encoder_memory = norm_rows(encoder_memory, enc_gain[GROUPS]).astype(jnp.bfloat16)
    encoder_memory = relay_memory(encoder_memory, group_index, lane_count)
    encoder_memory = lane_gather(encoder_memory, lane_bits, lane_index, 1)
    decoder_rows = docid_embed.shape[1]
    docid_span = decoder_rows // doc_count
    decoder_doc = jnp.arange(decoder_rows) // docid_span
    cross_heads = cross_query_key_value_weight.shape[1] // HD
    dec_normed = norm_rows(docid_embed, dec_gain[0]).astype(jnp.bfloat16)
    queries = jnp.einsum(
        "brd,cd->brc",
        dec_normed,
        cross_query_key_value_weight[0],
        preferred_element_type=jnp.float32,
    ).astype(jnp.bfloat16)
    memory_heads = jnp.einsum(
        "pye,qve->qpyv",
        encoder_memory,
        cross_query_key_value_weight[1:],
        preferred_element_type=jnp.float32,
    ).astype(jnp.bfloat16)

    def cross_one(sample_queries, sample_keys, sample_values, lengths):
        allowed = (decoder_doc[:, None] == key_doc[None, :]) & live_keys(
            lengths, key_doc, key_place
        )[None, :]
        return attend(sample_queries, sample_keys, sample_values, allowed)

    mixture = jax.vmap(cross_one)(
        queries.reshape(micro_count, decoder_rows, cross_heads, HD),
        memory_heads[0].reshape(micro_count, row_count, cross_heads, HD),
        memory_heads[1].reshape(micro_count, row_count, cross_heads, HD),
        doc_lengths,
    )
    cross_terms = jnp.einsum(
        "brc,cd->brd",
        mixture.reshape(micro_count, decoder_rows, -1),
        w_cross_out,
        preferred_element_type=jnp.float32,
    )
    cross_sum = lax.psum(cross_terms, "section")
    closing_rows = norm_rows(docid_embed.astype(jnp.float32) + cross_sum, dec_gain[1]).astype(
        jnp.bfloat16
    )
    scores_vocab = jnp.einsum(
        "brd,dv->brv", closing_rows, docid_head_weight, preferred_element_type=jnp.float32
    )
    vocab_local = docid_head_weight.shape[1]
    vocab_start = section_index * vocab_local
    matches = docid_targets[..., None] == vocab_start + jnp.arange(vocab_local)
    exponent_total, picked = lax.psum(
        (
            jnp.sum(jnp.exp(scores_vocab), axis=-1),
            jnp.sum(jnp.where(matches, scores_vocab, 0.0), axis=-1),
        ),
        "section",
    )
    token_loss = jnp.log(exponent_total) - picked
    mean_loss = lax.psum(jnp.sum(token_loss), "rep") / (token_loss.size * lax.axis_size("rep"))
    return (scores_vocab.astype(jnp.bfloat16), token_loss, mean_loss)


def encoder_kernel(
    sent,
    x_ref,
    gain_ref,
    row_doc_ref,
    key_doc_ref,
    wqkv_ref,
    wout_ref,
    mem_ref,
    wqkv_v,
    wout_v,
    hid,
    work,
    part,
    qkv,
    mix,
    w_sem,
    o_sem,
    x_sem,
    gs,
    gr,
    rs,
    rr,
    zs,
    zr,
    bs,
    br,
    ms,
    mr,
):
    rows, width = hid.shape
    half = sent // 2
    columns = width // PARTS
    tiles = wqkv_v.shape[0]
    per = tiles // 3
    section = lax.axis_index("section")
    count = lax.axis_size("section")
    group = section // 2
    lane = section % 2
    partner = section + 1 - 2 * lane
    ahead = lax.rem(section + 2, count)
    behind = lax.rem(section + count - 2, count)
    own = pl.ds(pl.multiple_of(lane * half, 16), half)
    other = pl.ds(pl.multiple_of((1 - lane) * half, 16), half)

    def cols(c):
        return pl.ds(pl.multiple_of(c * columns, columns), columns)

    def weight_copy(j):
        return pltpu.make_async_copy(
            wqkv_ref.at[j // per, pl.ds((j % per) * WTILE, WTILE)], wqkv_v.at[j], w_sem.at[j]
        )

    def out_copy(c):
        return pltpu.make_async_copy(wout_ref.at[:, cols(c)], wout_v.at[c], o_sem.at[c])

    def remote(src, dst, send, recv, device):
        return pltpu.make_async_remote_copy(
            src_ref=src,
            dst_ref=dst,
            send_sem=send,
            recv_sem=recv,
            device_id={"section": device},
            device_id_type=MESH,
        )

    def gather(c, block):
        return remote(hid.at[block, cols(c)], hid.at[block, cols(c)], gs.at[c], gr.at[c], partner)

    def reduce(c):
        return remote(work.at[other, cols(c)], part.at[:, cols(c)], rs.at[c], rr.at[c], partner)

    def hand(c):
        return remote(hid.at[own, cols(c)], hid.at[own, cols(c)], zs.at[c], zr.at[c], ahead)

    def back(c):
        return remote(mem_ref.at[own, cols(c)], mem_ref.at[own, cols(c)], bs.at[c], br.at[c], behind)

    def spread(c, block):
        return remote(
            mem_ref.at[block, cols(c)], mem_ref.at[block, cols(c)], ms.at[c], mr.at[c], partner
        )

    def each(size, body):
        def step(i, carry):
            body(i)
            return carry

        lax.fori_loop(0, size, step, 0)

    entry = pltpu.make_async_copy(x_ref.at[pl.ds(0, sent)], hid.at[pl.ds(0, sent)], x_sem)

    @pl.when(group == 0)
    def _():
        entry.start()

    for j in range(tiles):
        weight_copy(j).start()
    for c in range(PARTS):
        out_copy(c).start()

    barrier = pltpu.get_barrier_semaphore()
    for device in (partner, ahead, behind):
        pl.semaphore_signal(barrier, inc=1, device_id={"section": device}, device_id_type=MESH)
    pl.semaphore_wait(barrier, 3)

    if sent < rows:
        hid[sent:, :] = jnp.zeros((rows - sent, width), hid.dtype)
    if sent < mem_ref.shape[0]:
        mem_ref[sent:, :] = jnp.zeros((mem_ref.shape[0] - sent, width), mem_ref.dtype)

    @pl.when(group == 0)
    def _():
        entry.wait()

    @pl.when(group > 0)
    def _():
        def arrive(c):
            hand(c).wait_recv()
            gather(c, own).start()

        each(PARTS, arrive)

        def complete(c):
            gather(c, other).wait_recv()
            gather(c, own).wait_send()

        each(PARTS, complete)

    def norm(r):
        block = pl.ds(pl.multiple_of(r * 16, 16), 16)
        values = hid[block, :].astype(jnp.float32)
        scale = lax.rsqrt(jnp.mean(values * values, axis=-1, keepdims=True) + 1e-06)
        work[block, :] = (values * scale * gain_ref[...]).astype(work.dtype)

    each(rows // 16, norm)

    def project(j):
        pltpu.make_async_copy(
            wqkv_ref.at[0, pl.ds(0, WTILE)], wqkv_v.at[j], w_sem.at[j]
        ).wait()
        qkv[j] = lax.dot_general(
            work[...], wqkv_v[j], (((1,), (1,)), ((), ())), preferred_element_type=jnp.float32
        ).astype(qkv.dtype)

    each(tiles, project)
    pairs = WTILE // (2 * HD)

    def attend_pair(p):
        tile = p // pairs
        span = pl.ds(pl.multiple_of((p % pairs) * 2 * HD, 2 * HD), 2 * HD)
        queries = qkv[tile, :, span]
        keys = qkv[per + tile, :, span]
        values = qkv[2 * per + tile, :, span]
        allowed = row_doc_ref[...] == key_doc_ref[...]
        first = lax.broadcasted_iota(jnp.int32, (rows, 2 * HD), 1) < HD
        mixed = []
        for side in range(2):
            keep = first if side == 0 else jnp.logical_not(first)
            chosen = jnp.where(keep, queries.astype(jnp.float32), 0.0).astype(jnp.bfloat16)
            scores = lax.dot_general(
                chosen, keys, (((1,), (1,)), ((), ())), preferred_element_type=jnp.float32
            )
            weights = jnp.where(allowed, jnp.exp(scores), 0.0)
            shares = (weights / jnp.sum(weights, axis=-1, keepdims=True)).astype(jnp.bfloat16)
            mixed.append(jnp.dot(shares, values, preferred_element_type=jnp.float32))
        mix[:, pl.ds(pl.multiple_of(p * 2 * HD, 2 * HD), 2 * HD)] = jnp.where(
            first, mixed[0], mixed[1]
        ).astype(mix.dtype)

    each(per * pairs, attend_pair)

    def output(c):
        out_copy(c).wait()
        work[:, cols(c)] = jnp.dot(
            mix[...], wout_v[c], preferred_element_type=jnp.float32
        ).astype(work.dtype)
        reduce(c).start()

    each(PARTS, output)

    def total(c):
        reduce(c).wait_recv()
        return (
            hid[own, cols(c)].astype(jnp.float32)
            + work[own, cols(c)].astype(jnp.float32)
            + part[:, cols(c)].astype(jnp.float32)
        ).astype(hid.dtype)

    @pl.when(group < GROUPS - 1)
    def _():
        def finish(c):
            hid[own, cols(c)] = total(c)
            hand(c).start()

        each(PARTS, finish)

        def relay(c):
            back(c).wait_recv()

            @pl.when(group > 0)
            def _():
                back(c).start()

            spread(c, own).start()

        each(PARTS, relay)

    @pl.when(group == GROUPS - 1)
    def _():
        def finish(c):
            mem_ref[own, cols(c)] = total(c)
            back(c).start()
            spread(c, own).start()

        each(PARTS, finish)

    def drain(c):
        spread(c, other).wait_recv()
        spread(c, own).wait_send()
        reduce(c).wait_send()

        @pl.when(group < GROUPS - 1)
        def _():
            hand(c).wait_send()

        @pl.when(group > 0)
        def _():
            back(c).wait_send()

    each(PARTS, drain)


def encode(rows, sent, number, x, gain, row_doc, key_doc, wqkv, wout):
    total_rows, width = x.shape
    inner = wout.shape[0]
    tiles = 3 * (inner // WTILE)
    dma = pltpu.SemaphoreType.DMA
    vmem = pl.BlockSpec(memory_space=pltpu.VMEM)
    anywhere = pl.BlockSpec(memory_space=pl.ANY)
    return pl.pallas_call(
        functools.partial(encoder_kernel, sent),
        out_shape=jax.ShapeDtypeStruct((total_rows, width), jnp.bfloat16),
        in_specs=[anywhere, vmem, vmem, vmem, anywhere, anywhere],
        out_specs=vmem,
        scratch_shapes=[
            pltpu.VMEM((tiles, WTILE, width), jnp.bfloat16),
            pltpu.VMEM((PARTS, inner, width // PARTS), jnp.bfloat16),
            pltpu.VMEM((rows, width), jnp.bfloat16),
            pltpu.VMEM((rows, width), jnp.bfloat16),
            pltpu.VMEM((sent // 2, width), jnp.bfloat16),
            pltpu.VMEM((tiles, rows, WTILE), jnp.bfloat16),
            pltpu.VMEM((rows, inner), jnp.bfloat16),
            dma((tiles,)),
            dma((PARTS,)),
            dma,
        ]
        + [dma((PARTS,))] * 10,
        compiler_params=pltpu.CompilerParams(
            collective_id=number, has_side_effects=True, vmem_limit_bytes=67043328
        ),
        name=f"encoder_{sent}",
    )(x, gain, row_doc[:rows, None], key_doc[None, :rows], wqkv, wout)


def stream_kernel(
    sent,
    lengths_ref,
    x_ref,
    enc_gain_ref,
    dec_gain_ref,
    docid_ref,
    target_ref,
    wqkv_ref,
    wout_ref,
    wcross_ref,
    wclose_ref,
    whead_ref,
    logits_ref,
    token_ref,
    mean_ref,
    wqkv_v,
    wout_v,
    entered,
    hid,
    work,
    part,
    acc,
    squares,
    mix,
    memory,
    cross_acc,
    query_acc,
    terms,
    landed,
    partial,
    crossed_over,
    summed,
    closing,
    scores,
    stats,
    stats_landed,
    loss_ref,
    loss_landed,
    w_sem,
    o_sem,
    x_sem,
    gs,
    gr,
    rs,
    rr,
    zs,
    zr,
    bs,
    br,
    ms,
    mr,
    k_sem,
    q_sem,
    c_sem,
    h_sem,
    ys,
    yr,
    ts,
    tr,
    us,
    ur,
    fs,
    fr,
    ss,
    sr,
    ls,
    lr,
):
    rows, width = hid.shape
    half = sent // 2
    chunks, tiles, tile_columns, columns = wqkv_v.shape
    per = tiles // 3
    micro_count, doc_count = lengths_ref.shape
    doc_total = micro_count * doc_count
    doc_span = x_ref.shape[0] // doc_total
    share_count, share, _ = docid_ref.shape
    every = share_count * share
    blocks = whead_ref.shape[1] // tile_columns
    section = lax.axis_index("section")
    count = lax.axis_size("section")
    rep = lax.axis_index("rep")
    rep_count = lax.axis_size("rep")
    group = section // 2
    lane = section % 2
    partner = section + 1 - 2 * lane
    ahead = lax.rem(section + 2, count)
    behind = lax.rem(section + count - 2, count)
    own = pl.ds(pl.multiple_of(lane * half, 16), half)
    other = pl.ds(pl.multiple_of((1 - lane) * half, 16), half)

    def cols(c):
        return pl.ds(pl.multiple_of(c * columns, columns), columns)

    def weight_copy(c):
        return pltpu.make_async_copy(wqkv_ref.at[:, :, cols(c)], wqkv_v.at[c], w_sem.at[c])

    def out_copy(c):
        return pltpu.make_async_copy(wout_ref.at[:, cols(c)], wout_v.at[c], o_sem.at[c])

    def entry_copy(c):
        return pltpu.make_async_copy(x_ref.at[:, cols(c)], entered.at[:, cols(c)], x_sem.at[c])

    def key_copy(c):
        return pltpu.make_async_copy(
            wcross_ref.at[pl.ds(1, 2), :, cols(c)], wqkv_v.at[c, pl.ds(0, 2)], k_sem.at[c]
        )

    def query_copy(c):
        return pltpu.make_async_copy(wcross_ref.at[0, :, cols(c)], wqkv_v.at[c, 2], q_sem.at[c])

    def close_copy(c):
        return pltpu.make_async_copy(wclose_ref.at[:, cols(c)], wqkv_v.at[c, 3], c_sem.at[c])

    def head_copy(i):
        c = i // blocks
        b = i % blocks
        return pltpu.make_async_copy(
            whead_ref.at[cols(c), pl.ds(pl.multiple_of(b * tile_columns, 128), tile_columns)],
            wqkv_v.at[c, 4 + b],
            h_sem.at[i],
        )

    def remote(src, dst, send, recv, device):
        return pltpu.make_async_remote_copy(
            src_ref=src,
            dst_ref=dst,
            send_sem=send,
            recv_sem=recv,
            device_id={"section": device},
            device_id_type=MESH,
        )

    pieces = chunks * HALVES
    piece = columns // HALVES

    def span_of(i):
        return pl.ds(pl.multiple_of(i * piece, piece), piece)

    def gather(i, block):
        place = hid.at[block, span_of(i)]
        return remote(place, place, gs.at[i], gr.at[i], partner)

    def reduce(i):
        place = span_of(i)
        return remote(work.at[other, place], part.at[:, place], rs.at[i], rr.at[i], partner)

    def hand(i):
        place = hid.at[own, span_of(i)]
        return remote(place, place, zs.at[i], zr.at[i], ahead)

    def back(i):
        place = memory.at[own, span_of(i)]
        return remote(place, place, bs.at[i], br.at[i], behind)

    def spread(i, block):
        place = memory.at[block, span_of(i)]
        return remote(place, place, ms.at[i], mr.at[i], partner)

    def peer(k):
        return lax.rem(section + k, count)

    def source_of(k):
        return lax.rem(section + count - k, count)

    stretch = width // TAIL
    lanes = count // GROUPS
    own_slot = lane * GROUPS + group

    def tail_cols(t):
        return pl.ds(pl.multiple_of(t * stretch, stretch), stretch)

    def group_after(k):
        return lax.rem(group + k, GROUPS)

    def group_before(k):
        return lax.rem(group + GROUPS - k, GROUPS)

    def swap(t):
        theirs = pl.ds((1 - lane) * GROUPS, GROUPS)
        place = tail_cols(t)
        return remote(
            terms.at[theirs, :, place], landed.at[:, :, place], ys.at[t], yr.at[t], partner
        )

    def scatter(t, k):
        place = tail_cols(t)
        i = k * TAIL + t
        return remote(
            partial.at[group_after(k), :, place],
            crossed_over.at[group, :, place],
            ts.at[i],
            tr.at[i],
            group_after(k) * lanes + lane,
        )

    def scattered(t, k):
        place = tail_cols(t)
        i = k * TAIL + t
        return remote(
            partial.at[group, :, place],
            crossed_over.at[group_before(k), :, place],
            ts.at[i],
            tr.at[i],
            group_after(k) * lanes + lane,
        )

    def collect(t, k, slot):
        place = closing.at[slot, :, tail_cols(t)]
        i = k * TAIL + t
        return remote(place, place, us.at[i], ur.at[i], group_after(k) * lanes + lane)

    def across(t, member, side):
        place = closing.at[side * GROUPS + member, :, tail_cols(t)]
        i = member * TAIL + t
        return remote(place, place, fs.at[i], fr.at[i], partner)

    def share_stats(k, slot):
        return remote(stats, stats_landed.at[slot], ss.at[k], sr.at[k], peer(k))

    def share_loss(k, slot):
        return pltpu.make_async_remote_copy(
            src_ref=loss_ref,
            dst_ref=loss_landed.at[slot],
            send_sem=ls.at[k],
            recv_sem=lr.at[k],
            device_id={"rep": lax.rem(rep + k, rep_count)},
            device_id_type=MESH,
        )

    def each(size, body):
        def step(i, carry):
            body(i)
            return carry

        lax.fori_loop(0, size, step, 0)

    @pl.when(group == 0)
    def _():
        for c in range(chunks):
            entry_copy(c).start()

    for c in range(chunks):
        weight_copy(c).start()
    for c in range(chunks):
        out_copy(c).start()

    barrier = pltpu.get_barrier_semaphore()
    for k in range(1, count):
        pl.semaphore_signal(barrier, inc=1, device_id={"section": peer(k)}, device_id_type=MESH)
    for k in range(1, rep_count):
        pl.semaphore_signal(
            barrier, inc=1, device_id={"rep": lax.rem(rep + k, rep_count)}, device_id_type=MESH
        )
    pl.semaphore_wait(barrier, count + rep_count - 2)

    if sent < rows:
        hid[sent:, :] = jnp.zeros((rows - sent, width), hid.dtype)
        memory[sent:, :] = jnp.zeros((rows - sent, width), memory.dtype)
    acc[...] = jnp.zeros_like(acc)
    cross_acc[...] = jnp.zeros_like(cross_acc)
    query_acc[...] = jnp.zeros_like(query_acc)
    scores[...] = jnp.zeros_like(scores)
    squares[...] = jnp.zeros_like(squares)

    def placed(shape, dim):
        position = lax.broadcasted_iota(jnp.int32, shape, dim)
        owner = jnp.full(shape, -1, jnp.int32)
        source = jnp.full(shape, -1, jnp.int32)
        start = 0
        for d in range(doc_total):
            end = start + lengths_ref[d // doc_count, d % doc_count]
            inside = (position >= start) & (position < end)
            owner = jnp.where(inside, d, owner)
            source = jnp.where(inside, d * doc_span + position - start, source)
            start = end
        return owner, source

    row_doc, row_source = placed((rows, 1), 0)
    row_doc = jnp.maximum(row_doc, 0)
    key_doc, _ = placed((1, rows), 1)

    asked = target_ref.shape[1]
    wanted = jnp.concatenate(
        [jnp.broadcast_to(target_ref[m : m + 1, :], (asked, asked)) for m in range(micro_count)], 0
    )
    diagonal = lax.broadcasted_iota(jnp.int32, (every, asked), 0) % asked
    diagonal = diagonal == lax.broadcasted_iota(jnp.int32, (every, asked), 1)
    wanted = jnp.sum(
        jnp.where(diagonal, wanted.astype(jnp.float32), 0.0), axis=-1, keepdims=True
    )

    def project(c, weight_dim):
        values = hid[:, cols(c)].astype(jnp.float32)
        squares[...] += jnp.sum(values * values, axis=-1, keepdims=True)
        scaled = (values * enc_gain_ref[pl.ds(group, 1), cols(c)]).astype(jnp.bfloat16)

        for j in range(tiles):
            acc[j] += lax.dot_general(
                scaled,
                wqkv_v[c, j],
                (((1,), (weight_dim,)), ((), ())),
                preferred_element_type=jnp.float32,
            )

    @pl.when(group == 0)
    def _():
        origin = lax.broadcasted_iota(jnp.int32, (rows, x_ref.shape[0]), 1)
        pick = (row_source == origin).astype(jnp.float32).astype(jnp.bfloat16)

        def first(c):
            entry_copy(c).wait()
            hid[:, cols(c)] = jnp.dot(
                pick, entered[:, cols(c)], preferred_element_type=jnp.float32
            ).astype(hid.dtype)
            weight_copy(c).wait()
            project(c, 1)

        each(chunks, first)

    @pl.when(group > 0)
    def _():
        side = tile_columns // 2

        def turn(c):
            weight_copy(c).wait()

            def block(j):
                whole = wqkv_v[c, j]
                for a in range(2):
                    for b in range(2):
                        quarter = whole[a * side : (a + 1) * side, b * side : (b + 1) * side]
                        wqkv_v[c, j, b * side : (b + 1) * side, a * side : (a + 1) * side] = (
                            quarter.T
                        )

            each(tiles, block)

        each(chunks, turn)

        def step(i):
            @pl.when(i < chunks)
            def _():
                for u in range(HALVES):
                    hand(i * HALVES + u).wait_recv()
                    gather(i * HALVES + u, own).start()

            @pl.when(i >= AHEAD)
            def _():
                for u in range(HALVES):
                    gather((i - AHEAD) * HALVES + u, other).wait_recv()
                project(i - AHEAD, 0)

        each(chunks + AHEAD, step)

        def complete(i):
            gather(i, own).wait_send()

        each(pieces, complete)

    def fetch(c):
        query_copy(c).start()
        key_copy(c).start()
        close_copy(c).start()

    each(chunks, fetch)

    def fetch_head(i):
        head_copy(i).start()

    each(chunks * blocks, fetch_head)

    def halves(size):
        return lax.broadcasted_iota(jnp.int32, (size, 2 * HD), 1) < HD

    def share_keys(queries, keys, allowed):
        first = halves(queries.shape[0])
        both = jnp.concatenate(
            [jnp.where(first, queries, 0.0), jnp.where(first, 0.0, queries)], 0
        ).astype(jnp.bfloat16)
        raw = lax.dot_general(
            both, keys, (((1,), (1,)), ((), ())), preferred_element_type=jnp.float32
        )
        weights = jnp.where(allowed, jnp.exp(raw), 0.0)
        shares = weights * (1.0 / jnp.sum(weights, axis=-1, keepdims=True))
        return shares.astype(jnp.bfloat16)

    def mix_values(shares, values):
        size = shares.shape[0] // 2
        mixed = jnp.dot(shares, values, preferred_element_type=jnp.float32)
        return jnp.where(halves(size), mixed[:size], mixed[size:])

    pairs = tile_columns // (2 * HD)
    scale = lax.rsqrt(squares[...] * (1.0 / width) + 1e-06)
    allowed = row_doc == key_doc
    allowed = jnp.concatenate([allowed, allowed], 0)

    def pair_of(member, p):
        at = slice(p % pairs * 2 * HD, (p % pairs + 1) * 2 * HD)
        return acc[member * per + p // pairs, :, at] * scale

    everyone = range(per * pairs)
    shared = [
        share_keys(pair_of(0, p), pair_of(1, p).astype(jnp.bfloat16), allowed) for p in everyone
    ]
    for p in everyone:
        mixed = mix_values(shared[p], pair_of(2, p).astype(jnp.bfloat16))
        mix[:, p * 2 * HD : (p + 1) * 2 * HD] = mixed.astype(mix.dtype)

    def output(c):
        out_copy(c).wait()
        work[:, cols(c)] = jnp.dot(
            mix[...], wout_v[c], preferred_element_type=jnp.float32
        ).astype(work.dtype)
        for u in range(HALVES):
            reduce(c * HALVES + u).start()

    each(chunks, output)

    def total(i):
        reduce(i).wait_recv()
        return (
            hid[own, span_of(i)].astype(jnp.float32)
            + work[own, span_of(i)].astype(jnp.float32)
            + part[:, span_of(i)].astype(jnp.float32)
        ).astype(hid.dtype)

    @pl.when(group < GROUPS - 1)
    def _():
        def finish(i):
            hid[own, span_of(i)] = total(i)
            hand(i).start()

        each(pieces, finish)

    @pl.when(group == GROUPS - 1)
    def _():
        def finish(i):
            memory[own, span_of(i)] = total(i)
            back(i).start()
            spread(i, own).start()

        each(pieces, finish)

    def docid_rows(c):
        return docid_ref[:, :, cols(c)].astype(jnp.float32).reshape(every, columns)

    def ask(c, sums):
        values = docid_rows(c)
        scaled = (values * dec_gain_ref[0:1, cols(c)]).astype(jnp.bfloat16)
        query_copy(c).wait()
        query_acc[...] += lax.dot_general(
            scaled, wqkv_v[c, 2], (((1,), (1,)), ((), ())), preferred_element_type=jnp.float32
        )
        return sums + jnp.sum(values * values, axis=-1, keepdims=True)

    query_squares = lax.fori_loop(0, chunks, ask, jnp.zeros((every, 1), jnp.float32))
    query_scale = lax.rsqrt(query_squares * (1.0 / width) + 1e-06)
    squares[...] = jnp.zeros_like(squares)

    def recall(c):
        for u in range(HALVES):
            spread(c * HALVES + u, other).wait_recv()
        key_copy(c).wait()
        values = memory[:, cols(c)].astype(jnp.float32)
        squares[...] += jnp.sum(values * values, axis=-1, keepdims=True)
        scaled = (values * enc_gain_ref[GROUPS : GROUPS + 1, cols(c)]).astype(jnp.bfloat16)
        for j in range(2):
            cross_acc[j] += lax.dot_general(
                scaled, wqkv_v[c, j], (((1,), (1,)), ((), ())), preferred_element_type=jnp.float32
            )

    def relay(i):
        @pl.when((i < chunks) & (group < GROUPS - 1))
        def _():
            for u in range(HALVES):
                back(i * HALVES + u).wait_recv()

                @pl.when(group > 0)
                def _():
                    back(i * HALVES + u).start()

                spread(i * HALVES + u, own).start()

        @pl.when(i >= AHEAD)
        def _():
            recall(i - AHEAD)

    each(chunks + AHEAD, relay)

    memory_scale = lax.rsqrt(squares[...] * (1.0 / width) + 1e-06)
    asking = lax.broadcasted_iota(jnp.int32, (every, 1), 0) // (every // doc_total)
    visible = asking == key_doc
    visible = jnp.concatenate([visible, visible], 0)
    spans = [slice(p * 2 * HD, (p + 1) * 2 * HD) for p in range(pairs)]
    shared = [
        share_keys(
            query_acc[:, at] * query_scale,
            (cross_acc[0, :, at] * memory_scale).astype(jnp.bfloat16),
            visible,
        )
        for at in spans
    ]
    crossed = [
        mix_values(shared[p], (cross_acc[1, :, spans[p]] * memory_scale).astype(jnp.bfloat16))
        for p in range(pairs)
    ]
    crossed = [value.astype(jnp.bfloat16) for value in crossed]
    crossed = jnp.concatenate(crossed, 1)

    ratio = chunks // TAIL

    def close(t):
        for u in range(ratio):
            c = t * ratio + u
            close_copy(c).wait()
            product = jnp.dot(crossed, wqkv_v[c, 3], preferred_element_type=jnp.float32)
            terms[:, :, cols(c)] = product.reshape(share_count, share, columns).astype(terms.dtype)
        swap(t).start()

    each(TAIL, close)
    mine = pl.ds(lane * GROUPS, GROUPS)

    def halfway(t):
        swap(t).wait_recv()
        both = terms[mine, :, tail_cols(t)].astype(jnp.float32)
        both = both + landed[:, :, tail_cols(t)].astype(jnp.float32)
        partial[:, :, tail_cols(t)] = both.astype(partial.dtype)
        for m in range(1, GROUPS):
            scatter(t, m).start()

    each(TAIL, halfway)

    def finished(t, squares_so_far):
        place = tail_cols(t)
        value = docid_ref[own_slot, :, place].astype(jnp.float32)
        value = value + partial[group, :, place].astype(jnp.float32)
        for m in range(1, GROUPS):
            scattered(t, m).wait_recv()
            value = value + crossed_over[group_before(m), :, place].astype(jnp.float32)
        summed[:, place] = value
        return squares_so_far + jnp.sum(value * value, axis=-1, keepdims=True)

    close_squares = lax.fori_loop(0, TAIL, finished, jnp.zeros((share, 1), jnp.float32))
    close_scale = lax.rsqrt(close_squares * (1.0 / width) + 1e-06)

    def publish(t):
        place = tail_cols(t)
        value = summed[:, place] * close_scale * dec_gain_ref[1:2, place]
        closing[own_slot, :, place] = value.astype(closing.dtype)
        for m in range(1, GROUPS):
            collect(t, m, own_slot).start()
        across(t, group, lane).start()

    each(TAIL, publish)

    def arrive_head(i):
        head_copy(i).wait()

    each(chunks * blocks, arrive_head)

    def forward(t):
        for m in range(1, GROUPS):
            member = group_before(m)
            collect(t, m, lane * GROUPS + member).wait_recv()
            across(t, member, lane).start()

    def head(t):
        for m in range(GROUPS):
            across(t, m, 1 - lane).wait_recv()
        for u in range(ratio):
            c = t * ratio + u
            final = closing[:, :, cols(c)].astype(jnp.float32).reshape(every, columns)
            final = final.astype(jnp.bfloat16)
            for b in range(blocks):
                scores[b] += jnp.dot(final, wqkv_v[c, 4 + b], preferred_element_type=jnp.float32)

    def spread_rows(t):
        @pl.when(t < TAIL)
        def _():
            forward(t)

        @pl.when(t >= 1)
        def _():
            head(t - 1)

    each(TAIL + 1, spread_rows)
    summed_exp = jnp.zeros((every, 1), jnp.float32)
    picked = jnp.zeros((every, 1), jnp.float32)
    for b in range(blocks):
        values = scores[b]
        entry = lax.broadcasted_iota(jnp.int32, (every, tile_columns), 1)
        entry = (entry + (section * blocks + b) * tile_columns).astype(jnp.float32)
        summed_exp = summed_exp + jnp.sum(jnp.exp(values), axis=-1, keepdims=True)
        picked = picked + jnp.sum(
            jnp.where(entry == wanted, values, 0.0), axis=-1, keepdims=True
        )
    place = lax.broadcasted_iota(jnp.int32, (every, 128), 1)
    packed = jnp.where(place == 0, summed_exp, jnp.where(place == 1, picked, 0.0))
    packed = jnp.concatenate([packed, jnp.zeros((128 - every, 128), jnp.float32)], 0)
    stats[...] = packed.T[:8]
    for k in range(1, count):
        share_stats(k, section).start()
    stats_landed[section] = stats[...]
    for b in range(blocks):
        for m in range(micro_count):
            logits_ref[m, :, b * tile_columns : (b + 1) * tile_columns] = scores[
                b, m * asked : (m + 1) * asked
            ].astype(logits_ref.dtype)
    for k in range(1, count):
        share_stats(k, source_of(k)).wait_recv()
    gathered = stats_landed[0]
    for k in range(1, count):
        gathered = gathered + stats_landed[k]
    here = lax.broadcasted_iota(jnp.int32, (1, 128), 1) < every
    token = jnp.log(jnp.where(here, gathered[0:1], 1.0)) - jnp.where(here, gathered[1:2], 0.0)
    loss_ref[...] = jnp.broadcast_to(token, loss_ref.shape)
    for k in range(1, rep_count):
        share_loss(k, rep).start()
    loss_landed[rep] = loss_ref[...]
    for m in range(micro_count):
        token_ref[m : m + 1, :] = token[:, m * asked : (m + 1) * asked]
    for k in range(1, rep_count):
        share_loss(k, lax.rem(rep + rep_count - k, rep_count)).wait_recv()
    losses = loss_landed[0]
    for k in range(1, rep_count):
        losses = losses + loss_landed[k]
    mean = jnp.sum(losses[0:1], axis=-1, keepdims=True) / (every * rep_count)
    mean_ref[...] = jnp.broadcast_to(mean, mean_ref.shape)

    def drain(i):
        spread(i, own).wait_send()
        reduce(i).wait_send()

        @pl.when(group < GROUPS - 1)
        def _():
            hand(i).wait_send()

        @pl.when(group > 0)
        def _():
            back(i).wait_send()

    each(pieces, drain)

    def drain_tail(t):
        swap(t).wait_send()
        for m in range(1, GROUPS):
            scatter(t, m).wait_send()
            collect(t, m, own_slot).wait_send()
        for m in range(GROUPS):
            across(t, m, lane).wait_send()

    each(TAIL, drain_tail)
    for k in range(1, count):
        share_stats(k, section).wait_send()
    for k in range(1, rep_count):
        share_loss(k, rep).wait_send()


def stream(sent, number, lengths, x, enc_gain, dec_gain, docid, targets, *weights):
    total_rows, width = x.shape
    wqkv, wout, wcross, wclose, whead = weights
    rows = total_rows // 2
    inner = wout.shape[0]
    tiles = 3 * (inner // WTILE)
    columns = width // CHUNKS
    share_count, share, _ = docid.shape
    every = share_count * share
    vocab = whead.shape[1]
    dma = pltpu.SemaphoreType.DMA
    vmem = pl.BlockSpec(memory_space=pltpu.VMEM)
    smem = pl.BlockSpec(memory_space=pltpu.SMEM)
    anywhere = pl.BlockSpec(memory_space=pl.ANY)
    small = (8, 128)
    bf16 = jnp.bfloat16
    f32 = jnp.float32
    reps = lax.axis_size("rep")
    logits, token_loss, mean = pl.pallas_call(
        functools.partial(stream_kernel, sent),
        out_shape=(
            jax.ShapeDtypeStruct(targets.shape + (vocab,), bf16),
            jax.ShapeDtypeStruct(targets.shape, f32),
            jax.ShapeDtypeStruct((1, 1), f32),
        ),
        in_specs=[smem, anywhere, vmem, vmem, vmem, vmem] + [anywhere] * 5,
        out_specs=(vmem, vmem, vmem),
        scratch_shapes=[
            pltpu.VMEM((CHUNKS, tiles, WTILE, columns), bf16),
            pltpu.VMEM((CHUNKS, inner, columns), bf16),
            pltpu.VMEM((total_rows, width), bf16),
            pltpu.VMEM((rows, width), bf16),
            pltpu.VMEM((rows, width), bf16),
            pltpu.VMEM((sent // 2, width), bf16),
            pltpu.VMEM((tiles, rows, WTILE), f32),
            pltpu.VMEM((rows, 1), f32),
            pltpu.VMEM((rows, inner), bf16),
            pltpu.VMEM((rows, width), bf16),
            pltpu.VMEM((2, rows, WTILE), f32),
            pltpu.VMEM((every, WTILE), f32),
            pltpu.VMEM(docid.shape, bf16),
            pltpu.VMEM((GROUPS,) + docid.shape[1:], bf16),
            pltpu.VMEM((GROUPS,) + docid.shape[1:], bf16),
            pltpu.VMEM((GROUPS,) + docid.shape[1:], bf16),
            pltpu.VMEM(docid.shape[1:], f32),
            pltpu.VMEM(docid.shape, bf16),
            pltpu.VMEM((vocab // WTILE, every, WTILE), f32),
            pltpu.VMEM(small, f32),
            pltpu.VMEM((share_count,) + small, f32),
            pltpu.VMEM(small, f32),
            pltpu.VMEM((reps,) + small, f32),
        ]
        + [dma((CHUNKS,))] * 3
        + [dma((CHUNKS * HALVES,))] * 10
        + [dma((CHUNKS,))] * 3
        + [dma((CHUNKS * (vocab // WTILE),))]
        + [dma((TAIL,))] * 2
        + [dma((GROUPS * TAIL,))] * 6
        + [dma((share_count,))] * 2
        + [dma((reps,))] * 2,
        compiler_params=pltpu.CompilerParams(
            collective_id=number, has_side_effects=True, vmem_limit_bytes=67043328
        ),
        name=f"stream_{sent}",
    )(
        lengths,
        x,
        enc_gain,
        dec_gain,
        docid,
        targets,
        wqkv.reshape(tiles, WTILE, width),
        wout,
        wcross,
        wclose,
        whead,
    )
    return logits, token_loss, mean[0, 0]


def largest_kernel(limits, lengths_ref, out_ref, mine, landed, send, recv):
    me = lax.axis_index("rep")
    count = lax.axis_size("rep")
    barrier = pltpu.get_barrier_semaphore()
    for k in range(1, count):
        pl.semaphore_signal(
            barrier, inc=1, device_id={"rep": lax.rem(me + k, count)}, device_id_type=MESH
        )
    live = 0
    for m in range(lengths_ref.shape[0]):
        for d in range(lengths_ref.shape[1]):
            live = live + lengths_ref[m, d]
    mine[...] = jnp.full(mine.shape, live, jnp.int32).astype(jnp.float32)
    pl.semaphore_wait(barrier, count - 1)

    def share(k, slot):
        return pltpu.make_async_remote_copy(
            src_ref=mine,
            dst_ref=landed.at[slot],
            send_sem=send.at[k],
            recv_sem=recv.at[k],
            device_id={"rep": lax.rem(me + k, count)},
            device_id_type=MESH,
        )

    for k in range(1, count):
        share(k, me).start()
    most = mine[...]
    for k in range(1, count):
        slot = lax.rem(me + count - k, count)
        share(k, slot).wait_recv()
        most = jnp.maximum(most, landed[slot])
    choice = jnp.zeros(most.shape, jnp.float32)
    for limit in limits:
        choice = choice + jnp.where(most > limit, 1.0, 0.0)
    out_ref[0, 0] = jnp.max(choice).astype(jnp.int32)
    for k in range(1, count):
        share(k, me).wait_send()


def branch_choice(limits, lengths):
    count = lax.axis_size("rep")
    dma = pltpu.SemaphoreType.DMA
    small = (8, 128)
    return pl.pallas_call(
        functools.partial(largest_kernel, limits),
        out_shape=jax.ShapeDtypeStruct((1, 1), jnp.int32),
        in_specs=[pl.BlockSpec(memory_space=pltpu.SMEM)],
        out_specs=pl.BlockSpec(memory_space=pltpu.SMEM),
        scratch_shapes=[pltpu.VMEM(small, jnp.float32), pltpu.VMEM((count,) + small, jnp.float32)]
        + [dma((count,))] * 2,
        compiler_params=pltpu.CompilerParams(collective_id=10, has_side_effects=True),
        name="largest",
    )(lengths)[0, 0]


def butterfly(value, axis, combine):
    for bit in range(lax.axis_size(axis).bit_length() - 1):
        value = combine(value, from_partner(value, axis, bit))
    return value


def greet(me, count):
    barrier = pltpu.get_barrier_semaphore()
    for k in range(1, count):
        pl.semaphore_signal(
            barrier, inc=1, device_id={"section": lax.rem(me + k, count)}, device_id_type=MESH
        )
    pl.semaphore_wait(barrier, count - 1)


def to_peer(src, dst, send, recv, peer):
    return pltpu.make_async_remote_copy(
        src_ref=src,
        dst_ref=dst,
        send_sem=send,
        recv_sem=recv,
        device_id={"section": peer},
        device_id_type=MESH,
    )


def closing_kernel(terms, residual, gain, out, landed, s1, r1, s2, r2):
    count = terms.shape[0]
    me = lax.axis_index("section")
    greet(me, count)

    def scatter(k, slot):
        peer = lax.rem(me + k, count)
        return to_peer(terms.at[peer], landed.at[slot], s1.at[k], r1.at[k], peer)

    def gather(k, slot):
        return to_peer(out.at[slot], out.at[slot], s2.at[k], r2.at[k], lax.rem(me + k, count))

    for k in range(1, count):
        scatter(k, me).start()
    total = residual[...] + terms[me].astype(jnp.float32)
    for k in range(1, count):
        slot = lax.rem(me + count - k, count)
        scatter(k, slot).wait_recv()
        total = total + landed[slot].astype(jnp.float32)
    scale = lax.rsqrt(jnp.mean(total * total, axis=-1, keepdims=True) + 1e-06)
    out[me] = (total * scale * gain[...]).astype(out.dtype)
    for k in range(1, count):
        gather(k, me).start()
    for k in range(1, count):
        gather(k, lax.rem(me + count - k, count)).wait_recv()
    for k in range(1, count):
        scatter(k, me).wait_send()
        gather(k, me).wait_send()


def closing_rows_of(terms, residual, gain):
    count = terms.shape[0]
    dma = pltpu.SemaphoreType.DMA
    vmem = pl.BlockSpec(memory_space=pltpu.VMEM)
    return pl.pallas_call(
        closing_kernel,
        out_shape=jax.ShapeDtypeStruct(terms.shape, jnp.bfloat16),
        in_specs=[vmem] * 3,
        out_specs=vmem,
        scratch_shapes=[pltpu.VMEM(terms.shape, jnp.bfloat16)] + [dma((count,))] * 4,
        compiler_params=pltpu.CompilerParams(collective_id=8, has_side_effects=True),
        name="closing",
    )(terms, residual, gain)


def sums_kernel(value, out, landed, send, recv):
    count = landed.shape[0]
    me = lax.axis_index("section")
    greet(me, count)

    def share(k, slot):
        return to_peer(value, landed.at[slot], send.at[k], recv.at[k], lax.rem(me + k, count))

    for k in range(1, count):
        share(k, me).start()
    landed[me] = value[...]
    for k in range(1, count):
        share(k, lax.rem(me + count - k, count)).wait_recv()
    total = landed[0]
    for k in range(1, count):
        total = total + landed[k]
    out[...] = total
    for k in range(1, count):
        share(k, me).wait_send()


def section_sum(value, count):
    dma = pltpu.SemaphoreType.DMA
    vmem = pl.BlockSpec(memory_space=pltpu.VMEM)
    return pl.pallas_call(
        sums_kernel,
        out_shape=jax.ShapeDtypeStruct(value.shape, value.dtype),
        in_specs=[vmem],
        out_specs=vmem,
        scratch_shapes=[pltpu.VMEM((count,) + value.shape, value.dtype)] + [dma((count,))] * 2,
        compiler_params=pltpu.CompilerParams(collective_id=9, has_side_effects=True),
        name="section_sum",
    )(value)


def large_shards(
    document_token_embedding,
    doc_lengths,
    docid_embed,
    docid_targets,
    enc_gain,
    dec_gain,
    w_enc_qkv,
    w_enc_out,
    cross_query_key_value_weight,
    w_cross_out,
    docid_head_weight,
):
    section_index = lax.axis_index("section")
    group_index = section_index // 2
    micro_count, row_count, width = document_token_embedding.shape
    doc_count = doc_lengths.shape[1]
    doc_span = row_count // doc_count
    all_rows = micro_count * row_count
    positions = jnp.arange(all_rows)
    row_doc = (positions // doc_span).astype(jnp.int32)
    live = (jnp.arange(doc_span)[None, :] < doc_lengths.reshape(-1)[:, None]).reshape(-1)
    key_doc = jnp.where(live, row_doc, -1).astype(jnp.int32)
    gain = lax.dynamic_slice_in_dim(enc_gain, group_index, 1, 0)
    hidden = encode(
        all_rows,
        all_rows,
        2,
        document_token_embedding.reshape(all_rows, width),
        gain,
        row_doc,
        key_doc,
        w_enc_qkv,
        w_enc_out,
    )
    memory = norm_rows(hidden, enc_gain[GROUPS]).astype(jnp.bfloat16)

    decoder_rows = docid_embed.shape[1]
    every = micro_count * decoder_rows
    docid_span = decoder_rows // doc_count
    decoder_doc = jnp.arange(every) // docid_span
    cross_heads = cross_query_key_value_weight.shape[1] // HD
    flat_docid = docid_embed.reshape(every, width)
    dec_normed = norm_rows(flat_docid, dec_gain[0]).astype(jnp.bfloat16)

    def project(values, weight):
        return (
            jnp.einsum("rd,cd->rc", values, weight, preferred_element_type=jnp.float32)
            .astype(jnp.bfloat16)
            .reshape(-1, cross_heads, HD)
        )

    queries = project(dec_normed, cross_query_key_value_weight[0])
    keys = project(memory, cross_query_key_value_weight[1])
    values = project(memory, cross_query_key_value_weight[2])
    allowed = decoder_doc[:, None] == key_doc[None, :]
    mixture = attend(queries, keys, values, allowed).reshape(every, -1)
    cross_terms = jnp.dot(mixture, w_cross_out, preferred_element_type=jnp.float32)
    section_count = lax.axis_size("section")
    share = every // section_count
    residual = lax.dynamic_slice_in_dim(flat_docid, section_index * share, share, 0)
    closing = closing_rows_of(
        cross_terms.astype(jnp.bfloat16).reshape(section_count, share, width),
        residual.astype(jnp.float32),
        dec_gain[1:2],
    ).reshape(every, width)
    scores_vocab = jnp.dot(closing, docid_head_weight, preferred_element_type=jnp.float32)
    vocab_local = docid_head_weight.shape[1]
    targets = docid_targets.reshape(-1)
    matches = targets[:, None] == section_index * vocab_local + jnp.arange(vocab_local)
    sums = jnp.stack(
        [
            jnp.sum(jnp.exp(scores_vocab), axis=-1),
            jnp.sum(jnp.where(matches, scores_vocab, 0.0), axis=-1),
        ]
    )
    padding = ((0, -sums.shape[0] % 8), (0, -sums.shape[1] % 128))
    sums = section_sum(jnp.pad(sums, padding), section_count)[:2, :every]
    token_loss = jnp.log(sums[0]) - sums[1]
    loss_sum = butterfly(jnp.sum(token_loss)[None], "rep", jnp.add)[0]
    mean_loss = loss_sum / (token_loss.size * lax.axis_size("rep"))
    logits = scores_vocab.astype(jnp.bfloat16).reshape(micro_count, decoder_rows, vocab_local)
    return (logits, token_loss.reshape(docid_targets.shape), mean_loss)


def fast_shards(
    document_token_embedding,
    doc_lengths,
    docid_embed,
    docid_targets,
    enc_gain,
    dec_gain,
    *weights,
):
    micro_count, row_count, width = document_token_embedding.shape
    sizes = (row_count * 3 // 4, row_count)
    section_count = lax.axis_size("section")
    choice = branch_choice(sizes, doc_lengths)

    def streamed(sent, number):
        def run():
            return stream(
                sent,
                number,
                doc_lengths,
                document_token_embedding.reshape(micro_count * row_count, width),
                enc_gain,
                dec_gain,
                docid_embed.reshape(section_count, -1, width),
                docid_targets,
                *weights,
            )
        return run

    def large():
        return large_shards(
            document_token_embedding,
            doc_lengths,
            docid_embed,
            docid_targets,
            enc_gain,
            dec_gain,
            *weights,
        )

    branches = [streamed(sent, number) for number, sent in enumerate(sizes)] + [large]
    return lax.switch(choice, branches)


def solution(mesh):
    in_specs = (
        P("rep", None, None),
        P("rep", None),
        P("rep", None, None),
        P("rep", None),
        P(),
        P(),
        P(None, "section", None),
        P("section", None),
        P(None, "section", None),
        P("section", None),
        P(None, "section"),
    )
    out_specs = (P("rep", None, "section"), P("rep", None), P())
    local = shards if mesh.shape["section"] != 2 * GROUPS else fast_shards
    return jax.shard_map(local, mesh=mesh, in_specs=in_specs, out_specs=out_specs, check_vma=False)
```

```python
import functools

import jax
import jax.numpy as jnp
from jax import lax
from jax.experimental import pallas as pl
from jax.experimental.pallas import tpu as pltpu
from jax.sharding import PartitionSpec as P

HD = 64
GROUPS = 4
WTILE = 512
PARTS = 4
CHUNKS = 8
AHEAD = 3
HALVES = 2
TAIL = 4
MESH = pl.DeviceIdType.MESH


def from_partner(block, axis, distance):
    count = lax.axis_size(axis)
    route = []
    for low in range(count):
        high = low | 1 << distance
        if high != low and high < count:
            route += [(low, high), (high, low)]
    return lax.ppermute(block, axis, route)


def from_behind(block, axis, distance):
    devices = range(lax.axis_size(axis))
    route = [(i - distance, i) for i in devices if i - distance in devices]
    return lax.ppermute(block, axis, route)


def passed_along(shard, axis, by):
    size = lax.axis_size(axis)
    return lax.ppermute(shard, axis, [(i, (i + by) % size) for i in range(size)])


def norm_rows(values, gain):
    values = values.astype(jnp.float32)
    scale = lax.rsqrt(jnp.mean(values * values, axis=-1, keepdims=True) + 1e-06)
    return values * scale * gain


def attend(queries, key_rows, values, allowed):
    scores = jnp.einsum("qhe,khe->hqk", queries, key_rows, preferred_element_type=jnp.float32)
    attention_weight_rows = jnp.where(allowed[None], jnp.exp(scores), 0.0)
    probabilities = (
        attention_weight_rows / jnp.sum(attention_weight_rows, axis=-1, keepdims=True)
    ).astype(jnp.bfloat16)
    mixture = jnp.einsum("hqk,khe->qhe", probabilities, values, preferred_element_type=jnp.float32)
    return mixture.astype(jnp.bfloat16)


def live_keys(lengths, key_doc, key_place):
    owners = jnp.arange(lengths.shape[0])
    matches = (key_doc[:, None] == owners[None, :]) & (key_place[:, None] < lengths[None, :])
    return jnp.any(matches, axis=1)


def lane_gather(own_rows, lane_bits, lane_index, concat_dim):
    for bit_number in range(lane_bits):
        partner = from_partner(own_rows, "section", bit_number)
        lower_half = lane_index // (1 << bit_number) % 2 == 0
        own_rows = jnp.where(
            lower_half,
            jnp.concatenate([own_rows, partner], concat_dim),
            jnp.concatenate([partner, own_rows], concat_dim),
        )
    return own_rows


def lane_reduce(totals, lane_bits, lane_index):
    for bit_number in reversed(range(lane_bits)):
        half_rows = totals.shape[0] // 2
        lower_half = lane_index // (1 << bit_number) % 2 == 0
        kept_rows = jnp.where(lower_half, totals[:half_rows], totals[half_rows:])
        outgoing = jnp.where(lower_half, totals[half_rows:], totals[:half_rows])
        totals = kept_rows + from_partner(outgoing, "section", bit_number)
    return totals


def relay_memory(encoder_memory, group_index, lane_count):
    encoder_memory = jnp.where(group_index == 0, encoder_memory, jnp.zeros_like(encoder_memory))
    for stride in (1, 2):
        encoder_memory = encoder_memory + from_behind(
            encoder_memory, "section", stride * lane_count
        )
    return encoder_memory


def shards(
    document_token_embedding,
    doc_lengths,
    docid_embed,
    docid_targets,
    enc_gain,
    dec_gain,
    w_enc_qkv,
    w_enc_out,
    cross_query_key_value_weight,
    w_cross_out,
    docid_head_weight,
):
    lane_count = lax.axis_size("section") // GROUPS
    lane_bits = lane_count.bit_length() - 1
    section_index = lax.axis_index("section")
    group_index = section_index // lane_count
    lane_index = section_index % lane_count
    micro_count, row_count, model_width = document_token_embedding.shape
    doc_count = doc_lengths.shape[1]
    doc_span = row_count // doc_count
    block_rows = row_count // lane_count
    local_heads = w_enc_qkv.shape[1] // HD
    positions = jnp.arange(row_count)
    key_doc = positions // doc_span
    key_place = positions % doc_span
    same_doc = key_doc[:, None] == key_doc[None, :]

    def partial_update(normed, lengths):
        allowed = same_doc & live_keys(lengths, key_doc, key_place)[None, :]
        projected = jnp.einsum(
            "rd,mcd->mrc", normed, w_enc_qkv, preferred_element_type=jnp.float32
        ).astype(jnp.bfloat16)
        projected = projected.reshape(3, row_count, local_heads, HD)
        mixture = attend(projected[0], projected[1], projected[2], allowed).reshape(row_count, -1)
        return jnp.dot(mixture, w_enc_out, preferred_element_type=jnp.float32)

    def section_step(step_index, loop_state):
        handed, encoder_memory = loop_state
        micro_index = step_index - group_index
        slot_index = jnp.clip(micro_index, 0, micro_count - 1)
        lengths = lax.dynamic_index_in_dim(doc_lengths, slot_index, 0, keepdims=False)
        layer_gain = lax.dynamic_index_in_dim(enc_gain, group_index, 0, keepdims=False)
        incoming = lax.dynamic_index_in_dim(
            document_token_embedding, jnp.minimum(step_index, micro_count - 1), 0, keepdims=False
        )
        incoming = lax.dynamic_slice_in_dim(incoming, lane_index * block_rows, block_rows, 0)
        current = jnp.where(group_index == 0, incoming, handed)
        normed = lane_gather(
            norm_rows(current, layer_gain).astype(jnp.bfloat16), lane_bits, lane_index, 0
        )
        summed = lane_reduce(partial_update(normed, lengths), lane_bits, lane_index)
        result = (current.astype(jnp.float32) + summed).astype(jnp.bfloat16)
        handed = passed_along(result, "section", lane_count)
        finished_index = step_index - (GROUPS - 1)
        finished_slot = jnp.clip(finished_index, 0, micro_count - 1)
        keeping = (group_index == 0) & (finished_index >= 0) & (finished_index < micro_count)
        stored = lax.dynamic_update_index_in_dim(encoder_memory, handed, finished_slot, 0)
        encoder_memory = jnp.where(keeping, stored, encoder_memory)
        return (handed, encoder_memory)

    handed = jnp.zeros((block_rows, model_width), jnp.bfloat16)
    encoder_memory = jnp.zeros((micro_count, block_rows, model_width), jnp.bfloat16)
    handed, encoder_memory = lax.fori_loop(
        0, micro_count + GROUPS - 1, section_step, (handed, encoder_memory)
    )
    encoder_memory = norm_rows(encoder_memory, enc_gain[GROUPS]).astype(jnp.bfloat16)
    encoder_memory = relay_memory(encoder_memory, group_index, lane_count)
    encoder_memory = lane_gather(encoder_memory, lane_bits, lane_index, 1)
    decoder_rows = docid_embed.shape[1]
    docid_span = decoder_rows // doc_count
    decoder_doc = jnp.arange(decoder_rows) // docid_span
    cross_heads = cross_query_key_value_weight.shape[1] // HD
    dec_normed = norm_rows(docid_embed, dec_gain[0]).astype(jnp.bfloat16)
    queries = jnp.einsum(
        "brd,cd->brc",
        dec_normed,
        cross_query_key_value_weight[0],
        preferred_element_type=jnp.float32,
    ).astype(jnp.bfloat16)
    memory_heads = jnp.einsum(
        "pye,qve->qpyv",
        encoder_memory,
        cross_query_key_value_weight[1:],
        preferred_element_type=jnp.float32,
    ).astype(jnp.bfloat16)

    def cross_one(sample_queries, sample_keys, sample_values, lengths):
        allowed = (decoder_doc[:, None] == key_doc[None, :]) & live_keys(
            lengths, key_doc, key_place
        )[None, :]
        return attend(sample_queries, sample_keys, sample_values, allowed)

    mixture = jax.vmap(cross_one)(
        queries.reshape(micro_count, decoder_rows, cross_heads, HD),
        memory_heads[0].reshape(micro_count, row_count, cross_heads, HD),
        memory_heads[1].reshape(micro_count, row_count, cross_heads, HD),
        doc_lengths,
    )
    cross_terms = jnp.einsum(
        "brc,cd->brd",
        mixture.reshape(micro_count, decoder_rows, -1),
        w_cross_out,
        preferred_element_type=jnp.float32,
    )
    cross_sum = lax.psum(cross_terms, "section")
    closing_rows = norm_rows(docid_embed.astype(jnp.float32) + cross_sum, dec_gain[1]).astype(
        jnp.bfloat16
    )
    scores_vocab = jnp.einsum(
        "brd,dv->brv", closing_rows, docid_head_weight, preferred_element_type=jnp.float32
    )
    vocab_local = docid_head_weight.shape[1]
    vocab_start = section_index * vocab_local
    matches = docid_targets[..., None] == vocab_start + jnp.arange(vocab_local)
    exponent_total, picked = lax.psum(
        (
            jnp.sum(jnp.exp(scores_vocab), axis=-1),
            jnp.sum(jnp.where(matches, scores_vocab, 0.0), axis=-1),
        ),
        "section",
    )
    token_loss = jnp.log(exponent_total) - picked
    mean_loss = lax.psum(jnp.sum(token_loss), "rep") / (token_loss.size * lax.axis_size("rep"))
    return (scores_vocab.astype(jnp.bfloat16), token_loss, mean_loss)


def encoder_kernel(
    sent,
    x_ref,
    gain_ref,
    row_doc_ref,
    key_doc_ref,
    wqkv_ref,
    wout_ref,
    mem_ref,
    wqkv_v,
    wout_v,
    hid,
    work,
    part,
    qkv,
    mix,
    w_sem,
    o_sem,
    x_sem,
    gs,
    gr,
    rs,
    rr,
    zs,
    zr,
    bs,
    br,
    ms,
    mr,
):
    rows, width = hid.shape
    half = sent // 2
    columns = width // PARTS
    tiles = wqkv_v.shape[0]
    per = tiles // 3
    section = lax.axis_index("section")
    count = lax.axis_size("section")
    group = section // 2
    lane = section % 2
    partner = section + 1 - 2 * lane
    ahead = lax.rem(section + 2, count)
    behind = lax.rem(section + count - 2, count)
    own = pl.ds(pl.multiple_of(lane * half, 16), half)
    other = pl.ds(pl.multiple_of((1 - lane) * half, 16), half)

    def cols(c):
        return pl.ds(pl.multiple_of(c * columns, columns), columns)

    def weight_copy(j):
        return pltpu.make_async_copy(
            wqkv_ref.at[j // per, pl.ds((j % per) * WTILE, WTILE)], wqkv_v.at[j], w_sem.at[j]
        )

    def out_copy(c):
        return pltpu.make_async_copy(wout_ref.at[:, cols(c)], wout_v.at[c], o_sem.at[c])

    def remote(src, dst, send, recv, device):
        return pltpu.make_async_remote_copy(
            src_ref=src,
            dst_ref=dst,
            send_sem=send,
            recv_sem=recv,
            device_id={"section": device},
            device_id_type=MESH,
        )

    def gather(c, block):
        return remote(hid.at[block, cols(c)], hid.at[block, cols(c)], gs.at[c], gr.at[c], partner)

    def reduce(c):
        return remote(work.at[other, cols(c)], part.at[:, cols(c)], rs.at[c], rr.at[c], partner)

    def hand(c):
        return remote(hid.at[own, cols(c)], hid.at[own, cols(c)], zs.at[c], zr.at[c], ahead)

    def back(c):
        return remote(mem_ref.at[own, cols(c)], mem_ref.at[own, cols(c)], bs.at[c], br.at[c], behind)

    def spread(c, block):
        return remote(
            mem_ref.at[block, cols(c)], mem_ref.at[block, cols(c)], ms.at[c], mr.at[c], partner
        )

    def each(size, body):
        def step(i, carry):
            body(i)
            return carry

        lax.fori_loop(0, size, step, 0)

    entry = pltpu.make_async_copy(x_ref.at[pl.ds(0, sent)], hid.at[pl.ds(0, sent)], x_sem)

    @pl.when(group == 0)
    def _():
        entry.start()

    for j in range(tiles):
        weight_copy(j).start()
    for c in range(PARTS):
        out_copy(c).start()

    barrier = pltpu.get_barrier_semaphore()
    for device in (partner, ahead, behind):
        pl.semaphore_signal(barrier, inc=1, device_id={"section": device}, device_id_type=MESH)
    pl.semaphore_wait(barrier, 3)

    if sent < rows:
        hid[sent:, :] = jnp.zeros((rows - sent, width), hid.dtype)
    if sent < mem_ref.shape[0]:
        mem_ref[sent:, :] = jnp.zeros((mem_ref.shape[0] - sent, width), mem_ref.dtype)

    @pl.when(group == 0)
    def _():
        entry.wait()

    @pl.when(group > 0)
    def _():
        def arrive(c):
            hand(c).wait_recv()
            gather(c, own).start()

        each(PARTS, arrive)

        def complete(c):
            gather(c, other).wait_recv()
            gather(c, own).wait_send()

        each(PARTS, complete)

    def norm(r):
        block = pl.ds(pl.multiple_of(r * 16, 16), 16)
        values = hid[block, :].astype(jnp.float32)
        scale = lax.rsqrt(jnp.mean(values * values, axis=-1, keepdims=True) + 1e-06)
        work[block, :] = (values * scale * gain_ref[...]).astype(work.dtype)

    each(rows // 16, norm)

    def project(j):
        pltpu.make_async_copy(
            wqkv_ref.at[0, pl.ds(0, WTILE)], wqkv_v.at[j], w_sem.at[j]
        ).wait()
        qkv[j] = lax.dot_general(
            work[...], wqkv_v[j], (((1,), (1,)), ((), ())), preferred_element_type=jnp.float32
        ).astype(qkv.dtype)

    each(tiles, project)
    pairs = WTILE // (2 * HD)

    def attend_pair(p):
        tile = p // pairs
        span = pl.ds(pl.multiple_of((p % pairs) * 2 * HD, 2 * HD), 2 * HD)
        queries = qkv[tile, :, span]
        keys = qkv[per + tile, :, span]
        values = qkv[2 * per + tile, :, span]
        allowed = row_doc_ref[...] == key_doc_ref[...]
        first = lax.broadcasted_iota(jnp.int32, (rows, 2 * HD), 1) < HD
        mixed = []
        for side in range(2):
            keep = first if side == 0 else jnp.logical_not(first)
            chosen = jnp.where(keep, queries.astype(jnp.float32), 0.0).astype(jnp.bfloat16)
            scores = lax.dot_general(
                chosen, keys, (((1,), (1,)), ((), ())), preferred_element_type=jnp.float32
            )
            weights = jnp.where(allowed, jnp.exp(scores), 0.0)
            shares = (weights / jnp.sum(weights, axis=-1, keepdims=True)).astype(jnp.bfloat16)
            mixed.append(jnp.dot(shares, values, preferred_element_type=jnp.float32))
        mix[:, pl.ds(pl.multiple_of(p * 2 * HD, 2 * HD), 2 * HD)] = jnp.where(
            first, mixed[0], mixed[1]
        ).astype(mix.dtype)

    each(per * pairs, attend_pair)

    def output(c):
        out_copy(c).wait()
        work[:, cols(c)] = jnp.dot(
            mix[...], wout_v[c], preferred_element_type=jnp.float32
        ).astype(work.dtype)
        reduce(c).start()

    each(PARTS, output)

    def total(c):
        reduce(c).wait_recv()
        return (
            hid[own, cols(c)].astype(jnp.float32)
            + work[own, cols(c)].astype(jnp.float32)
            + part[:, cols(c)].astype(jnp.float32)
        ).astype(hid.dtype)

    @pl.when(group < GROUPS - 1)
    def _():
        def finish(c):
            hid[own, cols(c)] = total(c)
            hand(c).start()

        each(PARTS, finish)

        def relay(c):
            back(c).wait_recv()

            @pl.when(group > 0)
            def _():
                back(c).start()

            spread(c, own).start()

        each(PARTS, relay)

    @pl.when(group == GROUPS - 1)
    def _():
        def finish(c):
            mem_ref[own, cols(c)] = total(c)
            back(c).start()
            spread(c, own).start()

        each(PARTS, finish)

    def drain(c):
        spread(c, other).wait_recv()
        spread(c, own).wait_send()
        reduce(c).wait_send()

        @pl.when(group < GROUPS - 1)
        def _():
            hand(c).wait_send()

        @pl.when(group > 0)
        def _():
            back(c).wait_send()

    each(PARTS, drain)


def encode(rows, sent, number, x, gain, row_doc, key_doc, wqkv, wout):
    total_rows, width = x.shape
    inner = wout.shape[0]
    tiles = 3 * (inner // WTILE)
    dma = pltpu.SemaphoreType.DMA
    vmem = pl.BlockSpec(memory_space=pltpu.VMEM)
    anywhere = pl.BlockSpec(memory_space=pl.ANY)
    return pl.pallas_call(
        functools.partial(encoder_kernel, sent),
        out_shape=jax.ShapeDtypeStruct((total_rows, width), jnp.bfloat16),
        in_specs=[anywhere, vmem, vmem, vmem, anywhere, anywhere],
        out_specs=vmem,
        scratch_shapes=[
            pltpu.VMEM((tiles, WTILE, width), jnp.bfloat16),
            pltpu.VMEM((PARTS, inner, width // PARTS), jnp.bfloat16),
            pltpu.VMEM((rows, width), jnp.bfloat16),
            pltpu.VMEM((rows, width), jnp.bfloat16),
            pltpu.VMEM((sent // 2, width), jnp.bfloat16),
            pltpu.VMEM((tiles, rows, WTILE), jnp.bfloat16),
            pltpu.VMEM((rows, inner), jnp.bfloat16),
            dma((tiles,)),
            dma((PARTS,)),
            dma,
        ]
        + [dma((PARTS,))] * 10,
        compiler_params=pltpu.CompilerParams(
            collective_id=number, has_side_effects=True, vmem_limit_bytes=67043328
        ),
        name=f"encoder_{sent}",
    )(x, gain, row_doc[:rows, None], key_doc[None, :rows], wqkv, wout)


def stream_kernel(
    sent,
    lengths_ref,
    x_ref,
    enc_gain_ref,
    dec_gain_ref,
    docid_ref,
    target_ref,
    wqkv_ref,
    wout_ref,
    wcross_ref,
    wclose_ref,
    whead_ref,
    logits_ref,
    token_ref,
    mean_ref,
    wqkv_v,
    wout_v,
    hid,
    work,
    part,
    acc,
    squares,
    mix,
    memory,
    cross_acc,
    query_acc,
    terms,
    landed,
    partial,
    crossed_over,
    summed,
    closing,
    scores,
    stats,
    stats_landed,
    loss_ref,
    loss_landed,
    twin_acc,
    w_sem,
    o_sem,
    x_sem,
    gs,
    gr,
    rs,
    rr,
    zs,
    zr,
    bs,
    br,
    ms,
    mr,
    k_sem,
    q_sem,
    c_sem,
    h_sem,
    ys,
    yr,
    ts,
    tr,
    us,
    ur,
    fs,
    fr,
    ss,
    sr,
    ls,
    lr,
    ds,
    dr,
    es,
    er,
):
    rows, width = hid.shape
    half = sent // 2
    chunks, tiles, tile_columns, columns = wqkv_v.shape
    per = tiles // 3
    micro_count, doc_count = lengths_ref.shape
    doc_total = micro_count * doc_count
    doc_span = x_ref.shape[0] // doc_total
    share_count, share, _ = docid_ref.shape
    every = share_count * share
    blocks = whead_ref.shape[1] // tile_columns
    section = lax.axis_index("section")
    count = lax.axis_size("section")
    rep = lax.axis_index("rep")
    rep_count = lax.axis_size("rep")
    group = section // 2
    lane = section % 2
    partner = section + 1 - 2 * lane
    ahead = lax.rem(section + 2, count)
    behind = lax.rem(section + count - 2, count)
    own = pl.ds(pl.multiple_of(lane * half, 16), half)
    other = pl.ds(pl.multiple_of((1 - lane) * half, 16), half)

    def cols(c):
        return pl.ds(pl.multiple_of(c * columns, columns), columns)

    def weight_copy(c):
        return pltpu.make_async_copy(wqkv_ref.at[:, :, cols(c)], wqkv_v.at[c], w_sem.at[c])

    def out_copy(c):
        return pltpu.make_async_copy(wout_ref.at[:, cols(c)], wout_v.at[c], o_sem.at[c])

    shared_chunks = chunks // 2
    core = rep % 2
    twin = rep + 1 - 2 * core
    kept = core * shared_chunks
    spare = (1 - core) * shared_chunks
    total_rows = x_ref.shape[0]

    def entry_copy(c):
        place = wqkv_v.at[spare, c, pl.ds(0, total_rows)]
        return pltpu.make_async_copy(x_ref.at[:, cols(c)], place, x_sem.at[c])

    def key_copy(c):
        return pltpu.make_async_copy(
            wcross_ref.at[pl.ds(1, 2), :, cols(c)], wqkv_v.at[c, pl.ds(0, 2)], k_sem.at[c]
        )

    def query_copy(c):
        return pltpu.make_async_copy(wcross_ref.at[0, :, cols(c)], wqkv_v.at[c, 2], q_sem.at[c])

    def close_copy(c):
        return pltpu.make_async_copy(wclose_ref.at[:, cols(c)], wqkv_v.at[c, 3], c_sem.at[c])

    def head_copy(i):
        c = i // blocks
        b = i % blocks
        return pltpu.make_async_copy(
            whead_ref.at[cols(c), pl.ds(pl.multiple_of(b * tile_columns, 128), tile_columns)],
            wqkv_v.at[c, 4 + b],
            h_sem.at[i],
        )

    def remote(src, dst, send, recv, device):
        return pltpu.make_async_remote_copy(
            src_ref=src,
            dst_ref=dst,
            send_sem=send,
            recv_sem=recv,
            device_id={"section": device},
            device_id_type=MESH,
        )

    pieces = chunks * HALVES
    piece = columns // HALVES

    def span_of(i):
        return pl.ds(pl.multiple_of(i * piece, piece), piece)

    def gather(i, block):
        place = hid.at[block, span_of(i)]
        return remote(place, place, gs.at[i], gr.at[i], partner)

    def reduce(i):
        place = span_of(i)
        return remote(work.at[other, place], part.at[:, place], rs.at[i], rr.at[i], partner)

    def hand(i):
        place = hid.at[own, span_of(i)]
        return remote(place, place, zs.at[i], zr.at[i], ahead)

    def back(i):
        place = memory.at[own, span_of(i)]
        return remote(place, place, bs.at[i], br.at[i], behind)

    def spread(i, block):
        place = memory.at[block, span_of(i)]
        return remote(place, place, ms.at[i], mr.at[i], partner)

    def peer(k):
        return lax.rem(section + k, count)

    def source_of(k):
        return lax.rem(section + count - k, count)

    stretch = width // TAIL
    lanes = count // GROUPS
    own_slot = lane * GROUPS + group

    def tail_cols(t):
        return pl.ds(pl.multiple_of(t * stretch, stretch), stretch)

    def group_after(k):
        return lax.rem(group + k, GROUPS)

    def group_before(k):
        return lax.rem(group + GROUPS - k, GROUPS)

    def swap(t):
        theirs = pl.ds((1 - lane) * GROUPS, GROUPS)
        place = tail_cols(t)
        return remote(
            terms.at[theirs, :, place], landed.at[:, :, place], ys.at[t], yr.at[t], partner
        )

    def scatter(t, k):
        place = tail_cols(t)
        i = k * TAIL + t
        return remote(
            partial.at[group_after(k), :, place],
            crossed_over.at[group, :, place],
            ts.at[i],
            tr.at[i],
            group_after(k) * lanes + lane,
        )

    def scattered(t, k):
        place = tail_cols(t)
        i = k * TAIL + t
        return remote(
            partial.at[group, :, place],
            crossed_over.at[group_before(k), :, place],
            ts.at[i],
            tr.at[i],
            group_after(k) * lanes + lane,
        )

    def collect(t, k, slot):
        place = closing.at[slot, :, tail_cols(t)]
        i = k * TAIL + t
        return remote(place, place, us.at[i], ur.at[i], group_after(k) * lanes + lane)

    def across(t, member, side):
        place = closing.at[side * GROUPS + member, :, tail_cols(t)]
        i = member * TAIL + t
        return remote(place, place, fs.at[i], fr.at[i], partner)

    def share_stats(k, slot):
        return remote(stats, stats_landed.at[slot], ss.at[k], sr.at[k], peer(k))

    def share_loss(k, slot):
        return pltpu.make_async_remote_copy(
            src_ref=loss_ref,
            dst_ref=loss_landed.at[slot],
            send_sem=ls.at[k],
            recv_sem=lr.at[k],
            device_id={"rep": lax.rem(rep + k, rep_count)},
            device_id_type=MESH,
        )

    def to_twin(src, dst, send, recv):
        return pltpu.make_async_remote_copy(
            src_ref=src,
            dst_ref=dst,
            send_sem=send,
            recv_sem=recv,
            device_id={"rep": twin},
            device_id_type=MESH,
        )

    def lend(i):
        source = work.at[:, cols(spare + i)]
        return to_twin(source, wqkv_v.at[kept + 1, i, pl.ds(0, rows)], ds.at[i], dr.at[i])

    def lent(i):
        source = work.at[:, cols(spare + i)]
        return to_twin(source, wqkv_v.at[spare + 1, i, pl.ds(0, rows)], ds.at[i], dr.at[i])

    def give_back(j):
        source = wqkv_v.at[spare + 2, j, pl.ds(0, rows)]
        return to_twin(source, wqkv_v.at[kept + 2, j, pl.ds(rows, rows)], es.at[j], er.at[j])

    def given_back(j):
        source = wqkv_v.at[spare + 2, j, pl.ds(0, rows)]
        return to_twin(source, wqkv_v.at[spare + 2, j, pl.ds(rows, rows)], es.at[j], er.at[j])

    def each(size, body):
        def step(i, carry):
            body(i)
            return carry

        lax.fori_loop(0, size, step, 0)

    @pl.when(group == 0)
    def _():
        for c in range(chunks):
            entry_copy(c).start()
        for i in range(shared_chunks):
            weight_copy(kept + i).start()

    @pl.when(group > 0)
    def _():
        for c in range(chunks):
            weight_copy(c).start()

    for c in range(chunks):
        out_copy(c).start()

    barrier = pltpu.get_barrier_semaphore()
    for k in range(1, count):
        pl.semaphore_signal(barrier, inc=1, device_id={"section": peer(k)}, device_id_type=MESH)
    for k in range(1, rep_count):
        pl.semaphore_signal(
            barrier, inc=1, device_id={"rep": lax.rem(rep + k, rep_count)}, device_id_type=MESH
        )
    pl.semaphore_wait(barrier, count + rep_count - 2)

    if sent < rows:
        hid[sent:, :] = jnp.zeros((rows - sent, width), hid.dtype)
        memory[sent:, :] = jnp.zeros((rows - sent, width), memory.dtype)
    acc[...] = jnp.zeros_like(acc)
    cross_acc[...] = jnp.zeros_like(cross_acc)
    query_acc[...] = jnp.zeros_like(query_acc)
    scores[...] = jnp.zeros_like(scores)
    squares[...] = jnp.zeros_like(squares)

    def placed(shape, dim):
        position = lax.broadcasted_iota(jnp.int32, shape, dim)
        owner = jnp.full(shape, -1, jnp.int32)
        source = jnp.full(shape, -1, jnp.int32)
        start = 0
        for d in range(doc_total):
            end = start + lengths_ref[d // doc_count, d % doc_count]
            inside = (position >= start) & (position < end)
            owner = jnp.where(inside, d, owner)
            source = jnp.where(inside, d * doc_span + position - start, source)
            start = end
        return owner, source

    row_doc, row_source = placed((rows, 1), 0)
    row_doc = jnp.maximum(row_doc, 0)
    key_doc, _ = placed((1, rows), 1)

    asked = target_ref.shape[1]
    wanted = jnp.concatenate(
        [jnp.broadcast_to(target_ref[m : m + 1, :], (asked, asked)) for m in range(micro_count)], 0
    )
    diagonal = lax.broadcasted_iota(jnp.int32, (every, asked), 0) % asked
    diagonal = diagonal == lax.broadcasted_iota(jnp.int32, (every, asked), 1)
    wanted = jnp.sum(
        jnp.where(diagonal, wanted.astype(jnp.float32), 0.0), axis=-1, keepdims=True
    )

    def prepare(c):
        values = hid[:, cols(c)].astype(jnp.float32)
        squares[...] += jnp.sum(values * values, axis=-1, keepdims=True)
        return (values * enc_gain_ref[pl.ds(group, 1), cols(c)]).astype(jnp.bfloat16)

    def project(c):
        scaled = prepare(c)
        for j in range(tiles):
            acc[j] += jnp.dot(scaled, wqkv_v[c, j], preferred_element_type=jnp.float32)

    @pl.when(group == 0)
    def _():
        twin_acc[...] = jnp.zeros_like(twin_acc)
        origin = lax.broadcasted_iota(jnp.int32, (rows, x_ref.shape[0]), 1)
        pick = (row_source == origin).astype(jnp.float32).astype(jnp.bfloat16)

        def pack(c):
            entry_copy(c).wait()
            hid[:, cols(c)] = jnp.dot(
                pick, wqkv_v[spare, c, :total_rows], preferred_element_type=jnp.float32
            ).astype(hid.dtype)
            work[:, cols(c)] = prepare(c)

        def pack_lent(i):
            pack(spare + i)
            lend(i).start()

        def pack_kept(i):
            pack(kept + i)

        each(shared_chunks, pack_lent)
        each(shared_chunks, pack_kept)

        def add(i, last):
            c = kept + i
            weight_copy(c).wait()
            lent(i).wait_recv()
            both = jnp.concatenate([work[:, cols(c)], wqkv_v[spare + 1, i, :rows]], 0)
            for j in range(tiles):
                product = lax.dot_general(
                    both, wqkv_v[c, j], (((1,), (1,)), ((), ())), preferred_element_type=jnp.float32
                )
                acc[j] += product[:rows]
                if last:
                    theirs = twin_acc[j] + product[rows:]
                    wqkv_v[spare + 2, j, :rows] = theirs.astype(wqkv_v.dtype)
                    give_back(j).start()
                else:
                    twin_acc[j] += product[rows:]

        each(shared_chunks - 1, lambda i: add(i, False))
        add(shared_chunks - 1, True)
        for j in range(tiles):
            given_back(j).wait_recv()
            acc[j] += wqkv_v[spare + 2, j, rows : 2 * rows].astype(jnp.float32)
        for i in range(shared_chunks):
            lend(i).wait_send()
        for j in range(tiles):
            give_back(j).wait_send()

    @pl.when(group > 0)
    def _():
        side = tile_columns // 2

        def turn(c):
            weight_copy(c).wait()

            def block(j):
                whole = wqkv_v[c, j]
                for a in range(2):
                    for b in range(2):
                        quarter = whole[a * side : (a + 1) * side, b * side : (b + 1) * side]
                        wqkv_v[c, j, b * side : (b + 1) * side, a * side : (a + 1) * side] = (
                            quarter.T
                        )

            each(tiles, block)

        each(chunks, turn)

        def step(i):
            @pl.when(i < chunks)
            def _():
                for u in range(HALVES):
                    hand(i * HALVES + u).wait_recv()
                    gather(i * HALVES + u, own).start()

            @pl.when(i >= AHEAD)
            def _():
                for u in range(HALVES):
                    gather((i - AHEAD) * HALVES + u, other).wait_recv()
                project(i - AHEAD)

        each(chunks + AHEAD, step)

        def complete(i):
            gather(i, own).wait_send()

        each(pieces, complete)

    def fetch(c):
        query_copy(c).start()
        key_copy(c).start()
        close_copy(c).start()

    each(chunks, fetch)

    def fetch_head(i):
        head_copy(i).start()

    each(chunks * blocks, fetch_head)

    def halves(size):
        return lax.broadcasted_iota(jnp.int32, (size, 2 * HD), 1) < HD

    def share_keys(queries, keys, allowed):
        first = halves(queries.shape[0])
        both = jnp.concatenate(
            [jnp.where(first, queries, 0.0), jnp.where(first, 0.0, queries)], 0
        ).astype(jnp.bfloat16)
        raw = lax.dot_general(
            both, keys, (((1,), (1,)), ((), ())), preferred_element_type=jnp.float32
        )
        weights = jnp.where(allowed, jnp.exp(raw), 0.0)
        shares = weights * (1.0 / jnp.sum(weights, axis=-1, keepdims=True))
        return shares.astype(jnp.bfloat16)

    def mix_values(shares, values):
        size = shares.shape[0] // 2
        mixed = jnp.dot(shares, values, preferred_element_type=jnp.float32)
        return jnp.where(halves(size), mixed[:size], mixed[size:])

    pairs = tile_columns // (2 * HD)
    scale = lax.rsqrt(squares[...] * (1.0 / width) + 1e-06)
    allowed = row_doc == key_doc
    allowed = jnp.concatenate([allowed, allowed], 0)

    def pair_of(member, p):
        at = slice(p % pairs * 2 * HD, (p % pairs + 1) * 2 * HD)
        return acc[member * per + p // pairs, :, at] * scale

    everyone = range(per * pairs)
    shared = [
        share_keys(pair_of(0, p), pair_of(1, p).astype(jnp.bfloat16), allowed) for p in everyone
    ]
    for p in everyone:
        mixed = mix_values(shared[p], pair_of(2, p).astype(jnp.bfloat16))
        mix[:, p * 2 * HD : (p + 1) * 2 * HD] = mixed.astype(mix.dtype)

    def output(c):
        out_copy(c).wait()
        work[:, cols(c)] = jnp.dot(
            mix[...], wout_v[c], preferred_element_type=jnp.float32
        ).astype(work.dtype)
        for u in range(HALVES):
            reduce(c * HALVES + u).start()

    each(chunks, output)

    def total(i):
        reduce(i).wait_recv()
        return (
            hid[own, span_of(i)].astype(jnp.float32)
            + work[own, span_of(i)].astype(jnp.float32)
            + part[:, span_of(i)].astype(jnp.float32)
        ).astype(hid.dtype)

    @pl.when(group < GROUPS - 1)
    def _():
        def finish(i):
            hid[own, span_of(i)] = total(i)
            hand(i).start()

        each(pieces, finish)

    @pl.when(group == GROUPS - 1)
    def _():
        def finish(i):
            memory[own, span_of(i)] = total(i)
            back(i).start()
            spread(i, own).start()

        each(pieces, finish)

    def docid_rows(c):
        return docid_ref[:, :, cols(c)].astype(jnp.float32).reshape(every, columns)

    def ask(c, sums):
        values = docid_rows(c)
        scaled = (values * dec_gain_ref[0:1, cols(c)]).astype(jnp.bfloat16)
        query_copy(c).wait()
        query_acc[...] += lax.dot_general(
            scaled, wqkv_v[c, 2], (((1,), (1,)), ((), ())), preferred_element_type=jnp.float32
        )
        return sums + jnp.sum(values * values, axis=-1, keepdims=True)

    query_squares = lax.fori_loop(0, chunks, ask, jnp.zeros((every, 1), jnp.float32))
    query_scale = lax.rsqrt(query_squares * (1.0 / width) + 1e-06)
    squares[...] = jnp.zeros_like(squares)

    def recall(c):
        for u in range(HALVES):
            spread(c * HALVES + u, other).wait_recv()
        key_copy(c).wait()
        values = memory[:, cols(c)].astype(jnp.float32)
        squares[...] += jnp.sum(values * values, axis=-1, keepdims=True)
        scaled = (values * enc_gain_ref[GROUPS : GROUPS + 1, cols(c)]).astype(jnp.bfloat16)
        for j in range(2):
            cross_acc[j] += lax.dot_general(
                scaled, wqkv_v[c, j], (((1,), (1,)), ((), ())), preferred_element_type=jnp.float32
            )

    def relay(i):
        @pl.when((i < chunks) & (group < GROUPS - 1))
        def _():
            for u in range(HALVES):
                back(i * HALVES + u).wait_recv()

                @pl.when(group > 0)
                def _():
                    back(i * HALVES + u).start()

                spread(i * HALVES + u, own).start()

        @pl.when(i >= AHEAD)
        def _():
            recall(i - AHEAD)

    each(chunks + AHEAD, relay)

    memory_scale = lax.rsqrt(squares[...] * (1.0 / width) + 1e-06)
    asking = lax.broadcasted_iota(jnp.int32, (every, 1), 0) // (every // doc_total)
    visible = asking == key_doc
    visible = jnp.concatenate([visible, visible], 0)
    spans = [slice(p * 2 * HD, (p + 1) * 2 * HD) for p in range(pairs)]
    shared = [
        share_keys(
            query_acc[:, at] * query_scale,
            (cross_acc[0, :, at] * memory_scale).astype(jnp.bfloat16),
            visible,
        )
        for at in spans
    ]
    crossed = [
        mix_values(shared[p], (cross_acc[1, :, spans[p]] * memory_scale).astype(jnp.bfloat16))
        for p in range(pairs)
    ]
    crossed = [value.astype(jnp.bfloat16) for value in crossed]
    crossed = jnp.concatenate(crossed, 1)

    ratio = chunks // TAIL

    def close(t):
        for u in range(ratio):
            c = t * ratio + u
            close_copy(c).wait()
            product = jnp.dot(crossed, wqkv_v[c, 3], preferred_element_type=jnp.float32)
            terms[:, :, cols(c)] = product.reshape(share_count, share, columns).astype(terms.dtype)
        swap(t).start()

    each(TAIL, close)
    mine = pl.ds(lane * GROUPS, GROUPS)

    def halfway(t):
        swap(t).wait_recv()
        both = terms[mine, :, tail_cols(t)].astype(jnp.float32)
        both = both + landed[:, :, tail_cols(t)].astype(jnp.float32)
        partial[:, :, tail_cols(t)] = both.astype(partial.dtype)
        for m in range(1, GROUPS):
            scatter(t, m).start()

    each(TAIL, halfway)

    def finished(t, squares_so_far):
        place = tail_cols(t)
        value = docid_ref[own_slot, :, place].astype(jnp.float32)
        value = value + partial[group, :, place].astype(jnp.float32)
        for m in range(1, GROUPS):
            scattered(t, m).wait_recv()
            value = value + crossed_over[group_before(m), :, place].astype(jnp.float32)
        summed[:, place] = value
        return squares_so_far + jnp.sum(value * value, axis=-1, keepdims=True)

    close_squares = lax.fori_loop(0, TAIL, finished, jnp.zeros((share, 1), jnp.float32))
    close_scale = lax.rsqrt(close_squares * (1.0 / width) + 1e-06)

    def publish(t):
        place = tail_cols(t)
        value = summed[:, place] * close_scale * dec_gain_ref[1:2, place]
        closing[own_slot, :, place] = value.astype(closing.dtype)
        for m in range(1, GROUPS):
            collect(t, m, own_slot).start()
        across(t, group, lane).start()

    each(TAIL, publish)

    def arrive_head(i):
        head_copy(i).wait()

    each(chunks * blocks, arrive_head)

    def forward(t):
        for m in range(1, GROUPS):
            member = group_before(m)
            collect(t, m, lane * GROUPS + member).wait_recv()
            across(t, member, lane).start()

    def head(t):
        for m in range(GROUPS):
            across(t, m, 1 - lane).wait_recv()
        for u in range(ratio):
            c = t * ratio + u
            final = closing[:, :, cols(c)].astype(jnp.float32).reshape(every, columns)
            final = final.astype(jnp.bfloat16)
            for b in range(blocks):
                scores[b] += jnp.dot(final, wqkv_v[c, 4 + b], preferred_element_type=jnp.float32)

    def spread_rows(t):
        @pl.when(t < TAIL)
        def _():
            forward(t)

        @pl.when(t >= 1)
        def _():
            head(t - 1)

    each(TAIL + 1, spread_rows)
    summed_exp = jnp.zeros((every, 1), jnp.float32)
    picked = jnp.zeros((every, 1), jnp.float32)
    for b in range(blocks):
        values = scores[b]
        entry = lax.broadcasted_iota(jnp.int32, (every, tile_columns), 1)
        entry = (entry + (section * blocks + b) * tile_columns).astype(jnp.float32)
        summed_exp = summed_exp + jnp.sum(jnp.exp(values), axis=-1, keepdims=True)
        picked = picked + jnp.sum(
            jnp.where(entry == wanted, values, 0.0), axis=-1, keepdims=True
        )
    place = lax.broadcasted_iota(jnp.int32, (every, 128), 1)
    packed = jnp.where(place == 0, summed_exp, jnp.where(place == 1, picked, 0.0))
    packed = jnp.concatenate([packed, jnp.zeros((128 - every, 128), jnp.float32)], 0)
    stats[...] = packed.T[:8]
    for k in range(1, count):
        share_stats(k, section).start()
    stats_landed[section] = stats[...]
    for b in range(blocks):
        for m in range(micro_count):
            logits_ref[m, :, b * tile_columns : (b + 1) * tile_columns] = scores[
                b, m * asked : (m + 1) * asked
            ].astype(logits_ref.dtype)
    for k in range(1, count):
        share_stats(k, source_of(k)).wait_recv()
    gathered = stats_landed[0]
    for k in range(1, count):
        gathered = gathered + stats_landed[k]
    here = lax.broadcasted_iota(jnp.int32, (1, 128), 1) < every
    token = jnp.log(jnp.where(here, gathered[0:1], 1.0)) - jnp.where(here, gathered[1:2], 0.0)
    loss_ref[...] = jnp.broadcast_to(token, loss_ref.shape)
    for k in range(1, rep_count):
        share_loss(k, rep).start()
    loss_landed[rep] = loss_ref[...]
    for m in range(micro_count):
        token_ref[m : m + 1, :] = token[:, m * asked : (m + 1) * asked]
    for k in range(1, rep_count):
        share_loss(k, lax.rem(rep + rep_count - k, rep_count)).wait_recv()
    losses = loss_landed[0]
    for k in range(1, rep_count):
        losses = losses + loss_landed[k]
    mean = jnp.sum(losses[0:1], axis=-1, keepdims=True) / (every * rep_count)
    mean_ref[...] = jnp.broadcast_to(mean, mean_ref.shape)

    def drain(i):
        spread(i, own).wait_send()
        reduce(i).wait_send()

        @pl.when(group < GROUPS - 1)
        def _():
            hand(i).wait_send()

        @pl.when(group > 0)
        def _():
            back(i).wait_send()

    each(pieces, drain)

    def drain_tail(t):
        swap(t).wait_send()
        for m in range(1, GROUPS):
            scatter(t, m).wait_send()
            collect(t, m, own_slot).wait_send()
        for m in range(GROUPS):
            across(t, m, lane).wait_send()

    each(TAIL, drain_tail)
    for k in range(1, count):
        share_stats(k, section).wait_send()
    for k in range(1, rep_count):
        share_loss(k, rep).wait_send()


def stream(sent, number, lengths, x, enc_gain, dec_gain, docid, targets, *weights):
    total_rows, width = x.shape
    wqkv, wout, wcross, wclose, whead = weights
    rows = total_rows // 2
    inner = wout.shape[0]
    tiles = 3 * (inner // WTILE)
    columns = width // CHUNKS
    share_count, share, _ = docid.shape
    every = share_count * share
    vocab = whead.shape[1]
    dma = pltpu.SemaphoreType.DMA
    vmem = pl.BlockSpec(memory_space=pltpu.VMEM)
    smem = pl.BlockSpec(memory_space=pltpu.SMEM)
    anywhere = pl.BlockSpec(memory_space=pl.ANY)
    small = (8, 128)
    bf16 = jnp.bfloat16
    f32 = jnp.float32
    reps = lax.axis_size("rep")
    logits, token_loss, mean = pl.pallas_call(
        functools.partial(stream_kernel, sent),
        out_shape=(
            jax.ShapeDtypeStruct(targets.shape + (vocab,), bf16),
            jax.ShapeDtypeStruct(targets.shape, f32),
            jax.ShapeDtypeStruct((1, 1), f32),
        ),
        in_specs=[smem, anywhere, vmem, vmem, vmem, vmem] + [anywhere] * 5,
        out_specs=(vmem, vmem, vmem),
        scratch_shapes=[
            pltpu.VMEM((CHUNKS, tiles, WTILE, columns), bf16),
            pltpu.VMEM((CHUNKS, inner, columns), bf16),
            pltpu.VMEM((rows, width), bf16),
            pltpu.VMEM((rows, width), bf16),
            pltpu.VMEM((sent // 2, width), bf16),
            pltpu.VMEM((tiles, rows, WTILE), f32),
            pltpu.VMEM((rows, 1), f32),
            pltpu.VMEM((rows, inner), bf16),
            pltpu.VMEM((rows, width), bf16),
            pltpu.VMEM((2, rows, WTILE), f32),
            pltpu.VMEM((every, WTILE), f32),
            pltpu.VMEM(docid.shape, bf16),
            pltpu.VMEM((GROUPS,) + docid.shape[1:], bf16),
            pltpu.VMEM((GROUPS,) + docid.shape[1:], bf16),
            pltpu.VMEM((GROUPS,) + docid.shape[1:], bf16),
            pltpu.VMEM(docid.shape[1:], f32),
            pltpu.VMEM(docid.shape, bf16),
            pltpu.VMEM((vocab // WTILE, every, WTILE), f32),
            pltpu.VMEM(small, f32),
            pltpu.VMEM((share_count,) + small, f32),
            pltpu.VMEM(small, f32),
            pltpu.VMEM((reps,) + small, f32),
            pltpu.VMEM((tiles, rows, WTILE), f32),
        ]
        + [dma((CHUNKS,))] * 3
        + [dma((CHUNKS * HALVES,))] * 10
        + [dma((CHUNKS,))] * 3
        + [dma((CHUNKS * (vocab // WTILE),))]
        + [dma((TAIL,))] * 2
        + [dma((GROUPS * TAIL,))] * 6
        + [dma((share_count,))] * 2
        + [dma((reps,))] * 2
        + [dma((CHUNKS // 2,))] * 2
        + [dma((tiles,))] * 2,
        compiler_params=pltpu.CompilerParams(
            collective_id=number, has_side_effects=True, vmem_limit_bytes=67043328
        ),
        name=f"stream_{sent}",
    )(
        lengths,
        x,
        enc_gain,
        dec_gain,
        docid,
        targets,
        wqkv.reshape(tiles, WTILE, width),
        wout,
        wcross,
        wclose,
        whead,
    )
    return logits, token_loss, mean[0, 0]


def largest_kernel(limits, lengths_ref, out_ref, mine, landed, send, recv):
    me = lax.axis_index("rep")
    count = lax.axis_size("rep")
    barrier = pltpu.get_barrier_semaphore()
    for k in range(1, count):
        pl.semaphore_signal(
            barrier, inc=1, device_id={"rep": lax.rem(me + k, count)}, device_id_type=MESH
        )
    live = 0
    for m in range(lengths_ref.shape[0]):
        for d in range(lengths_ref.shape[1]):
            live = live + lengths_ref[m, d]
    mine[...] = jnp.full(mine.shape, live, jnp.int32).astype(jnp.float32)
    pl.semaphore_wait(barrier, count - 1)

    def share(k, slot):
        return pltpu.make_async_remote_copy(
            src_ref=mine,
            dst_ref=landed.at[slot],
            send_sem=send.at[k],
            recv_sem=recv.at[k],
            device_id={"rep": lax.rem(me + k, count)},
            device_id_type=MESH,
        )

    for k in range(1, count):
        share(k, me).start()
    most = mine[...]
    for k in range(1, count):
        slot = lax.rem(me + count - k, count)
        share(k, slot).wait_recv()
        most = jnp.maximum(most, landed[slot])
    choice = jnp.zeros(most.shape, jnp.float32)
    for limit in limits:
        choice = choice + jnp.where(most > limit, 1.0, 0.0)
    out_ref[0, 0] = jnp.max(choice).astype(jnp.int32)
    for k in range(1, count):
        share(k, me).wait_send()


def branch_choice(limits, lengths):
    count = lax.axis_size("rep")
    dma = pltpu.SemaphoreType.DMA
    small = (8, 128)
    return pl.pallas_call(
        functools.partial(largest_kernel, limits),
        out_shape=jax.ShapeDtypeStruct((1, 1), jnp.int32),
        in_specs=[pl.BlockSpec(memory_space=pltpu.SMEM)],
        out_specs=pl.BlockSpec(memory_space=pltpu.SMEM),
        scratch_shapes=[pltpu.VMEM(small, jnp.float32), pltpu.VMEM((count,) + small, jnp.float32)]
        + [dma((count,))] * 2,
        compiler_params=pltpu.CompilerParams(collective_id=10, has_side_effects=True),
        name="largest",
    )(lengths)[0, 0]


def butterfly(value, axis, combine):
    for bit in range(lax.axis_size(axis).bit_length() - 1):
        value = combine(value, from_partner(value, axis, bit))
    return value


def greet(me, count):
    barrier = pltpu.get_barrier_semaphore()
    for k in range(1, count):
        pl.semaphore_signal(
            barrier, inc=1, device_id={"section": lax.rem(me + k, count)}, device_id_type=MESH
        )
    pl.semaphore_wait(barrier, count - 1)


def to_peer(src, dst, send, recv, peer):
    return pltpu.make_async_remote_copy(
        src_ref=src,
        dst_ref=dst,
        send_sem=send,
        recv_sem=recv,
        device_id={"section": peer},
        device_id_type=MESH,
    )


def closing_kernel(terms, residual, gain, out, landed, s1, r1, s2, r2):
    count = terms.shape[0]
    me = lax.axis_index("section")
    greet(me, count)

    def scatter(k, slot):
        peer = lax.rem(me + k, count)
        return to_peer(terms.at[peer], landed.at[slot], s1.at[k], r1.at[k], peer)

    def gather(k, slot):
        return to_peer(out.at[slot], out.at[slot], s2.at[k], r2.at[k], lax.rem(me + k, count))

    for k in range(1, count):
        scatter(k, me).start()
    total = residual[...] + terms[me].astype(jnp.float32)
    for k in range(1, count):
        slot = lax.rem(me + count - k, count)
        scatter(k, slot).wait_recv()
        total = total + landed[slot].astype(jnp.float32)
    scale = lax.rsqrt(jnp.mean(total * total, axis=-1, keepdims=True) + 1e-06)
    out[me] = (total * scale * gain[...]).astype(out.dtype)
    for k in range(1, count):
        gather(k, me).start()
    for k in range(1, count):
        gather(k, lax.rem(me + count - k, count)).wait_recv()
    for k in range(1, count):
        scatter(k, me).wait_send()
        gather(k, me).wait_send()


def closing_rows_of(terms, residual, gain):
    count = terms.shape[0]
    dma = pltpu.SemaphoreType.DMA
    vmem = pl.BlockSpec(memory_space=pltpu.VMEM)
    return pl.pallas_call(
        closing_kernel,
        out_shape=jax.ShapeDtypeStruct(terms.shape, jnp.bfloat16),
        in_specs=[vmem] * 3,
        out_specs=vmem,
        scratch_shapes=[pltpu.VMEM(terms.shape, jnp.bfloat16)] + [dma((count,))] * 4,
        compiler_params=pltpu.CompilerParams(collective_id=8, has_side_effects=True),
        name="closing",
    )(terms, residual, gain)


def sums_kernel(value, out, landed, send, recv):
    count = landed.shape[0]
    me = lax.axis_index("section")
    greet(me, count)

    def share(k, slot):
        return to_peer(value, landed.at[slot], send.at[k], recv.at[k], lax.rem(me + k, count))

    for k in range(1, count):
        share(k, me).start()
    landed[me] = value[...]
    for k in range(1, count):
        share(k, lax.rem(me + count - k, count)).wait_recv()
    total = landed[0]
    for k in range(1, count):
        total = total + landed[k]
    out[...] = total
    for k in range(1, count):
        share(k, me).wait_send()


def section_sum(value, count):
    dma = pltpu.SemaphoreType.DMA
    vmem = pl.BlockSpec(memory_space=pltpu.VMEM)
    return pl.pallas_call(
        sums_kernel,
        out_shape=jax.ShapeDtypeStruct(value.shape, value.dtype),
        in_specs=[vmem],
        out_specs=vmem,
        scratch_shapes=[pltpu.VMEM((count,) + value.shape, value.dtype)] + [dma((count,))] * 2,
        compiler_params=pltpu.CompilerParams(collective_id=9, has_side_effects=True),
        name="section_sum",
    )(value)


def large_shards(
    document_token_embedding,
    doc_lengths,
    docid_embed,
    docid_targets,
    enc_gain,
    dec_gain,
    w_enc_qkv,
    w_enc_out,
    cross_query_key_value_weight,
    w_cross_out,
    docid_head_weight,
):
    section_index = lax.axis_index("section")
    group_index = section_index // 2
    micro_count, row_count, width = document_token_embedding.shape
    doc_count = doc_lengths.shape[1]
    doc_span = row_count // doc_count
    all_rows = micro_count * row_count
    positions = jnp.arange(all_rows)
    row_doc = (positions // doc_span).astype(jnp.int32)
    live = (jnp.arange(doc_span)[None, :] < doc_lengths.reshape(-1)[:, None]).reshape(-1)
    key_doc = jnp.where(live, row_doc, -1).astype(jnp.int32)
    gain = lax.dynamic_slice_in_dim(enc_gain, group_index, 1, 0)
    hidden = encode(
        all_rows,
        all_rows,
        2,
        document_token_embedding.reshape(all_rows, width),
        gain,
        row_doc,
        key_doc,
        w_enc_qkv,
        w_enc_out,
    )
    memory = norm_rows(hidden, enc_gain[GROUPS]).astype(jnp.bfloat16)

    decoder_rows = docid_embed.shape[1]
    every = micro_count * decoder_rows
    docid_span = decoder_rows // doc_count
    decoder_doc = jnp.arange(every) // docid_span
    cross_heads = cross_query_key_value_weight.shape[1] // HD
    flat_docid = docid_embed.reshape(every, width)
    dec_normed = norm_rows(flat_docid, dec_gain[0]).astype(jnp.bfloat16)

    def project(values, weight):
        return (
            jnp.einsum("rd,cd->rc", values, weight, preferred_element_type=jnp.float32)
            .astype(jnp.bfloat16)
            .reshape(-1, cross_heads, HD)
        )

    queries = project(dec_normed, cross_query_key_value_weight[0])
    keys = project(memory, cross_query_key_value_weight[1])
    values = project(memory, cross_query_key_value_weight[2])
    allowed = decoder_doc[:, None] == key_doc[None, :]
    mixture = attend(queries, keys, values, allowed).reshape(every, -1)
    cross_terms = jnp.dot(mixture, w_cross_out, preferred_element_type=jnp.float32)
    section_count = lax.axis_size("section")
    share = every // section_count
    residual = lax.dynamic_slice_in_dim(flat_docid, section_index * share, share, 0)
    closing = closing_rows_of(
        cross_terms.astype(jnp.bfloat16).reshape(section_count, share, width),
        residual.astype(jnp.float32),
        dec_gain[1:2],
    ).reshape(every, width)
    scores_vocab = jnp.dot(closing, docid_head_weight, preferred_element_type=jnp.float32)
    vocab_local = docid_head_weight.shape[1]
    targets = docid_targets.reshape(-1)
    matches = targets[:, None] == section_index * vocab_local + jnp.arange(vocab_local)
    sums = jnp.stack(
        [
            jnp.sum(jnp.exp(scores_vocab), axis=-1),
            jnp.sum(jnp.where(matches, scores_vocab, 0.0), axis=-1),
        ]
    )
    padding = ((0, -sums.shape[0] % 8), (0, -sums.shape[1] % 128))
    sums = section_sum(jnp.pad(sums, padding), section_count)[:2, :every]
    token_loss = jnp.log(sums[0]) - sums[1]
    loss_sum = butterfly(jnp.sum(token_loss)[None], "rep", jnp.add)[0]
    mean_loss = loss_sum / (token_loss.size * lax.axis_size("rep"))
    logits = scores_vocab.astype(jnp.bfloat16).reshape(micro_count, decoder_rows, vocab_local)
    return (logits, token_loss.reshape(docid_targets.shape), mean_loss)


def fast_shards(
    document_token_embedding,
    doc_lengths,
    docid_embed,
    docid_targets,
    enc_gain,
    dec_gain,
    *weights,
):
    micro_count, row_count, width = document_token_embedding.shape
    sizes = (row_count * 3 // 4, row_count)
    section_count = lax.axis_size("section")
    choice = branch_choice(sizes, doc_lengths)

    def streamed(sent, number):
        def run():
            return stream(
                sent,
                number,
                doc_lengths,
                document_token_embedding.reshape(micro_count * row_count, width),
                enc_gain,
                dec_gain,
                docid_embed.reshape(section_count, -1, width),
                docid_targets,
                *weights,
            )
        return run

    def large():
        return large_shards(
            document_token_embedding,
            doc_lengths,
            docid_embed,
            docid_targets,
            enc_gain,
            dec_gain,
            *weights,
        )

    branches = [streamed(sent, number) for number, sent in enumerate(sizes)] + [large]
    return lax.switch(choice, branches)


def solution(mesh):
    in_specs = (
        P("rep", None, None),
        P("rep", None),
        P("rep", None, None),
        P("rep", None),
        P(),
        P(),
        P(None, "section", None),
        P("section", None),
        P(None, "section", None),
        P("section", None),
        P(None, "section"),
    )
    out_specs = (P("rep", None, "section"), P("rep", None), P())
    fits = mesh.shape["section"] == 2 * GROUPS and mesh.shape["rep"] % 2 == 0
    local = fast_shards if fits else shards
    return jax.shard_map(local, mesh=mesh, in_specs=in_specs, out_specs=out_specs, check_vma=False)
```

```python
import functools

import jax
import jax.numpy as jnp
from jax import lax
from jax.experimental import pallas as pl
from jax.experimental.pallas import tpu as pltpu
from jax.sharding import PartitionSpec as P

HD = 64
GROUPS = 4
WTILE = 512
PARTS = 4
CHUNKS = 8
AHEAD = 3
HALVES = 2
TAIL = 4
MESH = pl.DeviceIdType.MESH


def from_partner(block, axis, distance):
    count = lax.axis_size(axis)
    route = []
    for low in range(count):
        high = low | 1 << distance
        if high != low and high < count:
            route += [(low, high), (high, low)]
    return lax.ppermute(block, axis, route)


def from_behind(block, axis, distance):
    devices = range(lax.axis_size(axis))
    route = [(i - distance, i) for i in devices if i - distance in devices]
    return lax.ppermute(block, axis, route)


def passed_along(shard, axis, by):
    size = lax.axis_size(axis)
    return lax.ppermute(shard, axis, [(i, (i + by) % size) for i in range(size)])


def norm_rows(values, gain):
    values = values.astype(jnp.float32)
    scale = lax.rsqrt(jnp.mean(values * values, axis=-1, keepdims=True) + 1e-06)
    return values * scale * gain


def attend(queries, key_rows, values, allowed):
    scores = jnp.einsum("qhe,khe->hqk", queries, key_rows, preferred_element_type=jnp.float32)
    attention_weight_rows = jnp.where(allowed[None], jnp.exp(scores), 0.0)
    probabilities = (
        attention_weight_rows / jnp.sum(attention_weight_rows, axis=-1, keepdims=True)
    ).astype(jnp.bfloat16)
    mixture = jnp.einsum("hqk,khe->qhe", probabilities, values, preferred_element_type=jnp.float32)
    return mixture.astype(jnp.bfloat16)


def live_keys(lengths, key_doc, key_place):
    owners = jnp.arange(lengths.shape[0])
    matches = (key_doc[:, None] == owners[None, :]) & (key_place[:, None] < lengths[None, :])
    return jnp.any(matches, axis=1)


def lane_gather(own_rows, lane_bits, lane_index, concat_dim):
    for bit_number in range(lane_bits):
        partner = from_partner(own_rows, "section", bit_number)
        lower_half = lane_index // (1 << bit_number) % 2 == 0
        own_rows = jnp.where(
            lower_half,
            jnp.concatenate([own_rows, partner], concat_dim),
            jnp.concatenate([partner, own_rows], concat_dim),
        )
    return own_rows


def lane_reduce(totals, lane_bits, lane_index):
    for bit_number in reversed(range(lane_bits)):
        half_rows = totals.shape[0] // 2
        lower_half = lane_index // (1 << bit_number) % 2 == 0
        kept_rows = jnp.where(lower_half, totals[:half_rows], totals[half_rows:])
        outgoing = jnp.where(lower_half, totals[half_rows:], totals[:half_rows])
        totals = kept_rows + from_partner(outgoing, "section", bit_number)
    return totals


def relay_memory(encoder_memory, group_index, lane_count):
    encoder_memory = jnp.where(group_index == 0, encoder_memory, jnp.zeros_like(encoder_memory))
    for stride in (1, 2):
        encoder_memory = encoder_memory + from_behind(
            encoder_memory, "section", stride * lane_count
        )
    return encoder_memory


def shards(
    document_token_embedding,
    doc_lengths,
    docid_embed,
    docid_targets,
    enc_gain,
    dec_gain,
    w_enc_qkv,
    w_enc_out,
    cross_query_key_value_weight,
    w_cross_out,
    docid_head_weight,
):
    lane_count = lax.axis_size("section") // GROUPS
    lane_bits = lane_count.bit_length() - 1
    section_index = lax.axis_index("section")
    group_index = section_index // lane_count
    lane_index = section_index % lane_count
    micro_count, row_count, model_width = document_token_embedding.shape
    doc_count = doc_lengths.shape[1]
    doc_span = row_count // doc_count
    block_rows = row_count // lane_count
    local_heads = w_enc_qkv.shape[1] // HD
    positions = jnp.arange(row_count)
    key_doc = positions // doc_span
    key_place = positions % doc_span
    same_doc = key_doc[:, None] == key_doc[None, :]

    def partial_update(normed, lengths):
        allowed = same_doc & live_keys(lengths, key_doc, key_place)[None, :]
        projected = jnp.einsum(
            "rd,mcd->mrc", normed, w_enc_qkv, preferred_element_type=jnp.float32
        ).astype(jnp.bfloat16)
        projected = projected.reshape(3, row_count, local_heads, HD)
        mixture = attend(projected[0], projected[1], projected[2], allowed).reshape(row_count, -1)
        return jnp.dot(mixture, w_enc_out, preferred_element_type=jnp.float32)

    def section_step(step_index, loop_state):
        handed, encoder_memory = loop_state
        micro_index = step_index - group_index
        slot_index = jnp.clip(micro_index, 0, micro_count - 1)
        lengths = lax.dynamic_index_in_dim(doc_lengths, slot_index, 0, keepdims=False)
        layer_gain = lax.dynamic_index_in_dim(enc_gain, group_index, 0, keepdims=False)
        incoming = lax.dynamic_index_in_dim(
            document_token_embedding, jnp.minimum(step_index, micro_count - 1), 0, keepdims=False
        )
        incoming = lax.dynamic_slice_in_dim(incoming, lane_index * block_rows, block_rows, 0)
        current = jnp.where(group_index == 0, incoming, handed)
        normed = lane_gather(
            norm_rows(current, layer_gain).astype(jnp.bfloat16), lane_bits, lane_index, 0
        )
        summed = lane_reduce(partial_update(normed, lengths), lane_bits, lane_index)
        result = (current.astype(jnp.float32) + summed).astype(jnp.bfloat16)
        handed = passed_along(result, "section", lane_count)
        finished_index = step_index - (GROUPS - 1)
        finished_slot = jnp.clip(finished_index, 0, micro_count - 1)
        keeping = (group_index == 0) & (finished_index >= 0) & (finished_index < micro_count)
        stored = lax.dynamic_update_index_in_dim(encoder_memory, handed, finished_slot, 0)
        encoder_memory = jnp.where(keeping, stored, encoder_memory)
        return (handed, encoder_memory)

    handed = jnp.zeros((block_rows, model_width), jnp.bfloat16)
    encoder_memory = jnp.zeros((micro_count, block_rows, model_width), jnp.bfloat16)
    handed, encoder_memory = lax.fori_loop(
        0, micro_count + GROUPS - 1, section_step, (handed, encoder_memory)
    )
    encoder_memory = norm_rows(encoder_memory, enc_gain[GROUPS]).astype(jnp.bfloat16)
    encoder_memory = relay_memory(encoder_memory, group_index, lane_count)
    encoder_memory = lane_gather(encoder_memory, lane_bits, lane_index, 1)
    decoder_rows = docid_embed.shape[1]
    docid_span = decoder_rows // doc_count
    decoder_doc = jnp.arange(decoder_rows) // docid_span
    cross_heads = cross_query_key_value_weight.shape[1] // HD
    dec_normed = norm_rows(docid_embed, dec_gain[0]).astype(jnp.bfloat16)
    queries = jnp.einsum(
        "brd,cd->brc",
        dec_normed,
        cross_query_key_value_weight[0],
        preferred_element_type=jnp.float32,
    ).astype(jnp.bfloat16)
    memory_heads = jnp.einsum(
        "pye,qve->qpyv",
        encoder_memory,
        cross_query_key_value_weight[1:],
        preferred_element_type=jnp.float32,
    ).astype(jnp.bfloat16)

    def cross_one(sample_queries, sample_keys, sample_values, lengths):
        allowed = (decoder_doc[:, None] == key_doc[None, :]) & live_keys(
            lengths, key_doc, key_place
        )[None, :]
        return attend(sample_queries, sample_keys, sample_values, allowed)

    mixture = jax.vmap(cross_one)(
        queries.reshape(micro_count, decoder_rows, cross_heads, HD),
        memory_heads[0].reshape(micro_count, row_count, cross_heads, HD),
        memory_heads[1].reshape(micro_count, row_count, cross_heads, HD),
        doc_lengths,
    )
    cross_terms = jnp.einsum(
        "brc,cd->brd",
        mixture.reshape(micro_count, decoder_rows, -1),
        w_cross_out,
        preferred_element_type=jnp.float32,
    )
    cross_sum = lax.psum(cross_terms, "section")
    closing_rows = norm_rows(docid_embed.astype(jnp.float32) + cross_sum, dec_gain[1]).astype(
        jnp.bfloat16
    )
    scores_vocab = jnp.einsum(
        "brd,dv->brv", closing_rows, docid_head_weight, preferred_element_type=jnp.float32
    )
    vocab_local = docid_head_weight.shape[1]
    vocab_start = section_index * vocab_local
    matches = docid_targets[..., None] == vocab_start + jnp.arange(vocab_local)
    exponent_total, picked = lax.psum(
        (
            jnp.sum(jnp.exp(scores_vocab), axis=-1),
            jnp.sum(jnp.where(matches, scores_vocab, 0.0), axis=-1),
        ),
        "section",
    )
    token_loss = jnp.log(exponent_total) - picked
    mean_loss = lax.psum(jnp.sum(token_loss), "rep") / (token_loss.size * lax.axis_size("rep"))
    return (scores_vocab.astype(jnp.bfloat16), token_loss, mean_loss)


def encoder_kernel(
    sent,
    x_ref,
    gain_ref,
    row_doc_ref,
    key_doc_ref,
    wqkv_ref,
    wout_ref,
    mem_ref,
    wqkv_v,
    wout_v,
    hid,
    work,
    part,
    qkv,
    mix,
    w_sem,
    o_sem,
    x_sem,
    gs,
    gr,
    rs,
    rr,
    zs,
    zr,
    bs,
    br,
    ms,
    mr,
):
    rows, width = hid.shape
    half = sent // 2
    columns = width // PARTS
    tiles = wqkv_v.shape[0]
    per = tiles // 3
    section = lax.axis_index("section")
    count = lax.axis_size("section")
    group = section // 2
    lane = section % 2
    partner = section + 1 - 2 * lane
    ahead = lax.rem(section + 2, count)
    behind = lax.rem(section + count - 2, count)
    own = pl.ds(pl.multiple_of(lane * half, 16), half)
    other = pl.ds(pl.multiple_of((1 - lane) * half, 16), half)

    def cols(c):
        return pl.ds(pl.multiple_of(c * columns, columns), columns)

    def weight_copy(j):
        return pltpu.make_async_copy(
            wqkv_ref.at[j // per, pl.ds((j % per) * WTILE, WTILE)], wqkv_v.at[j], w_sem.at[j]
        )

    def out_copy(c):
        return pltpu.make_async_copy(wout_ref.at[:, cols(c)], wout_v.at[c], o_sem.at[c])

    def remote(src, dst, send, recv, device):
        return pltpu.make_async_remote_copy(
            src_ref=src,
            dst_ref=dst,
            send_sem=send,
            recv_sem=recv,
            device_id={"section": device},
            device_id_type=MESH,
        )

    def gather(c, block):
        return remote(hid.at[block, cols(c)], hid.at[block, cols(c)], gs.at[c], gr.at[c], partner)

    def reduce(c):
        return remote(work.at[other, cols(c)], part.at[:, cols(c)], rs.at[c], rr.at[c], partner)

    def hand(c):
        return remote(hid.at[own, cols(c)], hid.at[own, cols(c)], zs.at[c], zr.at[c], ahead)

    def back(c):
        return remote(mem_ref.at[own, cols(c)], mem_ref.at[own, cols(c)], bs.at[c], br.at[c], behind)

    def spread(c, block):
        return remote(
            mem_ref.at[block, cols(c)], mem_ref.at[block, cols(c)], ms.at[c], mr.at[c], partner
        )

    def each(size, body):
        def step(i, carry):
            body(i)
            return carry

        lax.fori_loop(0, size, step, 0)

    entry = pltpu.make_async_copy(x_ref.at[pl.ds(0, sent)], hid.at[pl.ds(0, sent)], x_sem)

    @pl.when(group == 0)
    def _():
        entry.start()

    for j in range(tiles):
        weight_copy(j).start()
    for c in range(PARTS):
        out_copy(c).start()

    barrier = pltpu.get_barrier_semaphore()
    for device in (partner, ahead, behind):
        pl.semaphore_signal(barrier, inc=1, device_id={"section": device}, device_id_type=MESH)
    pl.semaphore_wait(barrier, 3)

    if sent < rows:
        hid[sent:, :] = jnp.zeros((rows - sent, width), hid.dtype)
    if sent < mem_ref.shape[0]:
        mem_ref[sent:, :] = jnp.zeros((mem_ref.shape[0] - sent, width), mem_ref.dtype)

    @pl.when(group == 0)
    def _():
        entry.wait()

    @pl.when(group > 0)
    def _():
        def arrive(c):
            hand(c).wait_recv()
            gather(c, own).start()

        each(PARTS, arrive)

        def complete(c):
            gather(c, other).wait_recv()
            gather(c, own).wait_send()

        each(PARTS, complete)

    def norm(r):
        block = pl.ds(pl.multiple_of(r * 16, 16), 16)
        values = hid[block, :].astype(jnp.float32)
        scale = lax.rsqrt(jnp.mean(values * values, axis=-1, keepdims=True) + 1e-06)
        work[block, :] = (values * scale * gain_ref[...]).astype(work.dtype)

    each(rows // 16, norm)

    def project(j):
        pltpu.make_async_copy(
            wqkv_ref.at[0, pl.ds(0, WTILE)], wqkv_v.at[j], w_sem.at[j]
        ).wait()
        qkv[j] = lax.dot_general(
            work[...], wqkv_v[j], (((1,), (1,)), ((), ())), preferred_element_type=jnp.float32
        ).astype(qkv.dtype)

    each(tiles, project)
    pairs = WTILE // (2 * HD)

    def attend_pair(p):
        tile = p // pairs
        span = pl.ds(pl.multiple_of((p % pairs) * 2 * HD, 2 * HD), 2 * HD)
        queries = qkv[tile, :, span]
        keys = qkv[per + tile, :, span]
        values = qkv[2 * per + tile, :, span]
        allowed = row_doc_ref[...] == key_doc_ref[...]
        first = lax.broadcasted_iota(jnp.int32, (rows, 2 * HD), 1) < HD
        mixed = []
        for side in range(2):
            keep = first if side == 0 else jnp.logical_not(first)
            chosen = jnp.where(keep, queries.astype(jnp.float32), 0.0).astype(jnp.bfloat16)
            scores = lax.dot_general(
                chosen, keys, (((1,), (1,)), ((), ())), preferred_element_type=jnp.float32
            )
            weights = jnp.where(allowed, jnp.exp(scores), 0.0)
            shares = (weights / jnp.sum(weights, axis=-1, keepdims=True)).astype(jnp.bfloat16)
            mixed.append(jnp.dot(shares, values, preferred_element_type=jnp.float32))
        mix[:, pl.ds(pl.multiple_of(p * 2 * HD, 2 * HD), 2 * HD)] = jnp.where(
            first, mixed[0], mixed[1]
        ).astype(mix.dtype)

    each(per * pairs, attend_pair)

    def output(c):
        out_copy(c).wait()
        work[:, cols(c)] = jnp.dot(
            mix[...], wout_v[c], preferred_element_type=jnp.float32
        ).astype(work.dtype)
        reduce(c).start()

    each(PARTS, output)

    def total(c):
        reduce(c).wait_recv()
        return (
            hid[own, cols(c)].astype(jnp.float32)
            + work[own, cols(c)].astype(jnp.float32)
            + part[:, cols(c)].astype(jnp.float32)
        ).astype(hid.dtype)

    @pl.when(group < GROUPS - 1)
    def _():
        def finish(c):
            hid[own, cols(c)] = total(c)
            hand(c).start()

        each(PARTS, finish)

        def relay(c):
            back(c).wait_recv()

            @pl.when(group > 0)
            def _():
                back(c).start()

            spread(c, own).start()

        each(PARTS, relay)

    @pl.when(group == GROUPS - 1)
    def _():
        def finish(c):
            mem_ref[own, cols(c)] = total(c)
            back(c).start()
            spread(c, own).start()

        each(PARTS, finish)

    def drain(c):
        spread(c, other).wait_recv()
        spread(c, own).wait_send()
        reduce(c).wait_send()

        @pl.when(group < GROUPS - 1)
        def _():
            hand(c).wait_send()

        @pl.when(group > 0)
        def _():
            back(c).wait_send()

    each(PARTS, drain)


def encode(rows, sent, number, x, gain, row_doc, key_doc, wqkv, wout):
    total_rows, width = x.shape
    inner = wout.shape[0]
    tiles = 3 * (inner // WTILE)
    dma = pltpu.SemaphoreType.DMA
    vmem = pl.BlockSpec(memory_space=pltpu.VMEM)
    anywhere = pl.BlockSpec(memory_space=pl.ANY)
    return pl.pallas_call(
        functools.partial(encoder_kernel, sent),
        out_shape=jax.ShapeDtypeStruct((total_rows, width), jnp.bfloat16),
        in_specs=[anywhere, vmem, vmem, vmem, anywhere, anywhere],
        out_specs=vmem,
        scratch_shapes=[
            pltpu.VMEM((tiles, WTILE, width), jnp.bfloat16),
            pltpu.VMEM((PARTS, inner, width // PARTS), jnp.bfloat16),
            pltpu.VMEM((rows, width), jnp.bfloat16),
            pltpu.VMEM((rows, width), jnp.bfloat16),
            pltpu.VMEM((sent // 2, width), jnp.bfloat16),
            pltpu.VMEM((tiles, rows, WTILE), jnp.bfloat16),
            pltpu.VMEM((rows, inner), jnp.bfloat16),
            dma((tiles,)),
            dma((PARTS,)),
            dma,
        ]
        + [dma((PARTS,))] * 10,
        compiler_params=pltpu.CompilerParams(
            collective_id=number, has_side_effects=True, vmem_limit_bytes=67043328
        ),
        name=f"encoder_{sent}",
    )(x, gain, row_doc[:rows, None], key_doc[None, :rows], wqkv, wout)


def stream_kernel(
    sent,
    lengths_ref,
    x_ref,
    enc_gain_ref,
    dec_gain_ref,
    docid_ref,
    target_ref,
    wqkv_ref,
    wout_ref,
    wcross_ref,
    wclose_ref,
    whead_ref,
    logits_ref,
    token_ref,
    mean_ref,
    wqkv_v,
    wout_v,
    hid,
    work,
    part,
    acc,
    squares,
    mix,
    memory,
    cross_acc,
    query_acc,
    terms,
    landed,
    partial,
    crossed_over,
    summed,
    closing,
    scores,
    stats,
    stats_landed,
    loss_ref,
    loss_landed,
    twin_acc,
    w_sem,
    o_sem,
    x_sem,
    gs,
    gr,
    rs,
    rr,
    zs,
    zr,
    bs,
    br,
    ms,
    mr,
    k_sem,
    q_sem,
    c_sem,
    h_sem,
    ys,
    yr,
    ts,
    tr,
    us,
    ur,
    fs,
    fr,
    ss,
    sr,
    ls,
    lr,
    ds,
    dr,
    es,
    er,
):
    rows, width = hid.shape
    half = sent // 2
    chunks, tiles, tile_columns, columns = wqkv_v.shape
    per = tiles // 3
    micro_count, doc_count = lengths_ref.shape
    doc_total = micro_count * doc_count
    doc_span = x_ref.shape[0] // doc_total
    share_count, share, _ = docid_ref.shape
    every = share_count * share
    blocks = whead_ref.shape[1] // tile_columns
    section = lax.axis_index("section")
    count = lax.axis_size("section")
    rep = lax.axis_index("rep")
    rep_count = lax.axis_size("rep")
    group = section // 2
    lane = section % 2
    partner = section + 1 - 2 * lane
    ahead = lax.rem(section + 2, count)
    behind = lax.rem(section + count - 2, count)
    own = pl.ds(pl.multiple_of(lane * half, 16), half)
    other = pl.ds(pl.multiple_of((1 - lane) * half, 16), half)

    def cols(c):
        return pl.ds(pl.multiple_of(c * columns, columns), columns)

    def weight_copy(c):
        return pltpu.make_async_copy(wqkv_ref.at[:, :, cols(c)], wqkv_v.at[c], w_sem.at[c])

    def out_copy(c):
        return pltpu.make_async_copy(wout_ref.at[:, cols(c)], wout_v.at[c], o_sem.at[c])

    shared_chunks = chunks // 2
    core = rep % 2
    twin = rep + 1 - 2 * core
    kept = core * shared_chunks
    spare = (1 - core) * shared_chunks
    total_rows = x_ref.shape[0]

    def entry_copy(c):
        place = wqkv_v.at[spare, c, pl.ds(0, total_rows)]
        return pltpu.make_async_copy(x_ref.at[:, cols(c)], place, x_sem.at[c])

    def key_copy(c):
        return pltpu.make_async_copy(
            wcross_ref.at[pl.ds(1, 2), :, cols(c)], wqkv_v.at[c, pl.ds(0, 2)], k_sem.at[c]
        )

    def query_copy(c):
        return pltpu.make_async_copy(wcross_ref.at[0, :, cols(c)], wqkv_v.at[c, 2], q_sem.at[c])

    def close_copy(c):
        return pltpu.make_async_copy(wclose_ref.at[:, cols(c)], wqkv_v.at[c, 3], c_sem.at[c])

    def head_copy(i):
        c = i // blocks
        b = i % blocks
        return pltpu.make_async_copy(
            whead_ref.at[cols(c), pl.ds(pl.multiple_of(b * tile_columns, 128), tile_columns)],
            wqkv_v.at[c, 4 + b],
            h_sem.at[i],
        )

    def remote(src, dst, send, recv, device):
        return pltpu.make_async_remote_copy(
            src_ref=src,
            dst_ref=dst,
            send_sem=send,
            recv_sem=recv,
            device_id={"section": device},
            device_id_type=MESH,
        )

    pieces = chunks * HALVES
    piece = columns // HALVES

    def span_of(i):
        return pl.ds(pl.multiple_of(i * piece, piece), piece)

    def gather(i, block):
        place = hid.at[block, span_of(i)]
        return remote(place, place, gs.at[i], gr.at[i], partner)

    def reduce(i):
        place = span_of(i)
        return remote(work.at[other, place], part.at[:, place], rs.at[i], rr.at[i], partner)

    def hand(i):
        place = hid.at[own, span_of(i)]
        return remote(place, place, zs.at[i], zr.at[i], ahead)

    def back(i):
        place = memory.at[own, span_of(i)]
        return remote(place, place, bs.at[i], br.at[i], behind)

    def spread(i, block):
        place = memory.at[block, span_of(i)]
        return remote(place, place, ms.at[i], mr.at[i], partner)

    def peer(k):
        return lax.rem(section + k, count)

    def source_of(k):
        return lax.rem(section + count - k, count)

    stretch = width // TAIL
    lanes = count // GROUPS
    own_slot = lane * GROUPS + group

    def tail_cols(t):
        return pl.ds(pl.multiple_of(t * stretch, stretch), stretch)

    def group_after(k):
        return lax.rem(group + k, GROUPS)

    def group_before(k):
        return lax.rem(group + GROUPS - k, GROUPS)

    def swap(t):
        theirs = pl.ds((1 - lane) * GROUPS, GROUPS)
        place = tail_cols(t)
        return remote(
            terms.at[theirs, :, place], landed.at[:, :, place], ys.at[t], yr.at[t], partner
        )

    def scatter(t, k):
        place = tail_cols(t)
        i = k * TAIL + t
        return remote(
            partial.at[group_after(k), :, place],
            crossed_over.at[group, :, place],
            ts.at[i],
            tr.at[i],
            group_after(k) * lanes + lane,
        )

    def scattered(t, k):
        place = tail_cols(t)
        i = k * TAIL + t
        return remote(
            partial.at[group, :, place],
            crossed_over.at[group_before(k), :, place],
            ts.at[i],
            tr.at[i],
            group_after(k) * lanes + lane,
        )

    def collect(t, k, slot):
        place = closing.at[slot, :, tail_cols(t)]
        i = k * TAIL + t
        return remote(place, place, us.at[i], ur.at[i], group_after(k) * lanes + lane)

    def across(t, member, side):
        place = closing.at[side * GROUPS + member, :, tail_cols(t)]
        i = member * TAIL + t
        return remote(place, place, fs.at[i], fr.at[i], partner)

    def share_stats(k, slot):
        return remote(stats, stats_landed.at[slot], ss.at[k], sr.at[k], peer(k))

    def share_loss(k, slot):
        return pltpu.make_async_remote_copy(
            src_ref=loss_ref,
            dst_ref=loss_landed.at[slot],
            send_sem=ls.at[k],
            recv_sem=lr.at[k],
            device_id={"rep": lax.rem(rep + k, rep_count)},
            device_id_type=MESH,
        )

    def to_twin(src, dst, send, recv):
        return pltpu.make_async_remote_copy(
            src_ref=src,
            dst_ref=dst,
            send_sem=send,
            recv_sem=recv,
            device_id={"rep": twin},
            device_id_type=MESH,
        )

    def lend(i):
        source = work.at[:, cols(spare + i)]
        return to_twin(source, wqkv_v.at[kept + 1, i, pl.ds(0, rows)], ds.at[i], dr.at[i])

    def lent(i):
        source = work.at[:, cols(spare + i)]
        return to_twin(source, wqkv_v.at[spare + 1, i, pl.ds(0, rows)], ds.at[i], dr.at[i])

    def give_back(j):
        source = wqkv_v.at[spare + 2, j, pl.ds(0, rows)]
        return to_twin(source, wqkv_v.at[kept + 2, j, pl.ds(rows, rows)], es.at[j], er.at[j])

    def given_back(j):
        source = wqkv_v.at[spare + 2, j, pl.ds(0, rows)]
        return to_twin(source, wqkv_v.at[spare + 2, j, pl.ds(rows, rows)], es.at[j], er.at[j])

    def each(size, body):
        def step(i, carry):
            body(i)
            return carry

        lax.fori_loop(0, size, step, 0)

    @pl.when(group == 0)
    def _():
        for c in range(chunks):
            entry_copy(c).start()
        for i in range(shared_chunks):
            weight_copy(kept + i).start()

    @pl.when(group > 0)
    def _():
        for c in range(chunks):
            weight_copy(c).start()

    for c in range(chunks):
        out_copy(c).start()

    barrier = pltpu.get_barrier_semaphore()
    for k in range(1, count):
        pl.semaphore_signal(barrier, inc=1, device_id={"section": peer(k)}, device_id_type=MESH)
    for k in range(1, rep_count):
        pl.semaphore_signal(
            barrier, inc=1, device_id={"rep": lax.rem(rep + k, rep_count)}, device_id_type=MESH
        )
    pl.semaphore_wait(barrier, count + rep_count - 2)

    if sent < rows:
        hid[sent:, :] = jnp.zeros((rows - sent, width), hid.dtype)
        memory[sent:, :] = jnp.zeros((rows - sent, width), memory.dtype)
    acc[...] = jnp.zeros_like(acc)
    cross_acc[...] = jnp.zeros_like(cross_acc)
    query_acc[...] = jnp.zeros_like(query_acc)
    scores[...] = jnp.zeros_like(scores)
    squares[...] = jnp.zeros_like(squares)

    def placed(shape, dim):
        position = lax.broadcasted_iota(jnp.int32, shape, dim)
        owner = jnp.full(shape, -1, jnp.int32)
        source = jnp.full(shape, -1, jnp.int32)
        start = 0
        for d in range(doc_total):
            end = start + lengths_ref[d // doc_count, d % doc_count]
            inside = (position >= start) & (position < end)
            owner = jnp.where(inside, d, owner)
            source = jnp.where(inside, d * doc_span + position - start, source)
            start = end
        return owner, source

    row_doc, row_source = placed((rows, 1), 0)
    row_doc = jnp.maximum(row_doc, 0)
    key_doc, _ = placed((1, rows), 1)

    asked = target_ref.shape[1]
    wanted = jnp.concatenate(
        [jnp.broadcast_to(target_ref[m : m + 1, :], (asked, asked)) for m in range(micro_count)], 0
    )
    diagonal = lax.broadcasted_iota(jnp.int32, (every, asked), 0) % asked
    diagonal = diagonal == lax.broadcasted_iota(jnp.int32, (every, asked), 1)
    wanted = jnp.sum(
        jnp.where(diagonal, wanted.astype(jnp.float32), 0.0), axis=-1, keepdims=True
    )

    def prepare(c):
        values = hid[:, cols(c)].astype(jnp.float32)
        squares[...] += jnp.sum(values * values, axis=-1, keepdims=True)
        return (values * enc_gain_ref[pl.ds(group, 1), cols(c)]).astype(jnp.bfloat16)

    def project(c):
        scaled = prepare(c)
        for j in range(tiles):
            acc[j] += jnp.dot(scaled, wqkv_v[c, j], preferred_element_type=jnp.float32)

    @pl.when(group == 0)
    def _():
        twin_acc[...] = jnp.zeros_like(twin_acc)
        origin = lax.broadcasted_iota(jnp.int32, (rows, x_ref.shape[0]), 1)
        pick = (row_source == origin).astype(jnp.float32).astype(jnp.bfloat16)

        def pack(c):
            entry_copy(c).wait()
            hid[:, cols(c)] = jnp.dot(
                pick, wqkv_v[spare, c, :total_rows], preferred_element_type=jnp.float32
            ).astype(hid.dtype)
            work[:, cols(c)] = prepare(c)

        def pack_lent(i):
            pack(spare + i)
            lend(i).start()

        def pack_kept(i):
            pack(kept + i)

        each(shared_chunks, pack_lent)
        each(shared_chunks, pack_kept)

        def add(i, last):
            c = kept + i
            weight_copy(c).wait()
            lent(i).wait_recv()
            both = jnp.concatenate([work[:, cols(c)], wqkv_v[spare + 1, i, :rows]], 0)
            for j in range(tiles):
                product = lax.dot_general(
                    both, wqkv_v[c, j], (((1,), (1,)), ((), ())), preferred_element_type=jnp.float32
                )
                acc[j] += product[:rows]
                if last:
                    theirs = twin_acc[j] + product[rows:]
                    wqkv_v[spare + 2, j, :rows] = theirs.astype(wqkv_v.dtype)
                    give_back(j).start()
                else:
                    twin_acc[j] += product[rows:]

        each(shared_chunks - 1, lambda i: add(i, False))
        add(shared_chunks - 1, True)
        for j in range(tiles):
            given_back(j).wait_recv()
            acc[j] += wqkv_v[spare + 2, j, rows : 2 * rows].astype(jnp.float32)
        for i in range(shared_chunks):
            lend(i).wait_send()

    @pl.when(group > 0)
    def _():
        side = tile_columns // 2

        def turn(c):
            weight_copy(c).wait()

            def block(j):
                whole = wqkv_v[c, j]
                for a in range(2):
                    for b in range(2):
                        quarter = whole[a * side : (a + 1) * side, b * side : (b + 1) * side]
                        wqkv_v[c, j, b * side : (b + 1) * side, a * side : (a + 1) * side] = (
                            quarter.T
                        )

            each(tiles, block)

        each(chunks, turn)

        def step(i):
            @pl.when(i < chunks)
            def _():
                for u in range(HALVES):
                    hand(i * HALVES + u).wait_recv()
                    gather(i * HALVES + u, own).start()

            @pl.when(i >= AHEAD)
            def _():
                for u in range(HALVES):
                    gather((i - AHEAD) * HALVES + u, other).wait_recv()
                project(i - AHEAD)

        each(chunks + AHEAD, step)

    def halves(size):
        return lax.broadcasted_iota(jnp.int32, (size, 2 * HD), 1) < HD

    def share_keys(queries, keys, allowed):
        first = halves(queries.shape[0])
        both = jnp.concatenate(
            [jnp.where(first, queries, 0.0), jnp.where(first, 0.0, queries)], 0
        ).astype(jnp.bfloat16)
        raw = lax.dot_general(
            both, keys, (((1,), (1,)), ((), ())), preferred_element_type=jnp.float32
        )
        weights = jnp.where(allowed, jnp.exp(raw), 0.0)
        shares = weights * (1.0 / jnp.sum(weights, axis=-1, keepdims=True))
        return shares.astype(jnp.bfloat16)

    def mix_values(shares, values):
        size = shares.shape[0] // 2
        mixed = jnp.dot(shares, values, preferred_element_type=jnp.float32)
        return jnp.where(halves(size), mixed[:size], mixed[size:])

    pairs = tile_columns // (2 * HD)
    scale = lax.rsqrt(squares[...] * (1.0 / width) + 1e-06)
    allowed = row_doc == key_doc
    allowed = jnp.concatenate([allowed, allowed], 0)

    def pair_of(member, p):
        at = slice(p % pairs * 2 * HD, (p % pairs + 1) * 2 * HD)
        return acc[member * per + p // pairs, :, at] * scale

    everyone = range(per * pairs)
    shared = [
        share_keys(pair_of(0, p), pair_of(1, p).astype(jnp.bfloat16), allowed) for p in everyone
    ]
    for p in everyone:
        mixed = mix_values(shared[p], pair_of(2, p).astype(jnp.bfloat16))
        mix[:, p * 2 * HD : (p + 1) * 2 * HD] = mixed.astype(mix.dtype)

    def output(c):
        out_copy(c).wait()
        work[:, cols(c)] = jnp.dot(
            mix[...], wout_v[c], preferred_element_type=jnp.float32
        ).astype(work.dtype)
        for u in range(HALVES):
            reduce(c * HALVES + u).start()

    each(chunks, output)

    @pl.when(group == 0)
    def _():
        def returned(j):
            give_back(j).wait_send()

        each(tiles, returned)

    @pl.when(group > 0)
    def _():
        def complete(i):
            gather(i, own).wait_send()

        each(pieces, complete)

    def total(i):
        reduce(i).wait_recv()
        return (
            hid[own, span_of(i)].astype(jnp.float32)
            + work[own, span_of(i)].astype(jnp.float32)
            + part[:, span_of(i)].astype(jnp.float32)
        ).astype(hid.dtype)

    @pl.when(group < GROUPS - 1)
    def _():
        def finish(i):
            hid[own, span_of(i)] = total(i)
            hand(i).start()

        each(pieces, finish)

    @pl.when(group == GROUPS - 1)
    def _():
        def finish(i):
            memory[own, span_of(i)] = total(i)
            back(i).start()
            spread(i, own).start()

        each(pieces, finish)

    def fetch(c):
        query_copy(c).start()
        key_copy(c).start()
        close_copy(c).start()

    each(chunks, fetch)

    def fetch_head(i):
        head_copy(i).start()

    each(chunks * blocks, fetch_head)

    def docid_rows(c):
        return docid_ref[:, :, cols(c)].astype(jnp.float32).reshape(every, columns)

    def ask(c, sums):
        values = docid_rows(c)
        scaled = (values * dec_gain_ref[0:1, cols(c)]).astype(jnp.bfloat16)
        query_copy(c).wait()
        query_acc[...] += lax.dot_general(
            scaled, wqkv_v[c, 2], (((1,), (1,)), ((), ())), preferred_element_type=jnp.float32
        )
        return sums + jnp.sum(values * values, axis=-1, keepdims=True)

    query_squares = lax.fori_loop(0, chunks, ask, jnp.zeros((every, 1), jnp.float32))
    query_scale = lax.rsqrt(query_squares * (1.0 / width) + 1e-06)
    squares[...] = jnp.zeros_like(squares)

    def recall(c):
        for u in range(HALVES):
            spread(c * HALVES + u, other).wait_recv()
        key_copy(c).wait()
        values = memory[:, cols(c)].astype(jnp.float32)
        squares[...] += jnp.sum(values * values, axis=-1, keepdims=True)
        scaled = (values * enc_gain_ref[GROUPS : GROUPS + 1, cols(c)]).astype(jnp.bfloat16)
        for j in range(2):
            cross_acc[j] += lax.dot_general(
                scaled, wqkv_v[c, j], (((1,), (1,)), ((), ())), preferred_element_type=jnp.float32
            )

    def relay(i):
        @pl.when((i < chunks) & (group < GROUPS - 1))
        def _():
            for u in range(HALVES):
                back(i * HALVES + u).wait_recv()

                @pl.when(group > 0)
                def _():
                    back(i * HALVES + u).start()

                spread(i * HALVES + u, own).start()

        @pl.when(i >= AHEAD)
        def _():
            recall(i - AHEAD)

    each(chunks + AHEAD, relay)

    memory_scale = lax.rsqrt(squares[...] * (1.0 / width) + 1e-06)
    asking = lax.broadcasted_iota(jnp.int32, (every, 1), 0) // (every // doc_total)
    visible = asking == key_doc
    visible = jnp.concatenate([visible, visible], 0)
    spans = [slice(p * 2 * HD, (p + 1) * 2 * HD) for p in range(pairs)]
    shared = [
        share_keys(
            query_acc[:, at] * query_scale,
            (cross_acc[0, :, at] * memory_scale).astype(jnp.bfloat16),
            visible,
        )
        for at in spans
    ]
    crossed = [
        mix_values(shared[p], (cross_acc[1, :, spans[p]] * memory_scale).astype(jnp.bfloat16))
        for p in range(pairs)
    ]
    crossed = [value.astype(jnp.bfloat16) for value in crossed]
    crossed = jnp.concatenate(crossed, 1)

    ratio = chunks // TAIL

    def close(t):
        for u in range(ratio):
            c = t * ratio + u
            close_copy(c).wait()
            product = jnp.dot(crossed, wqkv_v[c, 3], preferred_element_type=jnp.float32)
            terms[:, :, cols(c)] = product.reshape(share_count, share, columns).astype(terms.dtype)
        swap(t).start()

    each(TAIL, close)
    mine = pl.ds(lane * GROUPS, GROUPS)

    def halfway(t):
        swap(t).wait_recv()
        both = terms[mine, :, tail_cols(t)].astype(jnp.float32)
        both = both + landed[:, :, tail_cols(t)].astype(jnp.float32)
        partial[:, :, tail_cols(t)] = both.astype(partial.dtype)
        for m in range(1, GROUPS):
            scatter(t, m).start()

    each(TAIL, halfway)

    def finished(t, squares_so_far):
        place = tail_cols(t)
        value = docid_ref[own_slot, :, place].astype(jnp.float32)
        value = value + partial[group, :, place].astype(jnp.float32)
        for m in range(1, GROUPS):
            scattered(t, m).wait_recv()
            value = value + crossed_over[group_before(m), :, place].astype(jnp.float32)
        summed[:, place] = value
        return squares_so_far + jnp.sum(value * value, axis=-1, keepdims=True)

    close_squares = lax.fori_loop(0, TAIL, finished, jnp.zeros((share, 1), jnp.float32))
    close_scale = lax.rsqrt(close_squares * (1.0 / width) + 1e-06)

    def publish(t):
        place = tail_cols(t)
        value = summed[:, place] * close_scale * dec_gain_ref[1:2, place]
        closing[own_slot, :, place] = value.astype(closing.dtype)
        for m in range(1, GROUPS):
            collect(t, m, own_slot).start()
        across(t, group, lane).start()

    each(TAIL, publish)

    def arrive_head(i):
        head_copy(i).wait()

    each(chunks * blocks, arrive_head)

    def forward(t):
        for m in range(1, GROUPS):
            member = group_before(m)
            collect(t, m, lane * GROUPS + member).wait_recv()
            across(t, member, lane).start()

    def head(t):
        for m in range(GROUPS):
            across(t, m, 1 - lane).wait_recv()
        for u in range(ratio):
            c = t * ratio + u
            final = closing[:, :, cols(c)].astype(jnp.float32).reshape(every, columns)
            final = final.astype(jnp.bfloat16)
            for b in range(blocks):
                scores[b] += jnp.dot(final, wqkv_v[c, 4 + b], preferred_element_type=jnp.float32)

    def spread_rows(t):
        @pl.when(t < TAIL)
        def _():
            forward(t)

        @pl.when(t >= 1)
        def _():
            head(t - 1)

    each(TAIL + 1, spread_rows)
    summed_exp = jnp.zeros((every, 1), jnp.float32)
    picked = jnp.zeros((every, 1), jnp.float32)
    for b in range(blocks):
        values = scores[b]
        entry = lax.broadcasted_iota(jnp.int32, (every, tile_columns), 1)
        entry = (entry + (section * blocks + b) * tile_columns).astype(jnp.float32)
        summed_exp = summed_exp + jnp.sum(jnp.exp(values), axis=-1, keepdims=True)
        picked = picked + jnp.sum(
            jnp.where(entry == wanted, values, 0.0), axis=-1, keepdims=True
        )
    place = lax.broadcasted_iota(jnp.int32, (every, 128), 1)
    packed = jnp.where(place == 0, summed_exp, jnp.where(place == 1, picked, 0.0))
    packed = jnp.concatenate([packed, jnp.zeros((128 - every, 128), jnp.float32)], 0)
    stats[...] = packed.T[:8]
    for k in range(1, count):
        share_stats(k, section).start()
    stats_landed[section] = stats[...]
    for b in range(blocks):
        for m in range(micro_count):
            logits_ref[m, :, b * tile_columns : (b + 1) * tile_columns] = scores[
                b, m * asked : (m + 1) * asked
            ].astype(logits_ref.dtype)
    for k in range(1, count):
        share_stats(k, source_of(k)).wait_recv()
    gathered = stats_landed[0]
    for k in range(1, count):
        gathered = gathered + stats_landed[k]
    here = lax.broadcasted_iota(jnp.int32, (1, 128), 1) < every
    token = jnp.log(jnp.where(here, gathered[0:1], 1.0)) - jnp.where(here, gathered[1:2], 0.0)
    loss_ref[...] = jnp.broadcast_to(token, loss_ref.shape)
    for k in range(1, rep_count):
        share_loss(k, rep).start()
    loss_landed[rep] = loss_ref[...]
    for m in range(micro_count):
        token_ref[m : m + 1, :] = token[:, m * asked : (m + 1) * asked]
    for k in range(1, rep_count):
        share_loss(k, lax.rem(rep + rep_count - k, rep_count)).wait_recv()
    losses = loss_landed[0]
    for k in range(1, rep_count):
        losses = losses + loss_landed[k]
    mean = jnp.sum(losses[0:1], axis=-1, keepdims=True) / (every * rep_count)
    mean_ref[...] = jnp.broadcast_to(mean, mean_ref.shape)

    def drain(i):
        spread(i, own).wait_send()
        reduce(i).wait_send()

        @pl.when(group < GROUPS - 1)
        def _():
            hand(i).wait_send()

        @pl.when(group > 0)
        def _():
            back(i).wait_send()

    each(pieces, drain)

    def drain_tail(t):
        swap(t).wait_send()
        for m in range(1, GROUPS):
            scatter(t, m).wait_send()
            collect(t, m, own_slot).wait_send()
        for m in range(GROUPS):
            across(t, m, lane).wait_send()

    each(TAIL, drain_tail)
    for k in range(1, count):
        share_stats(k, section).wait_send()
    for k in range(1, rep_count):
        share_loss(k, rep).wait_send()


def stream(sent, number, lengths, x, enc_gain, dec_gain, docid, targets, *weights):
    total_rows, width = x.shape
    wqkv, wout, wcross, wclose, whead = weights
    rows = total_rows // 2
    inner = wout.shape[0]
    tiles = 3 * (inner // WTILE)
    columns = width // CHUNKS
    share_count, share, _ = docid.shape
    every = share_count * share
    vocab = whead.shape[1]
    dma = pltpu.SemaphoreType.DMA
    vmem = pl.BlockSpec(memory_space=pltpu.VMEM)
    smem = pl.BlockSpec(memory_space=pltpu.SMEM)
    anywhere = pl.BlockSpec(memory_space=pl.ANY)
    small = (8, 128)
    bf16 = jnp.bfloat16
    f32 = jnp.float32
    reps = lax.axis_size("rep")
    logits, token_loss, mean = pl.pallas_call(
        functools.partial(stream_kernel, sent),
        out_shape=(
            jax.ShapeDtypeStruct(targets.shape + (vocab,), bf16),
            jax.ShapeDtypeStruct(targets.shape, f32),
            jax.ShapeDtypeStruct((1, 1), f32),
        ),
        in_specs=[smem, anywhere, vmem, vmem, vmem, vmem] + [anywhere] * 5,
        out_specs=(vmem, vmem, vmem),
        scratch_shapes=[
            pltpu.VMEM((CHUNKS, tiles, WTILE, columns), bf16),
            pltpu.VMEM((CHUNKS, inner, columns), bf16),
            pltpu.VMEM((rows, width), bf16),
            pltpu.VMEM((rows, width), bf16),
            pltpu.VMEM((sent // 2, width), bf16),
            pltpu.VMEM((tiles, rows, WTILE), f32),
            pltpu.VMEM((rows, 1), f32),
            pltpu.VMEM((rows, inner), bf16),
            pltpu.VMEM((rows, width), bf16),
            pltpu.VMEM((2, rows, WTILE), f32),
            pltpu.VMEM((every, WTILE), f32),
            pltpu.VMEM(docid.shape, bf16),
            pltpu.VMEM((GROUPS,) + docid.shape[1:], bf16),
            pltpu.VMEM((GROUPS,) + docid.shape[1:], bf16),
            pltpu.VMEM((GROUPS,) + docid.shape[1:], bf16),
            pltpu.VMEM(docid.shape[1:], f32),
            pltpu.VMEM(docid.shape, bf16),
            pltpu.VMEM((vocab // WTILE, every, WTILE), f32),
            pltpu.VMEM(small, f32),
            pltpu.VMEM((share_count,) + small, f32),
            pltpu.VMEM(small, f32),
            pltpu.VMEM((reps,) + small, f32),
            pltpu.VMEM((tiles, rows, WTILE), f32),
        ]
        + [dma((CHUNKS,))] * 3
        + [dma((CHUNKS * HALVES,))] * 10
        + [dma((CHUNKS,))] * 3
        + [dma((CHUNKS * (vocab // WTILE),))]
        + [dma((TAIL,))] * 2
        + [dma((GROUPS * TAIL,))] * 6
        + [dma((share_count,))] * 2
        + [dma((reps,))] * 2
        + [dma((CHUNKS // 2,))] * 2
        + [dma((tiles,))] * 2,
        compiler_params=pltpu.CompilerParams(
            collective_id=number, has_side_effects=True, vmem_limit_bytes=67043328
        ),
        name=f"stream_{sent}",
    )(
        lengths,
        x,
        enc_gain,
        dec_gain,
        docid,
        targets,
        wqkv.reshape(tiles, WTILE, width),
        wout,
        wcross,
        wclose,
        whead,
    )
    return logits, token_loss, mean[0, 0]


def largest_kernel(limits, lengths_ref, out_ref, mine, landed, send, recv):
    me = lax.axis_index("rep")
    count = lax.axis_size("rep")
    barrier = pltpu.get_barrier_semaphore()
    for k in range(1, count):
        pl.semaphore_signal(
            barrier, inc=1, device_id={"rep": lax.rem(me + k, count)}, device_id_type=MESH
        )
    live = 0
    for m in range(lengths_ref.shape[0]):
        for d in range(lengths_ref.shape[1]):
            live = live + lengths_ref[m, d]
    mine[...] = jnp.full(mine.shape, live, jnp.int32).astype(jnp.float32)
    pl.semaphore_wait(barrier, count - 1)

    def share(k, slot):
        return pltpu.make_async_remote_copy(
            src_ref=mine,
            dst_ref=landed.at[slot],
            send_sem=send.at[k],
            recv_sem=recv.at[k],
            device_id={"rep": lax.rem(me + k, count)},
            device_id_type=MESH,
        )

    for k in range(1, count):
        share(k, me).start()
    most = mine[...]
    for k in range(1, count):
        slot = lax.rem(me + count - k, count)
        share(k, slot).wait_recv()
        most = jnp.maximum(most, landed[slot])
    choice = jnp.zeros(most.shape, jnp.float32)
    for limit in limits:
        choice = choice + jnp.where(most > limit, 1.0, 0.0)
    out_ref[0, 0] = jnp.max(choice).astype(jnp.int32)
    for k in range(1, count):
        share(k, me).wait_send()


def branch_choice(limits, lengths):
    count = lax.axis_size("rep")
    dma = pltpu.SemaphoreType.DMA
    small = (8, 128)
    return pl.pallas_call(
        functools.partial(largest_kernel, limits),
        out_shape=jax.ShapeDtypeStruct((1, 1), jnp.int32),
        in_specs=[pl.BlockSpec(memory_space=pltpu.SMEM)],
        out_specs=pl.BlockSpec(memory_space=pltpu.SMEM),
        scratch_shapes=[pltpu.VMEM(small, jnp.float32), pltpu.VMEM((count,) + small, jnp.float32)]
        + [dma((count,))] * 2,
        compiler_params=pltpu.CompilerParams(collective_id=10, has_side_effects=True),
        name="largest",
    )(lengths)[0, 0]


def butterfly(value, axis, combine):
    for bit in range(lax.axis_size(axis).bit_length() - 1):
        value = combine(value, from_partner(value, axis, bit))
    return value


def greet(me, count):
    barrier = pltpu.get_barrier_semaphore()
    for k in range(1, count):
        pl.semaphore_signal(
            barrier, inc=1, device_id={"section": lax.rem(me + k, count)}, device_id_type=MESH
        )
    pl.semaphore_wait(barrier, count - 1)


def to_peer(src, dst, send, recv, peer):
    return pltpu.make_async_remote_copy(
        src_ref=src,
        dst_ref=dst,
        send_sem=send,
        recv_sem=recv,
        device_id={"section": peer},
        device_id_type=MESH,
    )


def closing_kernel(terms, residual, gain, out, landed, s1, r1, s2, r2):
    count = terms.shape[0]
    me = lax.axis_index("section")
    greet(me, count)

    def scatter(k, slot):
        peer = lax.rem(me + k, count)
        return to_peer(terms.at[peer], landed.at[slot], s1.at[k], r1.at[k], peer)

    def gather(k, slot):
        return to_peer(out.at[slot], out.at[slot], s2.at[k], r2.at[k], lax.rem(me + k, count))

    for k in range(1, count):
        scatter(k, me).start()
    total = residual[...] + terms[me].astype(jnp.float32)
    for k in range(1, count):
        slot = lax.rem(me + count - k, count)
        scatter(k, slot).wait_recv()
        total = total + landed[slot].astype(jnp.float32)
    scale = lax.rsqrt(jnp.mean(total * total, axis=-1, keepdims=True) + 1e-06)
    out[me] = (total * scale * gain[...]).astype(out.dtype)
    for k in range(1, count):
        gather(k, me).start()
    for k in range(1, count):
        gather(k, lax.rem(me + count - k, count)).wait_recv()
    for k in range(1, count):
        scatter(k, me).wait_send()
        gather(k, me).wait_send()


def closing_rows_of(terms, residual, gain):
    count = terms.shape[0]
    dma = pltpu.SemaphoreType.DMA
    vmem = pl.BlockSpec(memory_space=pltpu.VMEM)
    return pl.pallas_call(
        closing_kernel,
        out_shape=jax.ShapeDtypeStruct(terms.shape, jnp.bfloat16),
        in_specs=[vmem] * 3,
        out_specs=vmem,
        scratch_shapes=[pltpu.VMEM(terms.shape, jnp.bfloat16)] + [dma((count,))] * 4,
        compiler_params=pltpu.CompilerParams(collective_id=8, has_side_effects=True),
        name="closing",
    )(terms, residual, gain)


def sums_kernel(value, out, landed, send, recv):
    count = landed.shape[0]
    me = lax.axis_index("section")
    greet(me, count)

    def share(k, slot):
        return to_peer(value, landed.at[slot], send.at[k], recv.at[k], lax.rem(me + k, count))

    for k in range(1, count):
        share(k, me).start()
    landed[me] = value[...]
    for k in range(1, count):
        share(k, lax.rem(me + count - k, count)).wait_recv()
    total = landed[0]
    for k in range(1, count):
        total = total + landed[k]
    out[...] = total
    for k in range(1, count):
        share(k, me).wait_send()


def section_sum(value, count):
    dma = pltpu.SemaphoreType.DMA
    vmem = pl.BlockSpec(memory_space=pltpu.VMEM)
    return pl.pallas_call(
        sums_kernel,
        out_shape=jax.ShapeDtypeStruct(value.shape, value.dtype),
        in_specs=[vmem],
        out_specs=vmem,
        scratch_shapes=[pltpu.VMEM((count,) + value.shape, value.dtype)] + [dma((count,))] * 2,
        compiler_params=pltpu.CompilerParams(collective_id=9, has_side_effects=True),
        name="section_sum",
    )(value)


def large_shards(
    document_token_embedding,
    doc_lengths,
    docid_embed,
    docid_targets,
    enc_gain,
    dec_gain,
    w_enc_qkv,
    w_enc_out,
    cross_query_key_value_weight,
    w_cross_out,
    docid_head_weight,
):
    section_index = lax.axis_index("section")
    group_index = section_index // 2
    micro_count, row_count, width = document_token_embedding.shape
    doc_count = doc_lengths.shape[1]
    doc_span = row_count // doc_count
    all_rows = micro_count * row_count
    positions = jnp.arange(all_rows)
    row_doc = (positions // doc_span).astype(jnp.int32)
    live = (jnp.arange(doc_span)[None, :] < doc_lengths.reshape(-1)[:, None]).reshape(-1)
    key_doc = jnp.where(live, row_doc, -1).astype(jnp.int32)
    gain = lax.dynamic_slice_in_dim(enc_gain, group_index, 1, 0)
    hidden = encode(
        all_rows,
        all_rows,
        2,
        document_token_embedding.reshape(all_rows, width),
        gain,
        row_doc,
        key_doc,
        w_enc_qkv,
        w_enc_out,
    )
    memory = norm_rows(hidden, enc_gain[GROUPS]).astype(jnp.bfloat16)

    decoder_rows = docid_embed.shape[1]
    every = micro_count * decoder_rows
    docid_span = decoder_rows // doc_count
    decoder_doc = jnp.arange(every) // docid_span
    cross_heads = cross_query_key_value_weight.shape[1] // HD
    flat_docid = docid_embed.reshape(every, width)
    dec_normed = norm_rows(flat_docid, dec_gain[0]).astype(jnp.bfloat16)

    def project(values, weight):
        return (
            jnp.einsum("rd,cd->rc", values, weight, preferred_element_type=jnp.float32)
            .astype(jnp.bfloat16)
            .reshape(-1, cross_heads, HD)
        )

    queries = project(dec_normed, cross_query_key_value_weight[0])
    keys = project(memory, cross_query_key_value_weight[1])
    values = project(memory, cross_query_key_value_weight[2])
    allowed = decoder_doc[:, None] == key_doc[None, :]
    mixture = attend(queries, keys, values, allowed).reshape(every, -1)
    cross_terms = jnp.dot(mixture, w_cross_out, preferred_element_type=jnp.float32)
    section_count = lax.axis_size("section")
    share = every // section_count
    residual = lax.dynamic_slice_in_dim(flat_docid, section_index * share, share, 0)
    closing = closing_rows_of(
        cross_terms.astype(jnp.bfloat16).reshape(section_count, share, width),
        residual.astype(jnp.float32),
        dec_gain[1:2],
    ).reshape(every, width)
    scores_vocab = jnp.dot(closing, docid_head_weight, preferred_element_type=jnp.float32)
    vocab_local = docid_head_weight.shape[1]
    targets = docid_targets.reshape(-1)
    matches = targets[:, None] == section_index * vocab_local + jnp.arange(vocab_local)
    sums = jnp.stack(
        [
            jnp.sum(jnp.exp(scores_vocab), axis=-1),
            jnp.sum(jnp.where(matches, scores_vocab, 0.0), axis=-1),
        ]
    )
    padding = ((0, -sums.shape[0] % 8), (0, -sums.shape[1] % 128))
    sums = section_sum(jnp.pad(sums, padding), section_count)[:2, :every]
    token_loss = jnp.log(sums[0]) - sums[1]
    loss_sum = butterfly(jnp.sum(token_loss)[None], "rep", jnp.add)[0]
    mean_loss = loss_sum / (token_loss.size * lax.axis_size("rep"))
    logits = scores_vocab.astype(jnp.bfloat16).reshape(micro_count, decoder_rows, vocab_local)
    return (logits, token_loss.reshape(docid_targets.shape), mean_loss)


def fast_shards(
    document_token_embedding,
    doc_lengths,
    docid_embed,
    docid_targets,
    enc_gain,
    dec_gain,
    *weights,
):
    micro_count, row_count, width = document_token_embedding.shape
    sizes = (row_count * 3 // 4, row_count)
    section_count = lax.axis_size("section")
    choice = branch_choice(sizes, doc_lengths)

    def streamed(sent, number):
        def run():
            return stream(
                sent,
                number,
                doc_lengths,
                document_token_embedding.reshape(micro_count * row_count, width),
                enc_gain,
                dec_gain,
                docid_embed.reshape(section_count, -1, width),
                docid_targets,
                *weights,
            )
        return run

    def large():
        return large_shards(
            document_token_embedding,
            doc_lengths,
            docid_embed,
            docid_targets,
            enc_gain,
            dec_gain,
            *weights,
        )

    branches = [streamed(sent, number) for number, sent in enumerate(sizes)] + [large]
    return lax.switch(choice, branches)


def solution(mesh):
    in_specs = (
        P("rep", None, None),
        P("rep", None),
        P("rep", None, None),
        P("rep", None),
        P(),
        P(),
        P(None, "section", None),
        P("section", None),
        P(None, "section", None),
        P("section", None),
        P(None, "section"),
    )
    out_specs = (P("rep", None, "section"), P("rep", None), P())
    fits = mesh.shape["section"] == 2 * GROUPS and mesh.shape["rep"] % 2 == 0
    local = fast_shards if fits else shards
    return jax.shard_map(local, mesh=mesh, in_specs=in_specs, out_specs=out_specs, check_vma=False)
```
